128 devices in a mesh: seq: 32 (over y, x, core), head: 4 (over z).
Axes of the slice: x: 4, y: 4, z: 4, core: 2. Of those that a mesh axis runs over, the one named last changes fastest.
Arguments:
- hidden: bfloat16 [3072, 4096], P('seq'), may hold values from -6 to 6
- norm_gain: float32 [4096], replicated, may hold values from 0.5 to 1.5
- w_query: bfloat16 [4096, 4096], P(None, 'head'), may hold values from -0.09375 to 0.09375
- w_key: bfloat16 [4096, 1024], P(None, 'head'), may hold values from -0.25 to 0.25
- w_value: bfloat16 [4096, 1024], P(None, 'head'), may hold values from -0.09375 to 0.09375
- w_out: bfloat16 [4096, 4096], P('head'), may hold values from -0.09375 to 0.09375
- stored_kv: bfloat16 [32768, 2, 8, 128], P('seq', None, 'head'), may hold values from -720 to 720
- selected: int32 [3072], replicated, may hold values from 0 to 32767, as said below
- prompt_order: int32 [8], replicated, may hold values from 0 to 7, each once
- store_slot: int32 [8], replicated, may hold values from 0 to 7, each once
Outputs:
- attn_out: bfloat16 [3072, 4096], P('seq', 'head')
- new_kv: bfloat16 [3072, 2, 8, 128], P('seq', None, 'head')
The draws below stay inside these ranges and needn't reach their ends.
Inputs may be any that keep to these rules, and one draw needn't show every extreme that they name: `selected`: each block of 1024 prompt positions holds exactly 96 distinct entries, which stand together in that block's place of the list, increasing.
All inputs are finite; a program needn't handle non-finite values.
Results may differ from the reference program's by a relative error of at most 0.02.
The reference program's roundings to bfloat16 on the way (of `normed`, `query`, `cache`, `weights` and `context`) count: a program that leaves them out, or rounds other values in their place, can miss the bound.
Values may be sent and summed in bfloat16 or wider, within the bound.
A program may use at most 192 MiB of HBM per device.

```python
import jax
import jax.numpy as jnp
from jax import lax

D = 4096
HEADS = 32
KV_HEADS = 8
HEAD_DIM = 128
PASSAGE = 4096
TOK_DEV = 1024
SEL = 96
SEQ_LEN = 32768
PASSAGES = 8
ROWS = 3072
N_SEQ = 32


def draw_stored_kv(key, part):
    first = jax.random.fold_in(jax.random.fold_in(key, 11), 0)
    shape = (SEQ_LEN, 2, KV_HEADS, HEAD_DIM)
    base = jnp.clip(jax.random.normal(first, shape, jnp.float32), -6.0, 6.0)
    scale = jnp.array([3.0, 1.0], jnp.float32)[None, :, None, None]
    return (base * scale).astype(jnp.bfloat16)


def draw_selected(key, part):
    blocks = SEQ_LEN // TOK_DEV
    scores = jax.random.randint(jax.random.fold_in(key, 23), (blocks, TOK_DEV), 0, 1 << 18)
    scores = scores * TOK_DEV + jnp.arange(TOK_DEV, dtype=jnp.int32)[None, :]
    _, picked = lax.top_k(scores, SEL)
    picked = jnp.sort(picked, axis=1)
    offsets = jnp.arange(blocks, dtype=jnp.int32)[:, None] * TOK_DEV
    return (picked + offsets).reshape(-1).astype(jnp.int32)


def steps_of(key, dims, cuts, least, top_value):
    def one(axis_at, parts):
        steps = jax.random.uniform(jax.random.fold_in(jax.random.fold_in(key, 6), axis_at), (parts,), jnp.float32, least / len(cuts), top_value / len(cuts))
        return jnp.repeat(jnp.exp(steps), dims[axis_at] // parts).reshape((-1,) + (1,) * (len(dims) - axis_at - 1))

    level = one(*cuts[0])
    for cut in cuts[1:]:
        level = level * one(*cut)
    return level


def normal_values(own_key, shape, width, limit, cuts=(), kind=jnp.bfloat16):
    values = width * jax.random.normal(own_key, shape, jnp.float32)
    if cuts:
        values = values * steps_of(own_key, shape, cuts, -0.22, 0.18)
    return jnp.clip(values, -limit, limit).astype(kind)


def setup_inputs(seed: int = 0) -> dict:
    key_of = jax.random.split(jax.random.key(seed), 11)
    hidden = normal_values(key_of[0], (ROWS, D), 1.0, 6.0, ((0, 32),))
    norm_gain = jnp.clip(1.0 + 0.1 * jax.random.normal(key_of[1], (D,), jnp.float32), 0.5, 1.5)
    w_query = normal_values(key_of[2], (D, HEADS * HEAD_DIM), D ** -0.5, 0.09375, ((1, 4),))
    w_key = normal_values(key_of[3], (D, KV_HEADS * HEAD_DIM), (D // 9) ** -0.5, 0.25, ((1, 4),))
    w_value = normal_values(key_of[4], (D, KV_HEADS * HEAD_DIM), D ** -0.5, 0.09375, ((1, 4),))
    w_out = normal_values(key_of[5], (HEADS * HEAD_DIM, D), (HEADS * HEAD_DIM) ** -0.5, 0.09375, ((0, 4),))
    stored_kv = draw_stored_kv(jax.random.fold_in(key_of[10], 71), 0)
    selected = draw_selected(jax.random.fold_in(key_of[10], 71), 0)
    prompt_order = jax.random.permutation(key_of[8], PASSAGES).astype(jnp.int32)
    store_slot = jax.random.permutation(key_of[9], PASSAGES).astype(jnp.int32)
    return dict(hidden=hidden, norm_gain=norm_gain, w_query=w_query, w_key=w_key, w_value=w_value, w_out=w_out, stored_kv=stored_kv, selected=selected, prompt_order=prompt_order, store_slot=store_slot)


def rope(x, pos):
    half = HEAD_DIM // 2
    freq = 500000.0 ** (-(jnp.arange(half, dtype=jnp.float32) * 2.0 / HEAD_DIM))
    angle = pos.astype(jnp.float32)[:, None] * freq[None, :]
    cosine = jnp.cos(angle)[:, None, :]
    sine = jnp.sin(angle)[:, None, :]
    first = x[..., :half]
    second = x[..., half:]
    return jnp.concatenate([first * cosine - second * sine, second * cosine + first * sine], -1)

def reference(hidden, norm_gain, w_query, w_key, w_value, w_out, stored_kv, selected, prompt_order, store_slot):
    group = HEADS // KV_HEADS
    widened = hidden.astype(jnp.float32)
    normed = (widened * lax.rsqrt(lax.optimization_barrier(jnp.mean(widened * widened, -1, keepdims=True)) + 1e-05) * norm_gain).astype(jnp.bfloat16)
    query = rope(jnp.dot(normed, w_query, preferred_element_type=jnp.float32).reshape(ROWS, HEADS, HEAD_DIM), selected).astype(jnp.bfloat16)
    fresh_key = rope(jnp.dot(normed, w_key, preferred_element_type=jnp.float32).reshape(ROWS, KV_HEADS, HEAD_DIM), selected)
    fresh_value = jnp.dot(normed, w_value, preferred_element_type=jnp.float32).reshape(ROWS, KV_HEADS, HEAD_DIM)
    new_kv = jnp.stack([fresh_key, fresh_value], 1).astype(jnp.bfloat16)
    slot_of_prompt = store_slot[prompt_order].astype(jnp.int32)
    stored = stored_kv.reshape(PASSAGES, PASSAGE, 2, KV_HEADS, HEAD_DIM)[slot_of_prompt]
    cache = stored.reshape(SEQ_LEN, 2, KV_HEADS, HEAD_DIM).at[selected].set(new_kv)
    keys = cache[:, 0]
    values = cache[:, 1]
    key_pos = jnp.arange(SEQ_LEN, dtype=jnp.int32)
    blocks = query.reshape(N_SEQ, SEL, HEADS, HEAD_DIM)
    pos_blocks = selected.reshape(N_SEQ, SEL)
    scale = 1.0 / HEAD_DIM ** 0.5

    def one_head(head):
        key_head = lax.dynamic_index_in_dim(keys, head // group, 1, False)
        value_head = lax.dynamic_index_in_dim(values, head // group, 1, False)

        def one_block(index):
            block = lax.dynamic_index_in_dim(blocks, index, 0, False)
            query_head = lax.dynamic_index_in_dim(block, head, 1, False)
            positions = lax.dynamic_index_in_dim(pos_blocks, index, 0, False)
            scores = jnp.dot(query_head, key_head.T, preferred_element_type=jnp.float32) * scale
            valid = key_pos[None, :] <= positions[:, None]
            scores = jnp.where(valid, scores, -1e+30)
            top = lax.optimization_barrier(jnp.max(scores, -1, keepdims=True))
            weights = jnp.where(valid, jnp.exp(scores - top), 0.0)
            total = lax.optimization_barrier(jnp.sum(weights, -1, keepdims=True))
            summed = jnp.dot(weights.astype(jnp.bfloat16), value_head, preferred_element_type=jnp.float32)
            return summed / total
        return lax.map(one_block, jnp.arange(N_SEQ, dtype=jnp.int32))
    context = lax.map(one_head, jnp.arange(HEADS, dtype=jnp.int32))
    context = context.transpose(1, 2, 0, 3).reshape(ROWS, HEADS * HEAD_DIM).astype(jnp.bfloat16)
    attn_out = jnp.dot(context, w_out, preferred_element_type=jnp.float32).astype(jnp.bfloat16)
    return (attn_out, new_kv)
```

```python
import functools

import jax
import jax.numpy as jnp
from jax import lax
from jax.experimental import pallas as pl
from jax.experimental.pallas import tpu as pltpu
from jax.sharding import PartitionSpec as P

HEADS = 32
KV_HEADS = 8
HEAD_DIM = 128
PASSAGE = 4096
SIDE = 4
GROUP = HEADS // KV_HEADS
BLOCK = 1024
SEL = 96
FRESH = 128
HALF_KEYS = BLOCK + FRESH
KEYS = 2 * HALF_KEYS
ROWS = GROUP * SEL
FAR = 1.0e9
NEG = -1.0e30
LOG_SCALE = 1.4426950408889634 / HEAD_DIM**0.5
F32 = jnp.float32
BF16 = jnp.bfloat16
MESH = pl.DeviceIdType.MESH


def walk(i):
    return i + i // 2 - 2 * (i // 3)


def pack_rows(column):
    lane = lax.broadcasted_iota(jnp.int32, (SEL, 128), 1)
    total = jnp.zeros((SEL, 128), F32)
    for h in range(GROUP):
        total = jnp.where(lane == h, column[h * SEL : (h + 1) * SEL], total)
    square = jnp.concatenate([total, jnp.zeros((128 - SEL, 128), F32)], 0)
    return square.T[:8]


def unpack_rows(packed):
    square = jnp.concatenate([packed, jnp.zeros((120, 128), F32)], 0).T
    return jnp.concatenate(
        [jnp.broadcast_to(square[:SEL, h : h + 1], (SEL, 128)) for h in range(GROUP)], 0
    )


def merge(parts, stats):
    top = functools.reduce(jnp.maximum, stats)
    factors = [jnp.exp2(s - top) for s in stats]
    total = functools.reduce(jnp.add, factors)
    merged = sum(
        part.astype(F32) * unpack_rows(factor / total) for part, factor in zip(parts, factors)
    )
    return merged, top + jnp.log2(total)


def kernel(
    query_in,
    key_in,
    value_in,
    key_pos,
    row_pos,
    w_out_in,
    out_ref,
    qbuf,
    kbuf,
    vbuf,
    wbuf,
    scores,
    tops,
    part,
    stat,
    rb_part,
    rb_stat,
    mid,
    mid_stat,
    ra_part,
    ra_stat,
    ctx,
    zsend,
    zrecv,
    local_sem,
    kv_ssem,
    kv_rsem,
    g_ssem,
    g_rsem,
    bp_ssem,
    bp_rsem,
    bs_ssem,
    bs_rsem,
    ap_ssem,
    ap_rsem,
    as_ssem,
    as_rsem,
    z_ssem,
    z_rsem,
):
    seq = lax.axis_index("seq")
    head = lax.axis_index("head")
    core = lax.rem(seq, 2)
    chip_x = lax.rem(seq // 2, SIDE)
    chip_y = seq // (2 * SIDE)

    def chip_seq(dx, dy):
        return (lax.rem(chip_y + dy, SIDE) * SIDE + lax.rem(chip_x + dx, SIDE)) * 2 + core

    def peer(g, da, db):
        return chip_seq(da, db) if g == 0 else chip_seq(db, da)

    def at(index):
        return (index, head)

    partner = (seq + 1 - 2 * core, head)

    barrier = pltpu.get_barrier_semaphore()
    others = [partner]
    for d in range(1, SIDE):
        others.append(at(chip_seq(d, 0)))
        others.append(at(chip_seq(0, d)))
        others.append((seq, lax.rem(head + d, SIDE)))
    for other in others:
        pl.semaphore_signal(barrier, inc=1, device_id=other, device_id_type=MESH)

    own_q = pltpu.make_async_copy(query_in, qbuf.at[:, 0], local_sem.at[0])
    own_k = pltpu.make_async_copy(key_in, kbuf.at[:, pl.ds(0, HALF_KEYS)], local_sem.at[1])
    own_v = pltpu.make_async_copy(value_in, vbuf.at[:, pl.ds(0, HALF_KEYS)], local_sem.at[2])
    own_q.start()
    own_k.start()
    own_v.start()
    weights = [
        pltpu.make_async_copy(
            w_out_in.at[:, pl.ds(n * 1024, 1024)], wbuf.at[n], local_sem.at[3 + n]
        )
        for n in range(SIDE)
    ]
    for copy in weights:
        copy.start()
    pl.semaphore_wait(barrier, len(others))

    kv_copies = [
        pltpu.make_async_remote_copy(
            src_ref=src,
            dst_ref=dst.at[:, pl.ds(HALF_KEYS, HALF_KEYS)],
            send_sem=kv_ssem.at[n],
            recv_sem=kv_rsem.at[n],
            device_id=partner,
            device_id_type=MESH,
        )
        for n, (src, dst) in enumerate(((key_in, kbuf), (value_in, vbuf)))
    ]
    for copy in kv_copies:
        copy.start()
    own_q.wait()

    def whole(g, src, dst, sem, to):
        return pltpu.make_async_remote_copy(
            src_ref=qbuf.at[g, src],
            dst_ref=qbuf.at[g, dst],
            send_sem=g_ssem.at[g, sem],
            recv_sem=g_rsem.at[g, dst, 0],
            device_id=at(to),
            device_id_type=MESH,
        )

    def halved(g, src, dst, half, sem, to):
        rows = pl.ds(half * (ROWS // 2), ROWS // 2)
        return pltpu.make_async_remote_copy(
            src_ref=qbuf.at[g, src, rows],
            dst_ref=qbuf.at[g, dst, rows],
            send_sem=g_ssem.at[g, sem],
            recv_sem=g_rsem.at[g, dst, half],
            device_id=at(to),
            device_id_type=MESH,
        )

    def a_sends(g):
        return [whole(g, 0, 12, 0, peer(g, 1, 0)), whole(g, 0, 4, 1, peer(g, 3, 0))]

    def a_forward(g, da):
        if da == 3:
            return halved(g, 12, 8, 0, 2, peer(g, 1, 0))
        return halved(g, 4, 8, 1, 3, peer(g, 3, 0))

    def b_sends(g, da):
        return [
            whole(g, da * 4, da * 4 + 3, 4 + 4 * da, peer(g, 0, 1)),
            whole(g, da * 4, da * 4 + 1, 5 + 4 * da, peer(g, 0, 3)),
        ]

    def b_forwards(g, da):
        return [
            halved(g, da * 4 + 3, da * 4 + 2, 0, 6 + 4 * da, peer(g, 0, 1)),
            halved(g, da * 4 + 1, da * 4 + 2, 1, 7 + 4 * da, peer(g, 0, 3)),
        ]

    def arrive(t, g):
        da = walk(lax.rem(t, 4))
        row = t // 4

        @pl.when(t == 0)
        def _():
            for copy in a_sends(g):
                copy.start()

        @pl.when(jnp.logical_or(t == 1, t == 2))
        def _():
            whole(g, 0, da * 4, 0, peer(g, 1, 0)).wait_recv()

        @pl.when(t == 1)
        def _():
            a_forward(g, 1).start()

        @pl.when(t == 2)
        def _():
            a_forward(g, 3).start()

        @pl.when(t == 3)
        def _():
            for half in range(2):
                halved(g, 0, 8, half, 0, peer(g, 1, 0)).wait_recv()

        @pl.when(row == 0)
        def _():
            for copy in b_sends(g, da):
                copy.start()

        @pl.when(row == 1)
        def _():
            for db in (1, 3):
                whole(g, 0, da * 4 + db, 0, peer(g, 1, 0)).wait_recv()
            for copy in b_forwards(g, da):
                copy.start()

        @pl.when(row == 2)
        def _():
            for half in range(2):
                halved(g, 0, da * 4 + 2, half, 0, peer(g, 1, 0)).wait_recv()

    def slot_of(t):
        return walk(lax.rem(t, 4)) * 4 + t // 4

    def score(t, g):
        da = walk(lax.rem(t, 4))
        owner = peer(g, da, t // 4)
        s = lax.dot_general(
            qbuf[g, slot_of(t)],
            kbuf[g],
            (((1,), (1,)), ((), ())),
            preferred_element_type=F32,
        )
        row = jnp.broadcast_to(row_pos[pl.ds(owner, 1), :], (128, 128)).T[:SEL, :1]
        pos = jnp.concatenate([row] * GROUP, 0)
        s = jnp.where(key_pos[...] <= pos, s, NEG)
        scores[g] = s
        tops[g] = jnp.broadcast_to(jnp.max(s, -1, keepdims=True), (ROWS, 128))

    def weigh(t, g):
        top = tops[g]
        e = jnp.exp2((scores[g] - top[:, :1]) * LOG_SCALE).astype(BF16)
        table = jnp.concatenate([vbuf[g], jnp.ones((KEYS, 128), BF16)], 1)
        summed = jnp.dot(e, table, preferred_element_type=F32)
        total = summed[:, 128:]
        part[g, t] = (summed[:, :128] / total).astype(BF16)
        stat[g, t] = pack_rows(top * LOG_SCALE + jnp.log2(total))

    def b_result(g, t, da, db):
        to = at(peer(g, 0, db))
        return [
            pltpu.make_async_remote_copy(
                src_ref=part.at[g, t],
                dst_ref=rb_part.at[g, da, db - 1],
                send_sem=bp_ssem.at[g, da, db - 1],
                recv_sem=bp_rsem.at[g, da, db - 1],
                device_id=to,
                device_id_type=MESH,
            ),
            pltpu.make_async_remote_copy(
                src_ref=stat.at[g, t],
                dst_ref=rb_stat.at[g, da, db - 1],
                send_sem=bs_ssem.at[g, da, db - 1],
                recv_sem=bs_rsem.at[g, da, db - 1],
                device_id=to,
                device_id_type=MESH,
            ),
        ]

    def pass_on(t, g):
        @pl.when(t >= 4)
        def _():
            for copy in b_result(g, t, walk(lax.rem(t, 4)), t // 4):
                copy.start()

    arrive(0, 0)
    arrive(0, 1)
    own_k.wait()
    own_v.wait()
    for copy in kv_copies:
        copy.wait()
    score(0, 0)

    def step(t, carry):
        @pl.when(t > 0)
        def _():
            arrive(t, 1)

        score(t, 1)
        weigh(t, 0)
        pass_on(t, 0)
        after = jnp.minimum(t + 1, 15)

        @pl.when(t < 15)
        def _():
            arrive(after, 0)

        score(after, 0)
        weigh(t, 1)
        pass_on(t, 1)
        return carry

    lax.fori_loop(0, 16, step, 0)

    def a_result(g, da):
        to = at(peer(g, da, 0))
        return [
            pltpu.make_async_remote_copy(
                src_ref=mid.at[g, da - 1],
                dst_ref=ra_part.at[g, da - 1],
                send_sem=ap_ssem.at[g, da - 1],
                recv_sem=ap_rsem.at[g, da - 1],
                device_id=to,
                device_id_type=MESH,
            ),
            pltpu.make_async_remote_copy(
                src_ref=mid_stat.at[g, da - 1],
                dst_ref=ra_stat.at[g, da - 1],
                send_sem=as_ssem.at[g, da - 1],
                recv_sem=as_rsem.at[g, da - 1],
                device_id=to,
                device_id_type=MESH,
            ),
        ]

    def line_sum(g, da, t):
        for db in range(1, SIDE):
            for copy in b_result(g, 0, da, db):
                copy.wait_recv()
        return merge(
            [part[g, t]] + [rb_part[g, da, n] for n in range(3)],
            [stat[g, t]] + [rb_stat[g, da, n] for n in range(3)],
        )

    for da, t in ((2, 3), (1, 1), (3, 2)):
        for g in range(2):
            merged, logs = line_sum(g, da, t)
            mid[g, da - 1] = merged.astype(BF16)
            mid_stat[g, da - 1] = logs
            for copy in a_result(g, da):
                copy.start()
    for g in range(2):
        merged, logs = line_sum(g, 0, 0)
        part[g, 0] = merged.astype(BF16)
        stat[g, 0] = logs
    for g in range(2):
        for da in (1, 3, 2):
            for copy in a_result(g, da):
                copy.wait_recv()
        merged, _ = merge(
            [part[g, 0]] + [ra_part[g, n] for n in range(3)],
            [stat[g, 0]] + [ra_stat[g, n] for n in range(3)],
        )
        for h in range(GROUP):
            ctx[:, pl.ds((g * GROUP + h) * 128, 128)] = merged[h * SEL : (h + 1) * SEL].astype(BF16)

    for copy in weights:
        copy.wait()

    def z_result(dz):
        return pltpu.make_async_remote_copy(
            src_ref=zsend.at[dz - 1],
            dst_ref=zrecv.at[dz - 1],
            send_sem=z_ssem.at[dz - 1],
            recv_sem=z_rsem.at[dz - 1],
            device_id=(seq, lax.rem(head + dz, SIDE)),
            device_id_type=MESH,
        )

    for dz in (2, 1, 3):
        zsend[dz - 1] = jnp.dot(
            ctx[...], wbuf[lax.rem(head + dz, SIDE)], preferred_element_type=F32
        ).astype(BF16)
        z_result(dz).start()
    total = jnp.dot(ctx[...], wbuf[head], preferred_element_type=F32).astype(BF16).astype(F32)
    for dz in (1, 3, 2):
        z_result(dz).wait_recv()
        total = total + zrecv[dz - 1].astype(F32)
    out_ref[...] = total.astype(BF16)

    for g in range(2):
        for copy in a_sends(g) + [a_forward(g, 3), a_forward(g, 1)]:
            copy.wait_send()
        for da in range(4):
            for copy in b_sends(g, da) + b_forwards(g, da):
                copy.wait_send()
            for db in range(1, 4):
                for copy in b_result(g, 0, da, db):
                    copy.wait_send()
        for da in range(1, 4):
            for copy in a_result(g, da):
                copy.wait_send()
    for dz in range(1, 4):
        z_result(dz).wait_send()


def attend(query, keys, values, key_pos, row_pos, w_out):
    vmem = pl.BlockSpec(memory_space=pltpu.VMEM)
    hbm = pl.BlockSpec(memory_space=pl.ANY)
    dma = pltpu.SemaphoreType.DMA
    return pl.pallas_call(
        kernel,
        out_shape=jax.ShapeDtypeStruct((SEL, 1024), BF16),
        in_specs=[hbm, hbm, hbm, vmem, vmem, hbm],
        out_specs=vmem,
        scratch_shapes=[
            pltpu.VMEM((2, 16, ROWS, 128), BF16),
            pltpu.VMEM((2, KEYS, 128), BF16),
            pltpu.VMEM((2, KEYS, 128), BF16),
            pltpu.VMEM((SIDE, 1024, 1024), BF16),
            pltpu.VMEM((2, ROWS, KEYS), F32),
            pltpu.VMEM((2, ROWS, 128), F32),
            pltpu.VMEM((2, 16, ROWS, 128), BF16),
            pltpu.VMEM((2, 16, 8, 128), F32),
            pltpu.VMEM((2, 4, 3, ROWS, 128), BF16),
            pltpu.VMEM((2, 4, 3, 8, 128), F32),
            pltpu.VMEM((2, 3, ROWS, 128), BF16),
            pltpu.VMEM((2, 3, 8, 128), F32),
            pltpu.VMEM((2, 3, ROWS, 128), BF16),
            pltpu.VMEM((2, 3, 8, 128), F32),
            pltpu.VMEM((SEL, 1024), BF16),
            pltpu.VMEM((3, SEL, 1024), BF16),
            pltpu.VMEM((3, SEL, 1024), BF16),
            dma((7,)),
            dma((2,)),
            dma((2,)),
            dma((2, 20)),
            dma((2, 16, 2)),
            dma((2, 4, 3)),
            dma((2, 4, 3)),
            dma((2, 4, 3)),
            dma((2, 4, 3)),
            dma((2, 3)),
            dma((2, 3)),
            dma((2, 3)),
            dma((2, 3)),
            dma((3,)),
            dma((3,)),
        ],
        compiler_params=pltpu.CompilerParams(
            collective_id=0, has_side_effects=True, vmem_limit_bytes=60_000_000
        ),
    )(query, keys, values, key_pos, row_pos, w_out)


def rope(x, pos):
    half = HEAD_DIM // 2
    freq = 500000.0 ** (-(jnp.arange(half, dtype=jnp.float32) * 2.0 / HEAD_DIM))
    angle = pos.astype(jnp.float32)[:, None] * freq[None, :]
    cosine = jnp.cos(angle)[:, None, :]
    sine = jnp.sin(angle)[:, None, :]
    first = x[..., :half]
    second = x[..., half:]
    return jnp.concatenate([first * cosine - second * sine, second * cosine + first * sine], -1)


def body(
    hidden, norm_gain, w_query, w_key, w_value, w_out, stored_kv, selected, prompt_order, store_slot
):
    seq_index = lax.axis_index("seq")
    own_rows = hidden.shape[0]
    shard_rows = stored_kv.shape[0]
    local_kv = w_key.shape[1] // HEAD_DIM
    passages = prompt_order.shape[0]
    per_passage = PASSAGE // shard_rows
    positions = lax.dynamic_slice_in_dim(selected, seq_index * own_rows, own_rows)
    widened = hidden.astype(jnp.float32)
    normed = (
        widened * lax.rsqrt(jnp.mean(widened * widened, -1, keepdims=True) + 1e-05) * norm_gain
    ).astype(jnp.bfloat16)
    query = rope(
        jnp.dot(normed, w_query, preferred_element_type=jnp.float32).reshape(
            own_rows, local_kv * GROUP, HEAD_DIM
        ),
        positions,
    )
    query = query.astype(jnp.bfloat16).transpose(1, 0, 2).reshape(local_kv, ROWS, HEAD_DIM)
    fresh_key = rope(
        jnp.dot(normed, w_key, preferred_element_type=jnp.float32).reshape(
            own_rows, local_kv, HEAD_DIM
        ),
        positions,
    )
    fresh_value = jnp.dot(normed, w_value, preferred_element_type=jnp.float32).reshape(
        own_rows, local_kv, HEAD_DIM
    )
    new_kv = jnp.stack([fresh_key, fresh_value], 1).astype(jnp.bfloat16)

    slots = jnp.arange(passages, dtype=jnp.int32)
    picker = (prompt_order[:, None] == slots[None, :]).astype(jnp.int32)
    slot_of_prompt = jnp.sum(picker * store_slot[None, :], 1)
    prompt_of_slot = jnp.sum(
        (slot_of_prompt[:, None] == slots[None, :]).astype(jnp.int32) * slots[:, None], 0
    )

    def positions_of(device):
        place = jnp.sum(jnp.where(slots == device // per_passage, prompt_of_slot, 0))
        block = place * per_passage + device % per_passage
        there = block * shard_rows + jnp.arange(shard_rows, dtype=jnp.int32)
        replaced = lax.dynamic_slice_in_dim(selected, block * own_rows, own_rows)
        gone = jnp.any(there[:, None] == replaced[None, :], 1)
        fresh = lax.dynamic_slice_in_dim(selected, device * own_rows, own_rows)
        return [
            jnp.where(gone, FAR, there.astype(F32)),
            fresh.astype(F32),
            jnp.full((FRESH - own_rows,), FAR, F32),
        ]

    other_core = seq_index + 1 - 2 * (seq_index % 2)
    key_pos = jnp.concatenate(positions_of(seq_index) + positions_of(other_core))[None]
    row_pos = jnp.pad(
        selected.astype(F32).reshape(-1, own_rows), ((0, 0), (0, 128 - own_rows))
    )
    both = jnp.concatenate(
        [
            stored_kv,
            new_kv,
            jnp.zeros((FRESH - own_rows, *new_kv.shape[1:]), BF16),
        ],
        0,
    ).transpose(1, 2, 0, 3)
    attn_out = attend(query, both[0], both[1], key_pos, row_pos, w_out)
    return (attn_out, new_kv)


def solution(mesh):
    in_specs = (
        P("seq", None),
        P(),
        P(None, "head"),
        P(None, "head"),
        P(None, "head"),
        P("head", None),
        P("seq", None, "head", None),
        P(),
        P(),
        P(),
    )
    out_specs = (P("seq", "head"), P("seq", None, "head", None))
    return jax.shard_map(body, mesh=mesh, in_specs=in_specs, out_specs=out_specs, check_vma=False)
```

```python
import functools

import jax
import jax.numpy as jnp
from jax import lax
from jax.experimental import pallas as pl
from jax.experimental.pallas import tpu as pltpu
from jax.sharding import PartitionSpec as P

D = 4096
HEADS = 32
KV_HEADS = 8
HEAD_DIM = 128
PASSAGE = 4096
PASSAGES = 8
SIDE = 4
GROUP = HEADS // KV_HEADS
BLOCK = 1024
SEL = 96
FRESH = 128
HALF_KEYS = BLOCK + FRESH
KEYS = 2 * HALF_KEYS
ROWS = GROUP * SEL
FAR = 1.0e9
NEG = -1.0e30
LOG_SCALE = 1.4426950408889634 / HEAD_DIM**0.5
F32 = jnp.float32
BF16 = jnp.bfloat16
MESH = pl.DeviceIdType.MESH


def walk(i):
    return i + i // 2 - 2 * (i // 3)


def walk_last(i):
    return 2 - i + 3 * (i // 2) - 2 * (i // 3)


def line_of(t):
    first = walk(lax.rem(t, 4))
    return first + (walk_last(lax.rem(t, 4)) - first) * (t // 12)


def pack_rows(column):
    lane = lax.broadcasted_iota(jnp.int32, (SEL, 128), 1)
    total = jnp.zeros((SEL, 128), F32)
    for h in range(GROUP):
        total = jnp.where(lane == h, column[h * SEL : (h + 1) * SEL], total)
    square = jnp.concatenate([total, jnp.zeros((128 - SEL, 128), F32)], 0)
    return square.T[:8]


def unpack_rows(packed):
    square = jnp.concatenate([packed, jnp.zeros((120, 128), F32)], 0).T
    return jnp.concatenate(
        [jnp.broadcast_to(square[:SEL, h : h + 1], (SEL, 128)) for h in range(GROUP)], 0
    )


def merge(parts, stats):
    top = functools.reduce(jnp.maximum, stats)
    factors = [jnp.exp2(s - top) for s in stats]
    total = functools.reduce(jnp.add, factors)
    merged = sum(
        part.astype(F32) * unpack_rows(factor / total) for part, factor in zip(parts, factors)
    )
    return merged, top + jnp.log2(total)


def kernel(
    prompt_order,
    store_slot,
    hidden_in,
    gain,
    cosine,
    sine,
    row_pos,
    stored_in,
    w_query_in,
    w_key_in,
    w_value_in,
    w_out_in,
    out_ref,
    new_ref,
    hid,
    normed,
    wq,
    wkv,
    stored,
    wide,
    fresh,
    key_pos,
    qbuf,
    kbuf,
    vbuf,
    wbuf,
    scores,
    tops,
    part,
    stat,
    rb_part,
    rb_stat,
    mid,
    mid_stat,
    ra_part,
    ra_stat,
    ctx,
    zsend,
    zrelay,
    zrecv,
    local_sem,
    kv_ssem,
    kv_rsem,
    g_ssem,
    g_rsem,
    bp_ssem,
    bp_rsem,
    bs_ssem,
    bs_rsem,
    ap_ssem,
    ap_rsem,
    as_ssem,
    as_rsem,
    z_ssem,
    z_rsem,
):
    seq = lax.axis_index("seq")
    head = lax.axis_index("head")
    core = lax.rem(seq, 2)
    chip_x = lax.rem(seq // 2, SIDE)
    chip_y = seq // (2 * SIDE)

    def chip_seq(dx, dy):
        return (lax.rem(chip_y + dy, SIDE) * SIDE + lax.rem(chip_x + dx, SIDE)) * 2 + core

    def peer(g, da, db):
        return chip_seq(da, db) if g == 0 else chip_seq(db, da)

    def at(index):
        return (index, head)

    def above(dz):
        return (seq, lax.rem(head + dz, SIDE))

    other_seq = seq + 1 - 2 * core
    partner = (other_seq, head)

    barrier = pltpu.get_barrier_semaphore()
    others = [partner]
    for d in range(1, SIDE):
        others.append(at(chip_seq(d, 0)))
        others.append(at(chip_seq(0, d)))
    others += [above(1), above(3)]
    for other in others:
        pl.semaphore_signal(barrier, inc=1, device_id=other, device_id_type=MESH)

    load = pltpu.make_async_copy
    half_depth = D // 2
    own_hidden = load(hidden_in, hid, local_sem.at[0])
    own_stored = load(stored_in, stored, local_sem.at[1])
    q_loads = [
        [
            load(
                w_query_in.at[pl.ds(n * half_depth, half_depth), pl.ds(g * 512, 512)],
                wq.at[g, n],
                local_sem.at[2 + 2 * g + n],
            )
            for n in range(2)
        ]
        for g in range(2)
    ]
    kv_loads = [
        load(src, wkv.at[n], local_sem.at[6 + n]) for n, src in enumerate((w_key_in, w_value_in))
    ]
    weights = [
        load(w_out_in.at[:, pl.ds(n * 1024, 1024)], wbuf.at[n], local_sem.at[8 + n])
        for n in range(SIDE)
    ]
    own_hidden.start()
    q_loads[0][0].start()
    own_stored.start()
    q_loads[0][1].start()
    for copy in q_loads[1] + kv_loads + weights:
        copy.start()

    order = [store_slot[prompt_order[i]] for i in range(PASSAGES)]
    lanes = lax.broadcasted_iota(jnp.int32, (1, BLOCK), 1)
    short = lax.broadcasted_iota(jnp.int32, (1, FRESH), 1)
    per_passage = PASSAGE // BLOCK
    for n, device in enumerate((seq, other_seq)):
        place = jnp.int32(0)
        for i in range(PASSAGES):
            place = jnp.where(order[i] == device // per_passage, i, place)
        block = place * per_passage + lax.rem(device, per_passage)
        there = (block * BLOCK + lanes).astype(F32)
        replaced = jnp.broadcast_to(row_pos[pl.ds(block, 1), :], (128, 128)).T[:SEL, :1]
        gone = jnp.max(jnp.where(replaced == there, FAR, 0.0), 0, keepdims=True)
        key_pos[:, pl.ds(n * HALF_KEYS, BLOCK)] = there + gone
        key_pos[:, pl.ds(n * HALF_KEYS + BLOCK, FRESH)] = jnp.where(
            short < SEL, row_pos[pl.ds(device, 1), :], FAR
        )

    own_hidden.wait()
    widened = hid[...].astype(F32)
    mean = jnp.mean(widened * widened, -1, keepdims=True)
    normed[...] = (widened * lax.rsqrt(mean + 1e-05) * gain[...]).astype(BF16)

    own_stored.wait()
    wide[...] = stored[...].astype(F32)
    for n, buf in enumerate((kbuf, vbuf)):
        for g in range(2):
            rows = wide[pl.ds(2 * n + g, BLOCK, stride=4), :]
            buf[g, pl.ds(0, BLOCK), :] = rows.astype(BF16)
    pl.semaphore_wait(barrier, len(others))

    def to_partner(n, first, count):
        buf = (kbuf, vbuf)[n]
        index = 2 * n + (first > 0)
        return pltpu.make_async_remote_copy(
            src_ref=buf.at[:, pl.ds(first, count)],
            dst_ref=buf.at[:, pl.ds(HALF_KEYS + first, count)],
            send_sem=kv_ssem.at[index],
            recv_sem=kv_rsem.at[index],
            device_id=partner,
            device_id_type=MESH,
        )

    stored_copies = [to_partner(n, 0, BLOCK) for n in range(2)]
    fresh_copies = [to_partner(n, BLOCK, FRESH) for n in range(2)]
    for copy in stored_copies:
        copy.start()

    def whole(g, src, dst, sem, to):
        return pltpu.make_async_remote_copy(
            src_ref=qbuf.at[g, src],
            dst_ref=qbuf.at[g, dst],
            send_sem=g_ssem.at[g, sem],
            recv_sem=g_rsem.at[g, dst, 0],
            device_id=at(to),
            device_id_type=MESH,
        )

    def halved(g, src, dst, half, sem, to):
        rows = pl.ds(half * (ROWS // 2), ROWS // 2)
        return pltpu.make_async_remote_copy(
            src_ref=qbuf.at[g, src, rows],
            dst_ref=qbuf.at[g, dst, rows],
            send_sem=g_ssem.at[g, sem],
            recv_sem=g_rsem.at[g, dst, half],
            device_id=at(to),
            device_id_type=MESH,
        )

    def a_sends(g):
        return [whole(g, 0, 12, 0, peer(g, 1, 0)), whole(g, 0, 4, 1, peer(g, 3, 0))]

    def a_forward(g, da):
        if da == 3:
            return halved(g, 12, 8, 0, 2, peer(g, 1, 0))
        return halved(g, 4, 8, 1, 3, peer(g, 3, 0))

    def b_sends(g, da):
        return [
            whole(g, da * 4, da * 4 + 3, 4 + 4 * da, peer(g, 0, 1)),
            whole(g, da * 4, da * 4 + 1, 5 + 4 * da, peer(g, 0, 3)),
        ]

    def b_forwards(g, da):
        return [
            halved(g, da * 4 + 3, da * 4 + 2, 0, 6 + 4 * da, peer(g, 0, 1)),
            halved(g, da * 4 + 1, da * 4 + 2, 1, 7 + 4 * da, peer(g, 0, 3)),
        ]

    cos = cosine[...]
    sin = sine[...]

    def turned(x):
        return x * cos + pltpu.roll(x, HEAD_DIM // 2, 1) * sin

    for g in range(2):
        total = None
        for n in range(2):
            q_loads[g][n].wait()
            term = jnp.dot(
                normed[:, pl.ds(n * half_depth, half_depth)],
                wq[g, n],
                preferred_element_type=F32,
            )
            total = term if total is None else total + term
        for h in range(GROUP):
            qbuf[g, 0, pl.ds(h * SEL, SEL), :] = turned(total[:, h * 128 : (h + 1) * 128]).astype(
                BF16
            )
        for copy in a_sends(g):
            copy.start()
    for g in range(2):
        for copy in b_sends(g, 0):
            copy.start()

    for n, buf in enumerate((kbuf, vbuf)):
        kv_loads[n].wait()
        made = jnp.dot(normed[...], wkv[n], preferred_element_type=F32)
        for g in range(2):
            value = made[:, g * 128 : (g + 1) * 128]
            if n == 0:
                value = turned(value)
            buf[g, pl.ds(BLOCK, SEL), :] = value.astype(BF16)
            buf[g, pl.ds(BLOCK + SEL, FRESH - SEL), :] = jnp.zeros((FRESH - SEL, 128), BF16)
            fresh[pl.ds(2 * n + g, SEL, stride=4), :] = value
        fresh_copies[n].start()
    new_ref[...] = fresh[...].astype(BF16)

    def arrive(t, g):
        da = line_of(t)
        row = t // 4

        @pl.when(jnp.logical_or(t == 1, t == 2))
        def _():
            whole(g, 0, da * 4, 0, peer(g, 1, 0)).wait_recv()

        @pl.when(t == 1)
        def _():
            a_forward(g, 1).start()

        @pl.when(t == 2)
        def _():
            a_forward(g, 3).start()

        @pl.when(t == 3)
        def _():
            for half in range(2):
                halved(g, 0, 8, half, 0, peer(g, 1, 0)).wait_recv()

        @pl.when(row == 0)
        def _():
            for copy in b_sends(g, da):
                copy.start()

        @pl.when(row == 1)
        def _():
            for db in (1, 3):
                whole(g, 0, da * 4 + db, 0, peer(g, 1, 0)).wait_recv()
            for copy in b_forwards(g, da):
                copy.start()

        @pl.when(row == 2)
        def _():
            for half in range(2):
                halved(g, 0, da * 4 + 2, half, 0, peer(g, 1, 0)).wait_recv()

    def score(t, g):
        da = line_of(t)
        owner = peer(g, da, t // 4)
        s = lax.dot_general(
            qbuf[g, da * 4 + t // 4],
            kbuf[g],
            (((1,), (1,)), ((), ())),
            preferred_element_type=F32,
        )
        row = jnp.broadcast_to(row_pos[pl.ds(owner, 1), :], (128, 128)).T[:SEL, :1]
        pos = jnp.concatenate([row] * GROUP, 0)
        s = jnp.where(key_pos[...] <= pos, s, NEG)
        scores[g] = s
        tops[g] = jnp.broadcast_to(jnp.max(s, -1, keepdims=True), (ROWS, 128))

    def weigh(t, g):
        top = tops[g]
        e = jnp.exp2((scores[g] - top[:, :1]) * LOG_SCALE).astype(BF16)
        table = jnp.concatenate([vbuf[g], jnp.ones((KEYS, 128), BF16)], 1)
        summed = jnp.dot(e, table, preferred_element_type=F32)
        total = summed[:, 128:]
        part[g, t] = (summed[:, :128] / total).astype(BF16)
        stat[g, t] = pack_rows(top * LOG_SCALE + jnp.log2(total))

    def b_result(g, t, da, db):
        to = at(peer(g, 0, db))
        return [
            pltpu.make_async_remote_copy(
                src_ref=src.at[g, t],
                dst_ref=dst.at[g, da, db - 1],
                send_sem=ssem.at[g, da, db - 1],
                recv_sem=rsem.at[g, da, db - 1],
                device_id=to,
                device_id_type=MESH,
            )
            for src, dst, ssem, rsem in (
                (part, rb_part, bp_ssem, bp_rsem),
                (stat, rb_stat, bs_ssem, bs_rsem),
            )
        ]

    def a_result(g, da):
        to = at(peer(g, da, 0))
        return [
            pltpu.make_async_remote_copy(
                src_ref=src.at[g, da - 1],
                dst_ref=dst.at[g, da - 1],
                send_sem=ssem.at[g, da - 1],
                recv_sem=rsem.at[g, da - 1],
                device_id=to,
                device_id_type=MESH,
            )
            for src, dst, ssem, rsem in (
                (mid, ra_part, ap_ssem, ap_rsem),
                (mid_stat, ra_stat, as_ssem, as_rsem),
            )
        ]

    def line_sum(g, da, t):
        for db in range(1, SIDE):
            for copy in b_result(g, 0, da, db):
                copy.wait_recv()
        return merge(
            [part[g, t]] + [rb_part[g, da, n] for n in range(3)],
            [stat[g, t]] + [rb_stat[g, da, n] for n in range(3)],
        )

    def finish_line(da, t):
        for g in range(2):
            merged, logs = line_sum(g, da, t)
            mid[g, da - 1] = merged.astype(BF16)
            mid_stat[g, da - 1] = logs
            for copy in a_result(g, da):
                copy.start()

    def pass_on(t, g):
        for copy in b_result(g, t, line_of(t), t // 4):
            copy.start()

    for copy in stored_copies + fresh_copies:
        copy.wait_recv()
    score(0, 0)

    def step(t, carry):
        @pl.when(t > 0)
        def _():
            arrive(t, 1)

        @pl.when(t == 14)
        def _():
            finish_line(2, 3)

        score(t, 1)
        weigh(t, 0)

        @pl.when(t >= 4)
        def _():
            pass_on(t, 0)

        arrive(t + 1, 0)
        score(t + 1, 0)
        weigh(t, 1)

        @pl.when(t >= 4)
        def _():
            pass_on(t, 1)

        return carry

    lax.fori_loop(0, 15, step, 0)
    score(15, 1)
    weigh(15, 0)
    pass_on(15, 0)
    finish_line(1, 1)
    weigh(15, 1)
    pass_on(15, 1)
    finish_line(3, 2)
    for g in range(2):
        merged, logs = line_sum(g, 0, 0)
        part[g, 0] = merged.astype(BF16)
        stat[g, 0] = logs
    for g in range(2):
        for da in (2, 1, 3):
            for copy in a_result(g, da):
                copy.wait_recv()
        merged, _ = merge(
            [part[g, 0]] + [ra_part[g, n] for n in range(3)],
            [stat[g, 0]] + [ra_stat[g, n] for n in range(3)],
        )
        for h in range(GROUP):
            ctx[:, pl.ds((g * GROUP + h) * 128, 128)] = merged[h * SEL : (h + 1) * SEL].astype(BF16)

    for copy in weights:
        copy.wait()

    lower = pl.ds(0, SEL // 2)
    upper = pl.ds(SEL // 2, SEL // 2)

    def z_copy(index, src, dst, dz):
        return pltpu.make_async_remote_copy(
            src_ref=src,
            dst_ref=dst,
            send_sem=z_ssem.at[index],
            recv_sem=z_rsem.at[index],
            device_id=above(dz),
            device_id_type=MESH,
        )

    def projected(dz):
        return jnp.dot(ctx[...], wbuf[lax.rem(head + dz, SIDE)], preferred_element_type=F32)

    up_far = z_copy(0, zsend.at[0, lower], zrelay.at[0], 1)
    down_far = z_copy(1, zsend.at[0, upper], zrelay.at[1], 3)
    up_free = z_copy(2, zsend.at[1, upper], zrecv.at[0, upper], 1)
    up_sum = z_copy(3, zsend.at[1, lower], zrecv.at[0, lower], 1)
    down_free = z_copy(4, zsend.at[2, lower], zrecv.at[1, lower], 3)
    down_sum = z_copy(5, zsend.at[2, upper], zrecv.at[1, upper], 3)
    zsend[0] = projected(2).astype(BF16)
    up_far.start()
    down_far.start()
    up = projected(1)
    zsend[1, upper] = up[SEL // 2 :].astype(BF16)
    up_free.start()
    up_far.wait_recv()
    zsend[1, lower] = (up[: SEL // 2] + zrelay[0].astype(F32)).astype(BF16)
    up_sum.start()
    down = projected(3)
    zsend[2, lower] = down[: SEL // 2].astype(BF16)
    down_free.start()
    down_far.wait_recv()
    zsend[2, upper] = (down[SEL // 2 :] + zrelay[1].astype(F32)).astype(BF16)
    down_sum.start()
    total = projected(0)
    for copy in (up_free, up_sum, down_free, down_sum):
        copy.wait_recv()
    out_ref[...] = (total + zrecv[0].astype(F32) + zrecv[1].astype(F32)).astype(BF16)

    for copy in stored_copies + fresh_copies:
        copy.wait_send()
    for g in range(2):
        for copy in a_sends(g) + [a_forward(g, 3), a_forward(g, 1)]:
            copy.wait_send()
        for da in range(4):
            for copy in b_sends(g, da) + b_forwards(g, da):
                copy.wait_send()
            for db in range(1, 4):
                for copy in b_result(g, 0, da, db):
                    copy.wait_send()
        for da in range(1, 4):
            for copy in a_result(g, da):
                copy.wait_send()
    for copy in (up_far, down_far, up_free, up_sum, down_free, down_sum):
        copy.wait_send()


def attend(*operands):
    vmem = pl.BlockSpec(memory_space=pltpu.VMEM)
    smem = pl.BlockSpec(memory_space=pltpu.SMEM)
    hbm = pl.BlockSpec(memory_space=pl.ANY)
    dma = pltpu.SemaphoreType.DMA
    return pl.pallas_call(
        kernel,
        out_shape=(
            jax.ShapeDtypeStruct((SEL, 1024), BF16),
            jax.ShapeDtypeStruct((4 * SEL, 128), BF16),
        ),
        in_specs=[smem, smem, hbm, vmem, vmem, vmem, vmem, hbm, hbm, hbm, hbm, hbm],
        out_specs=(vmem, vmem),
        scratch_shapes=[
            pltpu.VMEM((SEL, D), BF16),
            pltpu.VMEM((SEL, D), BF16),
            pltpu.VMEM((2, 2, D // 2, 512), BF16),
            pltpu.VMEM((2, D, 256), BF16),
            pltpu.VMEM((4 * BLOCK, 128), BF16),
            pltpu.VMEM((4 * BLOCK, 128), F32),
            pltpu.VMEM((4 * SEL, 128), F32),
            pltpu.VMEM((1, KEYS), F32),
            pltpu.VMEM((2, 16, ROWS, 128), BF16),
            pltpu.VMEM((2, KEYS, 128), BF16),
            pltpu.VMEM((2, KEYS, 128), BF16),
            pltpu.VMEM((SIDE, 1024, 1024), BF16),
            pltpu.VMEM((2, ROWS, KEYS), F32),
            pltpu.VMEM((2, ROWS, 128), F32),
            pltpu.VMEM((2, 16, ROWS, 128), BF16),
            pltpu.VMEM((2, 16, 8, 128), F32),
            pltpu.VMEM((2, 4, 3, ROWS, 128), BF16),
            pltpu.VMEM((2, 4, 3, 8, 128), F32),
            pltpu.VMEM((2, 3, ROWS, 128), BF16),
            pltpu.VMEM((2, 3, 8, 128), F32),
            pltpu.VMEM((2, 3, ROWS, 128), BF16),
            pltpu.VMEM((2, 3, 8, 128), F32),
            pltpu.VMEM((SEL, 1024), BF16),
            pltpu.VMEM((3, SEL, 1024), BF16),
            pltpu.VMEM((2, SEL // 2, 1024), BF16),
            pltpu.VMEM((2, SEL, 1024), BF16),
            dma((12,)),
            dma((4,)),
            dma((4,)),
            dma((2, 20)),
            dma((2, 16, 2)),
            dma((2, 4, 3)),
            dma((2, 4, 3)),
            dma((2, 4, 3)),
            dma((2, 4, 3)),
            dma((2, 3)),
            dma((2, 3)),
            dma((2, 3)),
            dma((2, 3)),
            dma((6,)),
            dma((6,)),
        ],
        compiler_params=pltpu.CompilerParams(
            collective_id=0, has_side_effects=True, vmem_limit_bytes=64_000_000
        ),
    )(*operands)


def body(
    hidden, norm_gain, w_query, w_key, w_value, w_out, stored_kv, selected, prompt_order, store_slot
):
    positions = lax.dynamic_slice_in_dim(selected, lax.axis_index("seq") * SEL, SEL)
    half = HEAD_DIM // 2
    freq = 500000.0 ** (-(jnp.arange(half, dtype=jnp.float32) * 2.0 / HEAD_DIM))
    angle = positions.astype(jnp.float32)[:, None] * freq[None, :]
    cosine = jnp.cos(angle)
    sine = jnp.sin(angle)
    row_pos = jnp.pad(selected.astype(F32).reshape(-1, SEL), ((0, 0), (0, 128 - SEL)))
    attn_out, new_kv = attend(
        prompt_order,
        store_slot,
        hidden,
        norm_gain[None],
        jnp.concatenate([cosine, cosine], 1),
        jnp.concatenate([-sine, sine], 1),
        row_pos,
        stored_kv.reshape(-1, HEAD_DIM),
        w_query,
        w_key,
        w_value,
        w_out,
    )
    return (attn_out, new_kv.reshape(SEL, 2, 2, HEAD_DIM))


def solution(mesh):
    in_specs = (
        P("seq", None),
        P(),
        P(None, "head"),
        P(None, "head"),
        P(None, "head"),
        P("head", None),
        P("seq", None, "head", None),
        P(),
        P(),
        P(),
    )
    out_specs = (P("seq", "head"), P("seq", None, "head", None))
    return jax.shard_map(body, mesh=mesh, in_specs=in_specs, out_specs=out_specs, check_vma=False)
```

```python
import functools

import jax
import jax.numpy as jnp
from jax import lax
from jax.experimental import pallas as pl
from jax.experimental.pallas import tpu as pltpu
from jax.sharding import PartitionSpec as P

D = 4096
HEADS = 32
KV_HEADS = 8
HEAD_DIM = 128
PASSAGE = 4096
PASSAGES = 8
SIDE = 4
GROUP = HEADS // KV_HEADS
BLOCK = 1024
SEL = 96
FRESH = 128
HALF_KEYS = BLOCK + FRESH
KEYS = 2 * HALF_KEYS
ROWS = GROUP * SEL
FAR = 1.0e9
NEG = -1.0e30
LOG_SCALE = 1.4426950408889634 / HEAD_DIM**0.5
F32 = jnp.float32
BF16 = jnp.bfloat16
MESH = pl.DeviceIdType.MESH


WALK = (
    (0, 1), (0, 3), (0, 2), (1, 1), (1, 3), (3, 1), (3, 3), (1, 2),
    (3, 2), (2, 1), (2, 3), (2, 2), (1, 0), (2, 0), (3, 0), (0, 0),
)
OWN = {da: t for t, (da, db) in enumerate(WALK) if db == 0}


def offset(t, axis):
    if isinstance(t, int):
        return WALK[t][axis]
    found = jnp.int32(0)
    for n, pair in enumerate(WALK):
        found = jnp.where(t == n, pair[axis], found)
    return found


def pack_rows(column):
    lane = lax.broadcasted_iota(jnp.int32, (SEL, 128), 1)
    total = jnp.zeros((SEL, 128), F32)
    for h in range(GROUP):
        total = jnp.where(lane == h, column[h * SEL : (h + 1) * SEL], total)
    square = jnp.concatenate([total, jnp.zeros((128 - SEL, 128), F32)], 0)
    return square.T[:8]


def unpack_rows(packed):
    square = jnp.concatenate([packed, jnp.zeros((120, 128), F32)], 0).T
    return jnp.concatenate(
        [jnp.broadcast_to(square[:SEL, h : h + 1], (SEL, 128)) for h in range(GROUP)], 0
    )


def merge(parts, stats):
    top = functools.reduce(jnp.maximum, stats)
    factors = [jnp.exp2(s - top) for s in stats]
    total = functools.reduce(jnp.add, factors)
    merged = sum(
        part.astype(F32) * unpack_rows(factor / total) for part, factor in zip(parts, factors)
    )
    return merged, top + jnp.log2(total)


def kernel(
    order_in,
    slot_in,
    hidden_in,
    gain_in,
    freq_in,
    selected_in,
    stored_in,
    w_query_in,
    w_key_in,
    w_value_in,
    w_out_in,
    out_ref,
    new_ref,
    prompt_order,
    store_slot,
    gain,
    freq,
    listed,
    row_pos,
    hid,
    normed,
    wq,
    wkv,
    stored,
    wide,
    fresh,
    key_pos,
    qbuf,
    kbuf,
    vbuf,
    wbuf,
    scores,
    tops,
    part,
    stat,
    rb_part,
    rb_stat,
    mid,
    mid_stat,
    ra_part,
    ra_stat,
    ctx,
    zsend,
    zrelay,
    zrecv,
    local_sem,
    kv_ssem,
    kv_rsem,
    g_ssem,
    g_rsem,
    bp_ssem,
    bp_rsem,
    bs_ssem,
    bs_rsem,
    ap_ssem,
    ap_rsem,
    as_ssem,
    as_rsem,
    z_ssem,
    z_rsem,
):
    seq = lax.axis_index("seq")
    head = lax.axis_index("head")
    core = lax.rem(seq, 2)
    chip_x = lax.rem(seq // 2, SIDE)
    chip_y = seq // (2 * SIDE)

    def chip_seq(dx, dy):
        return (lax.rem(chip_y + dy, SIDE) * SIDE + lax.rem(chip_x + dx, SIDE)) * 2 + core

    def peer(g, da, db):
        return chip_seq(da, db) if g == 0 else chip_seq(db, da)

    def at(index):
        return (index, head)

    def above(dz):
        return (seq, lax.rem(head + dz, SIDE))

    other_seq = seq + 1 - 2 * core
    partner = (other_seq, head)

    barrier = pltpu.get_barrier_semaphore()
    others = [partner]
    for d in range(1, SIDE):
        others.append(at(chip_seq(d, 0)))
        others.append(at(chip_seq(0, d)))
    others += [above(1), above(3)]
    for other in others:
        pl.semaphore_signal(barrier, inc=1, device_id=other, device_id_type=MESH)

    load = pltpu.make_async_copy
    half_depth = D // 2
    own_hidden = load(hidden_in, hid, local_sem.at[0])
    own_stored = load(stored_in, stored, local_sem.at[1])
    q_loads = [
        [
            load(
                w_query_in.at[pl.ds(n * half_depth, half_depth), pl.ds(g * 512, 512)],
                wq.at[g, n],
                local_sem.at[2 + 2 * g + n],
            )
            for n in range(2)
        ]
        for g in range(2)
    ]
    kv_loads = [
        load(src, wkv.at[n], local_sem.at[6 + n]) for n, src in enumerate((w_key_in, w_value_in))
    ]
    weights = [
        load(w_out_in.at[:, pl.ds(n * 1024, 1024)], wbuf.at[n], local_sem.at[8 + n])
        for n in range(SIDE)
    ]
    small = [
        load(src, dst, local_sem.at[12 + n])
        for n, (src, dst) in enumerate(
            (
                (selected_in, listed),
                (freq_in, freq),
                (gain_in, gain),
                (order_in, prompt_order),
                (slot_in, store_slot),
            )
        )
    ]
    for copy in small:
        copy.start()
    own_hidden.start()
    q_loads[0][0].start()
    own_stored.start()
    q_loads[0][1].start()
    for copy in q_loads[1] + kv_loads + weights:
        copy.start()

    for copy in small:
        copy.wait()

    wide[pl.ds(0, 24), :] = listed[...].astype(F32)
    thirds = [wide[pl.ds(n, 8, stride=3), :] for n in range(3)]
    lane = lax.broadcasted_iota(jnp.int32, (8, 128), 1)
    roll = pltpu.roll
    for n, rows in enumerate(
        (
            thirds[0],
            jnp.where(lane < 32, roll(thirds[0], 32, 1), roll(thirds[1], 32, 1)),
            jnp.where(lane < 64, roll(thirds[1], 64, 1), roll(thirds[2], 64, 1)),
            roll(thirds[2], 96, 1),
        )
    ):
        row_pos[pl.ds(n, 8, stride=4), :] = rows

    angle = jnp.broadcast_to(row_pos[pl.ds(seq, 1), :], (128, 128)).T[:SEL] * freq[...]
    cos = jnp.cos(angle)
    sin = jnp.sin(angle)
    sin = jnp.where(lax.broadcasted_iota(jnp.int32, (SEL, 128), 1) < HEAD_DIM // 2, -sin, sin)

    order = [store_slot[prompt_order[i]] for i in range(PASSAGES)]
    lanes = lax.broadcasted_iota(jnp.int32, (1, BLOCK), 1)
    short = lax.broadcasted_iota(jnp.int32, (1, FRESH), 1)
    per_passage = PASSAGE // BLOCK
    for n, device in enumerate((seq, other_seq)):
        place = jnp.int32(0)
        for i in range(PASSAGES):
            place = jnp.where(order[i] == device // per_passage, i, place)
        block = place * per_passage + lax.rem(device, per_passage)
        there = (block * BLOCK + lanes).astype(F32)
        replaced = jnp.broadcast_to(row_pos[pl.ds(block, 1), :], (128, 128)).T[:SEL, :1]
        gone = jnp.max(jnp.where(replaced == there, FAR, 0.0), 0, keepdims=True)
        key_pos[:, pl.ds(n * HALF_KEYS, BLOCK)] = there + gone
        key_pos[:, pl.ds(n * HALF_KEYS + BLOCK, FRESH)] = jnp.where(
            short < SEL, row_pos[pl.ds(device, 1), :], FAR
        )

    own_hidden.wait()
    widened = hid[...].astype(F32)
    mean = jnp.mean(widened * widened, -1, keepdims=True)
    normed[...] = (widened * lax.rsqrt(mean + 1e-05) * gain[...]).astype(BF16)

    own_stored.wait()
    wide[...] = stored[...].astype(F32)
    for n, buf in enumerate((kbuf, vbuf)):
        for g in range(2):
            rows = wide[pl.ds(2 * n + g, BLOCK, stride=4), :]
            buf[g, pl.ds(0, BLOCK), :] = rows.astype(BF16)
    pl.semaphore_wait(barrier, len(others))

    def to_partner(n, first, count):
        buf = (kbuf, vbuf)[n]
        index = 2 * n + (first > 0)
        return pltpu.make_async_remote_copy(
            src_ref=buf.at[:, pl.ds(first, count)],
            dst_ref=buf.at[:, pl.ds(HALF_KEYS + first, count)],
            send_sem=kv_ssem.at[index],
            recv_sem=kv_rsem.at[index],
            device_id=partner,
            device_id_type=MESH,
        )

    stored_copies = [to_partner(n, 0, BLOCK) for n in range(2)]
    fresh_copies = [to_partner(n, BLOCK, FRESH) for n in range(2)]
    for copy in stored_copies:
        copy.start()

    def whole(g, src, dst, sem, to):
        return pltpu.make_async_remote_copy(
            src_ref=qbuf.at[g, src],
            dst_ref=qbuf.at[g, dst],
            send_sem=g_ssem.at[g, sem],
            recv_sem=g_rsem.at[g, dst, 0],
            device_id=at(to),
            device_id_type=MESH,
        )

    def halved(g, src, dst, half, sem, to):
        rows = pl.ds(half * (ROWS // 2), ROWS // 2)
        return pltpu.make_async_remote_copy(
            src_ref=qbuf.at[g, src, rows],
            dst_ref=qbuf.at[g, dst, rows],
            send_sem=g_ssem.at[g, sem],
            recv_sem=g_rsem.at[g, dst, half],
            device_id=at(to),
            device_id_type=MESH,
        )

    def a_sends(g):
        return [whole(g, 0, 12, 0, peer(g, 1, 0)), whole(g, 0, 4, 1, peer(g, 3, 0))]

    def a_forward(g, da):
        if da == 3:
            return halved(g, 12, 8, 0, 2, peer(g, 1, 0))
        return halved(g, 4, 8, 1, 3, peer(g, 3, 0))

    def b_sends(g, da):
        return [
            whole(g, da * 4, da * 4 + 3, 4 + 4 * da, peer(g, 0, 1)),
            whole(g, da * 4, da * 4 + 1, 5 + 4 * da, peer(g, 0, 3)),
        ]

    def b_forwards(g, da):
        return [
            halved(g, da * 4 + 3, da * 4 + 2, 0, 6 + 4 * da, peer(g, 0, 1)),
            halved(g, da * 4 + 1, da * 4 + 2, 1, 7 + 4 * da, peer(g, 0, 3)),
        ]

    def turned(x):
        return x * cos + pltpu.roll(x, HEAD_DIM // 2, 1) * sin

    for g in range(2):
        total = None
        for n in range(2):
            q_loads[g][n].wait()
            term = jnp.dot(
                normed[:, pl.ds(n * half_depth, half_depth)],
                wq[g, n],
                preferred_element_type=F32,
            )
            total = term if total is None else total + term
        for h in range(GROUP):
            qbuf[g, 0, pl.ds(h * SEL, SEL), :] = turned(total[:, h * 128 : (h + 1) * 128]).astype(
                BF16
            )
        for copy in a_sends(g) + b_sends(g, 0):
            copy.start()

    for n, buf in enumerate((kbuf, vbuf)):
        kv_loads[n].wait()
        made = jnp.dot(normed[...], wkv[n], preferred_element_type=F32)
        for g in range(2):
            value = made[:, g * 128 : (g + 1) * 128]
            if n == 0:
                value = turned(value)
            buf[g, pl.ds(BLOCK, SEL), :] = value.astype(BF16)
            buf[g, pl.ds(BLOCK + SEL, FRESH - SEL), :] = jnp.zeros((FRESH - SEL, 128), BF16)
            fresh[pl.ds(2 * n + g, SEL, stride=4), :] = value
        fresh_copies[n].start()
    new_ref[...] = fresh[...].astype(BF16)

    def full(g, da, db):
        whole(g, 0, da * 4 + db, 0, peer(g, 1, 0)).wait_recv()

    def both_halves(g, da, db):
        for half in range(2):
            halved(g, 0, da * 4 + db, half, 0, peer(g, 1, 0)).wait_recv()

    def arrive(t, g):
        @pl.when(t == 0)
        def _():
            for db in (1, 3):
                full(g, 0, db)
            for copy in b_forwards(g, 0):
                copy.start()
            for da in (1, 3):
                full(g, da, 0)
                a_forward(g, da).start()
            for copy in b_sends(g, 1) + b_sends(g, 3):
                copy.start()

        @pl.when(t == 2)
        def _():
            both_halves(g, 0, 2)
            both_halves(g, 2, 0)
            for copy in b_sends(g, 2):
                copy.start()

        for first, da in ((3, 1), (5, 3), (9, 2)):

            @pl.when(t == first)
            def _(da=da):
                for db in (1, 3):
                    full(g, da, db)
                for copy in b_forwards(g, da):
                    copy.start()

        for last, da in ((7, 1), (8, 3), (11, 2)):

            @pl.when(t == last)
            def _(da=da):
                both_halves(g, da, 2)

    def score(t, g):
        da, db = offset(t, 0), offset(t, 1)
        owner = peer(g, da, db)
        s = lax.dot_general(
            qbuf[g, da * 4 + db],
            kbuf[g],
            (((1,), (1,)), ((), ())),
            preferred_element_type=F32,
        )
        row = jnp.broadcast_to(row_pos[pl.ds(owner, 1), :], (128, 128)).T[:SEL, :1]
        pos = jnp.concatenate([row] * GROUP, 0)
        s = jnp.where(key_pos[...] <= pos, s, NEG)
        scores[g] = s
        tops[g] = functools.reduce(
            jnp.maximum, [s[:, n * 128 : (n + 1) * 128] for n in range(KEYS // 128)]
        )

    def weigh(t, g):
        top = jnp.broadcast_to(jnp.max(tops[g], -1, keepdims=True), (ROWS, 128))
        e = jnp.exp2((scores[g] - top[:, :1]) * LOG_SCALE).astype(BF16)
        table = jnp.concatenate([vbuf[g], jnp.ones((KEYS, 128), BF16)], 1)
        summed = jnp.dot(e, table, preferred_element_type=F32)
        total = summed[:, 128:]
        part[g, t] = (summed[:, :128] / total).astype(BF16)
        stat[g, t] = pack_rows(top * LOG_SCALE + jnp.log2(total))

    def b_result(g, t, da, db):
        to = at(peer(g, 0, db))
        return [
            pltpu.make_async_remote_copy(
                src_ref=src.at[g, t],
                dst_ref=dst.at[g, da, db - 1],
                send_sem=ssem.at[g, da, db - 1],
                recv_sem=rsem.at[g, da, db - 1],
                device_id=to,
                device_id_type=MESH,
            )
            for src, dst, ssem, rsem in (
                (part, rb_part, bp_ssem, bp_rsem),
                (stat, rb_stat, bs_ssem, bs_rsem),
            )
        ]

    def a_result(g, da):
        to = at(peer(g, da, 0))
        return [
            pltpu.make_async_remote_copy(
                src_ref=src.at[g, da - 1],
                dst_ref=dst.at[g, da - 1],
                send_sem=ssem.at[g, da - 1],
                recv_sem=rsem.at[g, da - 1],
                device_id=to,
                device_id_type=MESH,
            )
            for src, dst, ssem, rsem in (
                (mid, ra_part, ap_ssem, ap_rsem),
                (mid_stat, ra_stat, as_ssem, as_rsem),
            )
        ]

    def line(g, da):
        for db in range(1, SIDE):
            for copy in b_result(g, 0, da, db):
                copy.wait_recv()
        t = OWN[da]
        return (
            [part[g, t]] + [rb_part[g, da, n] for n in range(3)],
            [stat[g, t]] + [rb_stat[g, da, n] for n in range(3)],
        )

    def finish_line(da):
        for g in range(2):
            merged, logs = merge(*line(g, da))
            mid[g, da - 1] = merged.astype(BF16)
            mid_stat[g, da - 1] = logs
            for copy in a_result(g, da):
                copy.start()

    def pass_on(t, g):
        @pl.when(t < 12)
        def _():
            for copy in b_result(g, t, offset(t, 0), offset(t, 1)):
                copy.start()

    for copy in stored_copies + fresh_copies:
        copy.wait_recv()
    arrive(jnp.int32(0), 0)
    score(0, 0)

    def step(t, carry):
        arrive(t, 1)
        for da in (1, 2):

            @pl.when(t == OWN[da] + 1)
            def _(da=da):
                finish_line(da)

        score(t, 1)
        weigh(t, 0)
        pass_on(t, 0)
        arrive(t + 1, 0)
        score(t + 1, 0)
        weigh(t, 1)
        pass_on(t, 1)
        return carry

    lax.fori_loop(0, 15, step, 0)
    finish_line(3)
    score(15, 1)
    weigh(15, 0)
    weigh(15, 1)
    for g in range(2):
        parts, stats = line(g, 0)
        for da in (1, 2, 3):
            for copy in a_result(g, da):
                copy.wait_recv()
        merged, _ = merge(
            parts + [ra_part[g, n] for n in range(3)], stats + [ra_stat[g, n] for n in range(3)]
        )
        for h in range(GROUP):
            ctx[:, pl.ds((g * GROUP + h) * 128, 128)] = merged[h * SEL : (h + 1) * SEL].astype(BF16)

    for copy in weights:
        copy.wait()

    lower = pl.ds(0, SEL // 2)
    upper = pl.ds(SEL // 2, SEL // 2)

    def z_copy(index, src, dst, dz):
        return pltpu.make_async_remote_copy(
            src_ref=src,
            dst_ref=dst,
            send_sem=z_ssem.at[index],
            recv_sem=z_rsem.at[index],
            device_id=above(dz),
            device_id_type=MESH,
        )

    def projected(dz):
        return jnp.dot(ctx[...], wbuf[lax.rem(head + dz, SIDE)], preferred_element_type=F32)

    up_far = z_copy(0, zsend.at[0, lower], zrelay.at[0], 1)
    down_far = z_copy(1, zsend.at[0, upper], zrelay.at[1], 3)
    up_free = z_copy(2, zsend.at[1, upper], zrecv.at[0, upper], 1)
    up_sum = z_copy(3, zsend.at[1, lower], zrecv.at[0, lower], 1)
    down_free = z_copy(4, zsend.at[2, lower], zrecv.at[1, lower], 3)
    down_sum = z_copy(5, zsend.at[2, upper], zrecv.at[1, upper], 3)
    zsend[0] = projected(2).astype(BF16)
    up_far.start()
    down_far.start()
    up = projected(1)
    zsend[1, upper] = up[SEL // 2 :].astype(BF16)
    up_free.start()
    up_far.wait_recv()
    zsend[1, lower] = (up[: SEL // 2] + zrelay[0].astype(F32)).astype(BF16)
    up_sum.start()
    down = projected(3)
    zsend[2, lower] = down[: SEL // 2].astype(BF16)
    down_free.start()
    down_far.wait_recv()
    zsend[2, upper] = (down[SEL // 2 :] + zrelay[1].astype(F32)).astype(BF16)
    down_sum.start()
    total = projected(0)
    for copy in (up_free, up_sum, down_free, down_sum):
        copy.wait_recv()
    out_ref[...] = (total + zrecv[0].astype(F32) + zrecv[1].astype(F32)).astype(BF16)

    for copy in stored_copies + fresh_copies:
        copy.wait_send()
    for g in range(2):
        for copy in a_sends(g) + [a_forward(g, 3), a_forward(g, 1)]:
            copy.wait_send()
        for da in range(4):
            for copy in b_sends(g, da) + b_forwards(g, da):
                copy.wait_send()
            for db in range(1, 4):
                for copy in b_result(g, 0, da, db):
                    copy.wait_send()
        for da in range(1, 4):
            for copy in a_result(g, da):
                copy.wait_send()
    for copy in (up_far, down_far, up_free, up_sum, down_free, down_sum):
        copy.wait_send()


def attend(*operands):
    vmem = pl.BlockSpec(memory_space=pltpu.VMEM)
    hbm = pl.BlockSpec(memory_space=pl.ANY)
    dma = pltpu.SemaphoreType.DMA
    return pl.pallas_call(
        kernel,
        out_shape=(
            pltpu.VMEM((SEL, 1024), BF16),
            pltpu.VMEM((4 * SEL, 128), BF16),
        ),
        in_specs=[hbm] * 11,
        out_specs=(vmem, vmem),
        scratch_shapes=[
            pltpu.SMEM((PASSAGES,), jnp.int32),
            pltpu.SMEM((PASSAGES,), jnp.int32),
            pltpu.VMEM((1, D), F32),
            pltpu.VMEM((1, 128), F32),
            pltpu.VMEM((24, 128), jnp.int32),
            pltpu.VMEM((32, 128), F32),
            pltpu.VMEM((SEL, D), BF16),
            pltpu.VMEM((SEL, D), BF16),
            pltpu.VMEM((2, 2, D // 2, 512), BF16),
            pltpu.VMEM((2, D, 256), BF16),
            pltpu.VMEM((4 * BLOCK, 128), BF16),
            pltpu.VMEM((4 * BLOCK, 128), F32),
            pltpu.VMEM((4 * SEL, 128), F32),
            pltpu.VMEM((1, KEYS), F32),
            pltpu.VMEM((2, 16, ROWS, 128), BF16),
            pltpu.VMEM((2, KEYS, 128), BF16),
            pltpu.VMEM((2, KEYS, 128), BF16),
            pltpu.VMEM((SIDE, 1024, 1024), BF16),
            pltpu.VMEM((2, ROWS, KEYS), F32),
            pltpu.VMEM((2, ROWS, 128), F32),
            pltpu.VMEM((2, 16, ROWS, 128), BF16),
            pltpu.VMEM((2, 16, 8, 128), F32),
            pltpu.VMEM((2, 4, 3, ROWS, 128), BF16),
            pltpu.VMEM((2, 4, 3, 8, 128), F32),
            pltpu.VMEM((2, 3, ROWS, 128), BF16),
            pltpu.VMEM((2, 3, 8, 128), F32),
            pltpu.VMEM((2, 3, ROWS, 128), BF16),
            pltpu.VMEM((2, 3, 8, 128), F32),
            pltpu.VMEM((SEL, 1024), BF16),
            pltpu.VMEM((3, SEL, 1024), BF16),
            pltpu.VMEM((2, SEL // 2, 1024), BF16),
            pltpu.VMEM((2, SEL, 1024), BF16),
            dma((17,)),
            dma((4,)),
            dma((4,)),
            dma((2, 20)),
            dma((2, 16, 2)),
            dma((2, 4, 3)),
            dma((2, 4, 3)),
            dma((2, 4, 3)),
            dma((2, 4, 3)),
            dma((2, 3)),
            dma((2, 3)),
            dma((2, 3)),
            dma((2, 3)),
            dma((6,)),
            dma((6,)),
        ],
        compiler_params=pltpu.CompilerParams(
            collective_id=0, has_side_effects=True, vmem_limit_bytes=64_000_000
        ),
    )(*operands)


def body(
    hidden, norm_gain, w_query, w_key, w_value, w_out, stored_kv, selected, prompt_order, store_slot
):
    half = HEAD_DIM // 2
    index = jnp.arange(HEAD_DIM, dtype=jnp.int32) % half
    freq = 500000.0 ** (-(index.astype(F32) * 2.0 / HEAD_DIM))
    attn_out, new_kv = attend(
        prompt_order,
        store_slot,
        hidden,
        norm_gain[None],
        freq[None],
        selected.reshape(24, 128),
        stored_kv.reshape(-1, HEAD_DIM),
        w_query,
        w_key,
        w_value,
        w_out,
    )
    return (attn_out, new_kv.reshape(SEL, 2, 2, HEAD_DIM))


def solution(mesh):
    in_specs = (
        P("seq", None),
        P(),
        P(None, "head"),
        P(None, "head"),
        P(None, "head"),
        P("head", None),
        P("seq", None, "head", None),
        P(),
        P(),
        P(),
    )
    out_specs = (P("seq", "head"), P("seq", None, "head", None))
    return jax.shard_map(body, mesh=mesh, in_specs=in_specs, out_specs=out_specs, check_vma=False)
```

```python
import functools

import jax
import jax.numpy as jnp
from jax import lax
from jax.experimental import pallas as pl
from jax.experimental.pallas import tpu as pltpu
from jax.sharding import PartitionSpec as P

D = 4096
HEADS = 32
KV_HEADS = 8
HEAD_DIM = 128
PASSAGE = 4096
PASSAGES = 8
SIDE = 4
GROUP = HEADS // KV_HEADS
BLOCK = 1024
SEL = 96
FRESH = 128
KEYS = 2 * BLOCK
ROWS = GROUP * SEL
NEG = -1.0e30
LOG_SCALE = 1.4426950408889634 / HEAD_DIM**0.5
F32 = jnp.float32
BF16 = jnp.bfloat16
MESH = pl.DeviceIdType.MESH


WALK = (
    (0, 1), (0, 3), (0, 2), (1, 1), (1, 3), (3, 1), (3, 3), (1, 2),
    (3, 2), (2, 1), (2, 3), (2, 2), (1, 0), (2, 0), (3, 0), (0, 0),
)
OWN = {da: t for t, (da, db) in enumerate(WALK) if db == 0}


def offset(t, axis):
    if isinstance(t, int):
        return WALK[t][axis]
    found = jnp.int32(0)
    for n, pair in enumerate(WALK):
        found = jnp.where(t == n, pair[axis], found)
    return found


def pack_rows(column):
    lane = lax.broadcasted_iota(jnp.int32, (SEL, 128), 1)
    total = jnp.zeros((SEL, 128), F32)
    for h in range(GROUP):
        total = jnp.where(lane == h, column[h * SEL : (h + 1) * SEL], total)
    square = jnp.concatenate([total, jnp.zeros((128 - SEL, 128), F32)], 0)
    return square.T[:8]


def unpack_rows(packed):
    square = jnp.concatenate([packed, jnp.zeros((120, 128), F32)], 0).T
    return jnp.concatenate(
        [jnp.broadcast_to(square[:SEL, h : h + 1], (SEL, 128)) for h in range(GROUP)], 0
    )


def merge(parts, stats):
    top = functools.reduce(jnp.maximum, stats)
    factors = [jnp.exp2(s - top) for s in stats]
    total = functools.reduce(jnp.add, factors)
    merged = sum(
        part.astype(F32) * unpack_rows(factor / total) for part, factor in zip(parts, factors)
    )
    return merged, top + jnp.log2(total)


def kernel(
    order_in,
    slot_in,
    hidden_in,
    gain_in,
    freq_in,
    selected_in,
    stored_in,
    w_query_in,
    w_key_in,
    w_value_in,
    w_out_in,
    out_ref,
    new_ref,
    prompt_order,
    store_slot,
    gain,
    freq,
    listed,
    row_pos,
    hid,
    normed,
    wq,
    wkv,
    stored,
    wide,
    fresh,
    made_kv,
    key_pos,
    qbuf,
    kbuf,
    vbuf,
    wbuf,
    scores,
    tops,
    part,
    stat,
    rb_part,
    rb_stat,
    mid,
    mid_stat,
    ra_part,
    ra_stat,
    ctx,
    zsend,
    zrelay,
    zrecv,
    local_sem,
    kv_ssem,
    kv_rsem,
    g_ssem,
    g_rsem,
    bp_ssem,
    bp_rsem,
    bs_ssem,
    bs_rsem,
    ap_ssem,
    ap_rsem,
    as_ssem,
    as_rsem,
    z_ssem,
    z_rsem,
):
    seq = lax.axis_index("seq")
    head = lax.axis_index("head")
    core = lax.rem(seq, 2)
    chip_x = lax.rem(seq // 2, SIDE)
    chip_y = seq // (2 * SIDE)

    def chip_seq(dx, dy):
        return (lax.rem(chip_y + dy, SIDE) * SIDE + lax.rem(chip_x + dx, SIDE)) * 2 + core

    def peer(g, da, db):
        return chip_seq(da, db) if g == 0 else chip_seq(db, da)

    def at(index):
        return (index, head)

    def above(dz):
        return (seq, lax.rem(head + dz, SIDE))

    other_seq = seq + 1 - 2 * core
    partner = (other_seq, head)

    barrier = pltpu.get_barrier_semaphore()
    others = [partner]
    for d in range(1, SIDE):
        others.append(at(chip_seq(d, 0)))
        others.append(at(chip_seq(0, d)))
    others += [above(1), above(3)]
    for other in others:
        pl.semaphore_signal(barrier, inc=1, device_id=other, device_id_type=MESH)

    load = pltpu.make_async_copy
    half_depth = D // 2
    own_hidden = load(hidden_in, hid, local_sem.at[0])
    own_stored = load(stored_in, stored, local_sem.at[1])
    q_loads = [
        [
            load(
                w_query_in.at[pl.ds(n * half_depth, half_depth), pl.ds(g * 512, 512)],
                wq.at[g, n],
                local_sem.at[2 + 2 * g + n],
            )
            for n in range(2)
        ]
        for g in range(2)
    ]
    kv_loads = [
        load(src, wkv.at[n], local_sem.at[6 + n]) for n, src in enumerate((w_key_in, w_value_in))
    ]
    weights = [
        load(w_out_in.at[:, pl.ds(n * 1024, 1024)], wbuf.at[n], local_sem.at[8 + n])
        for n in range(SIDE)
    ]
    small = [
        load(src, dst, local_sem.at[12 + n])
        for n, (src, dst) in enumerate(
            (
                (selected_in, listed),
                (freq_in, freq),
                (gain_in, gain),
                (order_in, prompt_order),
                (slot_in, store_slot),
            )
        )
    ]
    for copy in small:
        copy.start()
    own_hidden.start()
    for copy in q_loads[0]:
        copy.start()

    for copy in small:
        copy.wait()

    wide[pl.ds(0, 24), :] = listed[...].astype(F32)
    thirds = [wide[pl.ds(n, 8, stride=3), :] for n in range(3)]
    lane = lax.broadcasted_iota(jnp.int32, (8, 128), 1)
    roll = pltpu.roll
    for n, rows in enumerate(
        (
            thirds[0],
            jnp.where(lane < 32, roll(thirds[0], 32, 1), roll(thirds[1], 32, 1)),
            jnp.where(lane < 64, roll(thirds[1], 64, 1), roll(thirds[2], 64, 1)),
            roll(thirds[2], 96, 1),
        )
    ):
        row_pos[pl.ds(n, 8, stride=4), :] = rows

    angle = jnp.broadcast_to(row_pos[pl.ds(seq, 1), :], (128, 128)).T[:SEL] * freq[...]
    cos = jnp.cos(angle)
    sin = jnp.sin(angle)
    sin = jnp.where(lax.broadcasted_iota(jnp.int32, (SEL, 128), 1) < HEAD_DIM // 2, -sin, sin)

    order = [store_slot[prompt_order[i]] for i in range(PASSAGES)]
    lanes = lax.broadcasted_iota(jnp.int32, (1, BLOCK), 1)
    per_passage = PASSAGE // BLOCK
    blocks = []
    for n, device in enumerate((seq, other_seq)):
        place = jnp.int32(0)
        for i in range(PASSAGES):
            place = jnp.where(order[i] == device // per_passage, i, place)
        block = place * per_passage + lax.rem(device, per_passage)
        blocks.append(block)
        there = (block * BLOCK + lanes).astype(F32)
        replaced = jnp.broadcast_to(row_pos[pl.ds(block, 1), :], (128, 128)).T[:SEL, :1]
        made = jnp.broadcast_to(row_pos[pl.ds(device, 1), :], (128, 128)).T[:SEL, :1]
        put = jnp.sum(jnp.where(replaced == there, made + 1.0, 0.0), 0, keepdims=True)
        key_pos[:, pl.ds(n * BLOCK, BLOCK)] = jnp.where(put > 0.0, put - 1.0, there)

    own_hidden.wait()
    own_stored.start()
    q_loads[1][0].start()
    widened = hid[...].astype(F32)
    mean = jnp.mean(widened * widened, -1, keepdims=True)
    normed[...] = (widened * lax.rsqrt(mean + 1e-05) * gain[...]).astype(BF16)

    def to_partner(index, src, dst):
        return pltpu.make_async_remote_copy(
            src_ref=src,
            dst_ref=dst,
            send_sem=kv_ssem.at[index],
            recv_sem=kv_rsem.at[index],
            device_id=partner,
            device_id_type=MESH,
        )

    stored_copies = [
        to_partner(n, buf.at[:, pl.ds(0, BLOCK)], buf.at[:, pl.ds(BLOCK, BLOCK)])
        for n, buf in enumerate((kbuf, vbuf))
    ]
    fresh_copies = [to_partner(2 + n, made_kv.at[0, n], made_kv.at[1, n]) for n in range(2)]

    def whole(g, src, dst, sem, to):
        return pltpu.make_async_remote_copy(
            src_ref=qbuf.at[g, src],
            dst_ref=qbuf.at[g, dst],
            send_sem=g_ssem.at[g, sem],
            recv_sem=g_rsem.at[g, dst, 0],
            device_id=at(to),
            device_id_type=MESH,
        )

    def halved(g, src, dst, half, sem, to):
        rows = pl.ds(half * (ROWS // 2), ROWS // 2)
        return pltpu.make_async_remote_copy(
            src_ref=qbuf.at[g, src, rows],
            dst_ref=qbuf.at[g, dst, rows],
            send_sem=g_ssem.at[g, sem],
            recv_sem=g_rsem.at[g, dst, half],
            device_id=at(to),
            device_id_type=MESH,
        )

    def a_sends(g):
        return [whole(g, 0, 12, 0, peer(g, 1, 0)), whole(g, 0, 4, 1, peer(g, 3, 0))]

    def a_forward(g, da):
        if da == 3:
            return halved(g, 12, 8, 0, 2, peer(g, 1, 0))
        return halved(g, 4, 8, 1, 3, peer(g, 3, 0))

    def b_sends(g, da):
        return [
            whole(g, da * 4, da * 4 + 3, 4 + 4 * da, peer(g, 0, 1)),
            whole(g, da * 4, da * 4 + 1, 5 + 4 * da, peer(g, 0, 3)),
        ]

    def b_forwards(g, da):
        return [
            halved(g, da * 4 + 3, da * 4 + 2, 0, 6 + 4 * da, peer(g, 0, 1)),
            halved(g, da * 4 + 1, da * 4 + 2, 1, 7 + 4 * da, peer(g, 0, 3)),
        ]

    def turned(x):
        return x * cos + pltpu.roll(x, HEAD_DIM // 2, 1) * sin

    pl.semaphore_wait(barrier, len(others))
    later = {(0, 0): q_loads[1][1], (0, 1): kv_loads[0], (1, 0): kv_loads[1]}
    for g in range(2):
        total = None
        for n in range(2):
            q_loads[g][n].wait()
            if (g, n) in later:
                later[g, n].start()
            term = jnp.dot(
                normed[:, pl.ds(n * half_depth, half_depth)],
                wq[g, n],
                preferred_element_type=F32,
            )
            total = term if total is None else total + term
        for h in range(GROUP):
            qbuf[g, 0, pl.ds(h * SEL, SEL), :] = turned(total[:, h * 128 : (h + 1) * 128]).astype(
                BF16
            )
        for copy in a_sends(g) + b_sends(g, 0):
            copy.start()
        if g == 0:
            own_stored.wait()
            wide[...] = stored[...].astype(F32)
            for n, buf in enumerate((kbuf, vbuf)):
                for k in range(2):
                    rows = wide[pl.ds(2 * n + k, BLOCK, stride=4), :]
                    buf[k, pl.ds(0, BLOCK), :] = rows.astype(BF16)
                stored_copies[n].start()

    for n in range(2):
        kv_loads[n].wait()
        made = jnp.dot(normed[...], wkv[n], preferred_element_type=F32)
        made_kv[0, n, pl.ds(SEL, FRESH - SEL), :] = jnp.zeros((FRESH - SEL, 256), BF16)
        for g in range(2):
            value = made[:, g * 128 : (g + 1) * 128]
            if n == 0:
                value = turned(value)
            made_kv[0, n, pl.ds(0, SEL), pl.ds(g * 128, 128)] = value.astype(BF16)
            fresh[pl.ds(2 * n + g, SEL, stride=4), :] = value
        fresh_copies[n].start()
    for copy in weights:
        copy.start()

    def put_in(n):
        replaced = row_pos[pl.ds(blocks[n], 1), :]
        source = jnp.concatenate(
            [made_kv[n, 0], made_kv[n, 1], jnp.ones((FRESH, 128), BF16)], 1
        )
        for first in range(0, BLOCK, 256):
            there = blocks[n] * BLOCK + first + lax.broadcasted_iota(jnp.int32, (256, 128), 0)
            usable = lax.broadcasted_iota(jnp.int32, (256, 128), 1) < SEL
            chosen = jnp.logical_and(there.astype(F32) == replaced, usable)
            rows = jnp.dot(
                jnp.where(chosen, 1.0, 0.0).astype(BF16), source, preferred_element_type=F32
            )
            gone = rows[:, 512:] > 0.5
            where = pl.ds(n * BLOCK + first, 256)
            for k, (buf, g) in enumerate(((kbuf, 0), (kbuf, 1), (vbuf, 0), (vbuf, 1))):
                old = buf[g, where, :].astype(F32)
                buf[g, where, :] = jnp.where(gone, rows[:, k * 128 : (k + 1) * 128], old).astype(
                    BF16
                )

    for copy in stored_copies:
        copy.wait_send()
    put_in(0)
    new_ref[...] = fresh[...].astype(BF16)

    def full(g, da, db):
        whole(g, 0, da * 4 + db, 0, peer(g, 1, 0)).wait_recv()

    def both_halves(g, da, db):
        for half in range(2):
            halved(g, 0, da * 4 + db, half, 0, peer(g, 1, 0)).wait_recv()

    def arrive(t, g):
        @pl.when(t == 0)
        def _():
            for db in (1, 3):
                full(g, 0, db)
            for copy in b_forwards(g, 0):
                copy.start()
            for da in (1, 3):
                full(g, da, 0)
                a_forward(g, da).start()
            for copy in b_sends(g, 1) + b_sends(g, 3):
                copy.start()

        @pl.when(t == 2)
        def _():
            both_halves(g, 0, 2)
            both_halves(g, 2, 0)
            for copy in b_sends(g, 2):
                copy.start()

        for first, da in ((3, 1), (5, 3), (9, 2)):

            @pl.when(t == first)
            def _(da=da):
                for db in (1, 3):
                    full(g, da, db)
                for copy in b_forwards(g, da):
                    copy.start()

        for last, da in ((7, 1), (8, 3), (11, 2)):

            @pl.when(t == last)
            def _(da=da):
                both_halves(g, da, 2)

    def score(t, g):
        da, db = offset(t, 0), offset(t, 1)
        owner = peer(g, da, db)
        s = lax.dot_general(
            qbuf[g, da * 4 + db],
            kbuf[g],
            (((1,), (1,)), ((), ())),
            preferred_element_type=F32,
        )
        row = jnp.broadcast_to(row_pos[pl.ds(owner, 1), :], (128, 128)).T[:SEL, :1]
        pos = jnp.concatenate([row] * GROUP, 0)
        s = jnp.where(key_pos[...] <= pos, s, NEG)
        scores[g] = s
        tops[g] = functools.reduce(
            jnp.maximum, [s[:, n * 128 : (n + 1) * 128] for n in range(KEYS // 128)]
        )

    def weigh(t, g):
        top = jnp.broadcast_to(jnp.max(tops[g], -1, keepdims=True), (ROWS, 128))
        e = jnp.exp2((scores[g] - top[:, :1]) * LOG_SCALE).astype(BF16)
        table = jnp.concatenate([vbuf[g], jnp.ones((KEYS, 128), BF16)], 1)
        summed = jnp.dot(e, table, preferred_element_type=F32)
        total = summed[:, 128:]
        part[g, t] = (summed[:, :128] / total).astype(BF16)
        stat[g, t] = pack_rows(top * LOG_SCALE + jnp.log2(total))

    def b_result(g, t, da, db):
        to = at(peer(g, 0, db))
        return [
            pltpu.make_async_remote_copy(
                src_ref=src.at[g, t],
                dst_ref=dst.at[g, da, db - 1],
                send_sem=ssem.at[g, da, db - 1],
                recv_sem=rsem.at[g, da, db - 1],
                device_id=to,
                device_id_type=MESH,
            )
            for src, dst, ssem, rsem in (
                (part, rb_part, bp_ssem, bp_rsem),
                (stat, rb_stat, bs_ssem, bs_rsem),
            )
        ]

    def a_result(g, da):
        to = at(peer(g, da, 0))
        return [
            pltpu.make_async_remote_copy(
                src_ref=src.at[g, da - 1],
                dst_ref=dst.at[g, da - 1],
                send_sem=ssem.at[g, da - 1],
                recv_sem=rsem.at[g, da - 1],
                device_id=to,
                device_id_type=MESH,
            )
            for src, dst, ssem, rsem in (
                (mid, ra_part, ap_ssem, ap_rsem),
                (mid_stat, ra_stat, as_ssem, as_rsem),
            )
        ]

    def line(g, da):
        for db in range(1, SIDE):
            for copy in b_result(g, 0, da, db):
                copy.wait_recv()
        t = OWN[da]
        return (
            [part[g, t]] + [rb_part[g, da, n] for n in range(3)],
            [stat[g, t]] + [rb_stat[g, da, n] for n in range(3)],
        )

    def finish_line(da):
        for g in range(2):
            merged, logs = merge(*line(g, da))
            mid[g, da - 1] = merged.astype(BF16)
            mid_stat[g, da - 1] = logs
            for copy in a_result(g, da):
                copy.start()

    def pass_on(t, g):
        @pl.when(t < 12)
        def _():
            for copy in b_result(g, t, offset(t, 0), offset(t, 1)):
                copy.start()

    for copy in stored_copies + fresh_copies:
        copy.wait_recv()
    put_in(1)
    arrive(jnp.int32(0), 0)
    score(0, 0)

    def step(t, carry):
        arrive(t, 1)
        for da in (1, 2):

            @pl.when(t == OWN[da] + 1)
            def _(da=da):
                finish_line(da)

        score(t, 1)
        weigh(t, 0)
        pass_on(t, 0)
        arrive(t + 1, 0)
        score(t + 1, 0)
        weigh(t, 1)
        pass_on(t, 1)
        return carry

    lax.fori_loop(0, 15, step, 0)
    finish_line(3)
    score(15, 1)
    weigh(15, 0)
    weigh(15, 1)
    for g in range(2):
        parts, stats = line(g, 0)
        for da in (1, 2, 3):
            for copy in a_result(g, da):
                copy.wait_recv()
        merged, _ = merge(
            parts + [ra_part[g, n] for n in range(3)], stats + [ra_stat[g, n] for n in range(3)]
        )
        for h in range(GROUP):
            ctx[:, pl.ds((g * GROUP + h) * 128, 128)] = merged[h * SEL : (h + 1) * SEL].astype(BF16)

    for copy in weights:
        copy.wait()

    lower = pl.ds(0, SEL // 2)
    upper = pl.ds(SEL // 2, SEL // 2)

    def z_copy(index, src, dst, dz):
        return pltpu.make_async_remote_copy(
            src_ref=src,
            dst_ref=dst,
            send_sem=z_ssem.at[index],
            recv_sem=z_rsem.at[index],
            device_id=above(dz),
            device_id_type=MESH,
        )

    def projected(dz):
        return jnp.dot(ctx[...], wbuf[lax.rem(head + dz, SIDE)], preferred_element_type=F32)

    up_far = z_copy(0, zsend.at[0, lower], zrelay.at[0], 1)
    down_far = z_copy(1, zsend.at[0, upper], zrelay.at[1], 3)
    up_free = z_copy(2, zsend.at[1, upper], zrecv.at[0, upper], 1)
    up_sum = z_copy(3, zsend.at[1, lower], zrecv.at[0, lower], 1)
    down_free = z_copy(4, zsend.at[2, lower], zrecv.at[1, lower], 3)
    down_sum = z_copy(5, zsend.at[2, upper], zrecv.at[1, upper], 3)
    zsend[0] = projected(2).astype(BF16)
    up_far.start()
    down_far.start()
    up = projected(1)
    zsend[1, upper] = up[SEL // 2 :].astype(BF16)
    up_free.start()
    up_far.wait_recv()
    zsend[1, lower] = (up[: SEL // 2] + zrelay[0].astype(F32)).astype(BF16)
    up_sum.start()
    down = projected(3)
    zsend[2, lower] = down[: SEL // 2].astype(BF16)
    down_free.start()
    down_far.wait_recv()
    zsend[2, upper] = (down[SEL // 2 :] + zrelay[1].astype(F32)).astype(BF16)
    down_sum.start()
    total = projected(0)
    for copy in (up_free, up_sum, down_free, down_sum):
        copy.wait_recv()
    out_ref[...] = (total + zrecv[0].astype(F32) + zrecv[1].astype(F32)).astype(BF16)

    for copy in fresh_copies:
        copy.wait_send()
    for g in range(2):
        for copy in a_sends(g) + [a_forward(g, 3), a_forward(g, 1)]:
            copy.wait_send()
        for da in range(4):
            for copy in b_sends(g, da) + b_forwards(g, da):
                copy.wait_send()
            for db in range(1, 4):
                for copy in b_result(g, 0, da, db):
                    copy.wait_send()
        for da in range(1, 4):
            for copy in a_result(g, da):
                copy.wait_send()
    for copy in (up_far, down_far, up_free, up_sum, down_free, down_sum):
        copy.wait_send()


def attend(*operands):
    vmem = pl.BlockSpec(memory_space=pltpu.VMEM)
    hbm = pl.BlockSpec(memory_space=pl.ANY)
    dma = pltpu.SemaphoreType.DMA
    return pl.pallas_call(
        kernel,
        out_shape=(
            pltpu.VMEM((SEL, 1024), BF16),
            pltpu.VMEM((4 * SEL, 128), BF16),
        ),
        in_specs=[hbm] * 11,
        out_specs=(vmem, vmem),
        scratch_shapes=[
            pltpu.SMEM((PASSAGES,), jnp.int32),
            pltpu.SMEM((PASSAGES,), jnp.int32),
            pltpu.VMEM((1, D), F32),
            pltpu.VMEM((1, 128), F32),
            pltpu.VMEM((24, 128), jnp.int32),
            pltpu.VMEM((32, 128), F32),
            pltpu.VMEM((SEL, D), BF16),
            pltpu.VMEM((SEL, D), BF16),
            pltpu.VMEM((2, 2, D // 2, 512), BF16),
            pltpu.VMEM((2, D, 256), BF16),
            pltpu.VMEM((4 * BLOCK, 128), BF16),
            pltpu.VMEM((4 * BLOCK, 128), F32),
            pltpu.VMEM((4 * SEL, 128), F32),
            pltpu.VMEM((2, 2, FRESH, 256), BF16),
            pltpu.VMEM((1, KEYS), F32),
            pltpu.VMEM((2, 16, ROWS, 128), BF16),
            pltpu.VMEM((2, KEYS, 128), BF16),
            pltpu.VMEM((2, KEYS, 128), BF16),
            pltpu.VMEM((SIDE, 1024, 1024), BF16),
            pltpu.VMEM((2, ROWS, KEYS), F32),
            pltpu.VMEM((2, ROWS, 128), F32),
            pltpu.VMEM((2, 16, ROWS, 128), BF16),
            pltpu.VMEM((2, 16, 8, 128), F32),
            pltpu.VMEM((2, 4, 3, ROWS, 128), BF16),
            pltpu.VMEM((2, 4, 3, 8, 128), F32),
            pltpu.VMEM((2, 3, ROWS, 128), BF16),
            pltpu.VMEM((2, 3, 8, 128), F32),
            pltpu.VMEM((2, 3, ROWS, 128), BF16),
            pltpu.VMEM((2, 3, 8, 128), F32),
            pltpu.VMEM((SEL, 1024), BF16),
            pltpu.VMEM((3, SEL, 1024), BF16),
            pltpu.VMEM((2, SEL // 2, 1024), BF16),
            pltpu.VMEM((2, SEL, 1024), BF16),
            dma((17,)),
            dma((4,)),
            dma((4,)),
            dma((2, 20)),
            dma((2, 16, 2)),
            dma((2, 4, 3)),
            dma((2, 4, 3)),
            dma((2, 4, 3)),
            dma((2, 4, 3)),
            dma((2, 3)),
            dma((2, 3)),
            dma((2, 3)),
            dma((2, 3)),
            dma((6,)),
            dma((6,)),
        ],
        compiler_params=pltpu.CompilerParams(
            collective_id=0, has_side_effects=True, vmem_limit_bytes=64_000_000
        ),
    )(*operands)


def body(
    hidden, norm_gain, w_query, w_key, w_value, w_out, stored_kv, selected, prompt_order, store_slot
):
    half = HEAD_DIM // 2
    index = jnp.arange(HEAD_DIM, dtype=jnp.int32) % half
    freq = 500000.0 ** (-(index.astype(F32) * 2.0 / HEAD_DIM))
    attn_out, new_kv = attend(
        prompt_order,
        store_slot,
        hidden,
        norm_gain[None],
        freq[None],
        selected.reshape(24, 128),
        stored_kv.reshape(-1, HEAD_DIM),
        w_query,
        w_key,
        w_value,
        w_out,
    )
    return (attn_out, new_kv.reshape(SEL, 2, 2, HEAD_DIM))


def solution(mesh):
    in_specs = (
        P("seq", None),
        P(),
        P(None, "head"),
        P(None, "head"),
        P(None, "head"),
        P("head", None),
        P("seq", None, "head", None),
        P(),
        P(),
        P(),
    )
    out_specs = (P("seq", "head"), P("seq", None, "head", None))
    return jax.shard_map(body, mesh=mesh, in_specs=in_specs, out_specs=out_specs, check_vma=False)
```

```python
import functools

import jax
import jax.numpy as jnp
from jax import lax
from jax.experimental import pallas as pl
from jax.experimental.pallas import tpu as pltpu
from jax.sharding import PartitionSpec as P

D = 4096
HEADS = 32
KV_HEADS = 8
HEAD_DIM = 128
PASSAGE = 4096
PASSAGES = 8
SIDE = 4
GROUP = HEADS // KV_HEADS
BLOCK = 1024
SEL = 96
FRESH = 128
KEYS = 2 * BLOCK
ROWS = GROUP * SEL
NEG = -1.0e30
LOG_SCALE = 1.4426950408889634 / HEAD_DIM**0.5
F32 = jnp.float32
BF16 = jnp.bfloat16
MESH = pl.DeviceIdType.MESH


WALK = (
    (0, 1), (0, 3), (0, 2), (1, 1), (1, 3), (3, 1), (3, 3), (2, 1),
    (2, 3), (1, 2), (2, 2), (3, 2), (2, 0), (1, 0), (3, 0), (0, 0),
)
OWN = {da: t for t, (da, db) in enumerate(WALK) if db == 0}


def offset(t, axis):
    if isinstance(t, int):
        return WALK[t][axis]
    found = jnp.int32(0)
    for n, pair in enumerate(WALK):
        found = jnp.where(t == n, pair[axis], found)
    return found


def pack_rows(column):
    lane = lax.broadcasted_iota(jnp.int32, (SEL, 128), 1)
    total = jnp.zeros((SEL, 128), F32)
    for h in range(GROUP):
        total = jnp.where(lane == h, column[h * SEL : (h + 1) * SEL], total)
    square = jnp.concatenate([total, jnp.zeros((128 - SEL, 128), F32)], 0)
    return square.T[:8]


def unpack_rows(packed):
    square = jnp.concatenate([packed, jnp.zeros((120, 128), F32)], 0).T
    return jnp.concatenate(
        [jnp.broadcast_to(square[:SEL, h : h + 1], (SEL, 128)) for h in range(GROUP)], 0
    )


def merge(parts, stats):
    top = functools.reduce(jnp.maximum, stats)
    factors = [jnp.exp2(s - top) for s in stats]
    total = functools.reduce(jnp.add, factors)
    merged = sum(
        part.astype(F32) * unpack_rows(factor / total) for part, factor in zip(parts, factors)
    )
    return merged, top + jnp.log2(total)


def kernel(
    order_in,
    slot_in,
    hidden_in,
    gain_in,
    freq_in,
    selected_in,
    stored_in,
    w_query_in,
    w_key_in,
    w_value_in,
    w_out_in,
    out_ref,
    new_ref,
    prompt_order,
    store_slot,
    gain,
    freq,
    listed,
    row_pos,
    hid,
    normed,
    wq,
    wkv,
    stored,
    wide,
    fresh,
    made_kv,
    key_pos,
    qbuf,
    kbuf,
    vbuf,
    wbuf,
    scores,
    tops,
    part,
    stat,
    rb_part,
    rb_stat,
    mid,
    mid_stat,
    ra_part,
    ra_stat,
    ctx,
    zsend,
    zrelay,
    zrecv,
    local_sem,
    kv_ssem,
    kv_rsem,
    g_ssem,
    g_rsem,
    bp_ssem,
    bp_rsem,
    bs_ssem,
    bs_rsem,
    ap_ssem,
    ap_rsem,
    as_ssem,
    as_rsem,
    z_ssem,
    z_rsem,
):
    seq = lax.axis_index("seq")
    head = lax.axis_index("head")
    core = lax.rem(seq, 2)
    chip_x = lax.rem(seq // 2, SIDE)
    chip_y = seq // (2 * SIDE)

    def chip_seq(dx, dy):
        return (lax.rem(chip_y + dy, SIDE) * SIDE + lax.rem(chip_x + dx, SIDE)) * 2 + core

    def peer(g, da, db):
        return chip_seq(da, db) if g == 0 else chip_seq(db, da)

    def at(index):
        return (index, head)

    def above(dz):
        return (seq, lax.rem(head + dz, SIDE))

    other_seq = seq + 1 - 2 * core
    partner = (other_seq, head)

    barrier = pltpu.get_barrier_semaphore()
    others = [partner]
    for d in range(1, SIDE):
        others.append(at(chip_seq(d, 0)))
        others.append(at(chip_seq(0, d)))
    others += [above(1), above(3)]
    for other in others:
        pl.semaphore_signal(barrier, inc=1, device_id=other, device_id_type=MESH)

    load = pltpu.make_async_copy
    half_depth = D // 2
    own_hidden = load(hidden_in, hid, local_sem.at[0])
    own_stored = load(stored_in, stored, local_sem.at[1])
    q_loads = [
        [
            load(
                w_query_in.at[pl.ds(n * half_depth, half_depth), pl.ds(g * 512, 512)],
                wq.at[g, n],
                local_sem.at[2 + 2 * g + n],
            )
            for n in range(2)
        ]
        for g in range(2)
    ]
    kv_loads = [
        load(src, wkv.at[n], local_sem.at[6 + n]) for n, src in enumerate((w_key_in, w_value_in))
    ]
    weights = [
        load(w_out_in.at[:, pl.ds(n * 1024, 1024)], wbuf.at[n], local_sem.at[8 + n])
        for n in range(SIDE)
    ]
    small = [
        load(src, dst, local_sem.at[12 + n])
        for n, (src, dst) in enumerate(
            (
                (selected_in, listed),
                (freq_in, freq),
                (gain_in, gain),
                (order_in, prompt_order),
                (slot_in, store_slot),
            )
        )
    ]
    for copy in small:
        copy.start()
    own_hidden.start()
    for copy in q_loads[0]:
        copy.start()

    for copy in small:
        copy.wait()

    wide[pl.ds(0, 24), :] = listed[...].astype(F32)
    thirds = [wide[pl.ds(n, 8, stride=3), :] for n in range(3)]
    lane = lax.broadcasted_iota(jnp.int32, (8, 128), 1)
    roll = pltpu.roll
    for n, rows in enumerate(
        (
            thirds[0],
            jnp.where(lane < 32, roll(thirds[0], 32, 1), roll(thirds[1], 32, 1)),
            jnp.where(lane < 64, roll(thirds[1], 64, 1), roll(thirds[2], 64, 1)),
            roll(thirds[2], 96, 1),
        )
    ):
        row_pos[pl.ds(n, 8, stride=4), :] = rows

    angle = jnp.broadcast_to(row_pos[pl.ds(seq, 1), :], (128, 128)).T[:SEL] * freq[...]
    cos = jnp.cos(angle)
    sin = jnp.sin(angle)
    sin = jnp.where(lax.broadcasted_iota(jnp.int32, (SEL, 128), 1) < HEAD_DIM // 2, -sin, sin)

    order = [store_slot[prompt_order[i]] for i in range(PASSAGES)]
    lanes = lax.broadcasted_iota(jnp.int32, (1, BLOCK), 1)
    per_passage = PASSAGE // BLOCK
    blocks = []
    for n, device in enumerate((seq, other_seq)):
        place = jnp.int32(0)
        for i in range(PASSAGES):
            place = jnp.where(order[i] == device // per_passage, i, place)
        block = place * per_passage + lax.rem(device, per_passage)
        blocks.append(block)
        there = (block * BLOCK + lanes).astype(F32)
        replaced = jnp.broadcast_to(row_pos[pl.ds(block, 1), :], (128, 128)).T[:SEL, :1]
        made = jnp.broadcast_to(row_pos[pl.ds(device, 1), :], (128, 128)).T[:SEL, :1]
        put = jnp.sum(jnp.where(replaced == there, made + 1.0, 0.0), 0, keepdims=True)
        key_pos[:, pl.ds(n * BLOCK, BLOCK)] = jnp.where(put > 0.0, put - 1.0, there)

    own_hidden.wait()
    own_stored.start()
    q_loads[1][0].start()
    widened = hid[...].astype(F32)
    mean = jnp.mean(widened * widened, -1, keepdims=True)
    normed[...] = (widened * lax.rsqrt(mean + 1e-05) * gain[...]).astype(BF16)

    def to_partner(index, src, dst):
        return pltpu.make_async_remote_copy(
            src_ref=src,
            dst_ref=dst,
            send_sem=kv_ssem.at[index],
            recv_sem=kv_rsem.at[index],
            device_id=partner,
            device_id_type=MESH,
        )

    stored_copies = [
        to_partner(n, buf.at[:, pl.ds(0, BLOCK)], buf.at[:, pl.ds(BLOCK, BLOCK)])
        for n, buf in enumerate((kbuf, vbuf))
    ]
    fresh_copies = [to_partner(2 + n, made_kv.at[0, n], made_kv.at[1, n]) for n in range(2)]

    def whole(g, src, dst, sem, to):
        return pltpu.make_async_remote_copy(
            src_ref=qbuf.at[g, src],
            dst_ref=qbuf.at[g, dst],
            send_sem=g_ssem.at[g, sem],
            recv_sem=g_rsem.at[g, dst, 0],
            device_id=at(to),
            device_id_type=MESH,
        )

    def halved(g, src, dst, half, sem, to):
        rows = pl.ds(half * (ROWS // 2), ROWS // 2)
        return pltpu.make_async_remote_copy(
            src_ref=qbuf.at[g, src, rows],
            dst_ref=qbuf.at[g, dst, rows],
            send_sem=g_ssem.at[g, sem],
            recv_sem=g_rsem.at[g, dst, half],
            device_id=at(to),
            device_id_type=MESH,
        )

    def a_sends(g):
        return [whole(g, 0, 12, 0, peer(g, 1, 0)), whole(g, 0, 4, 1, peer(g, 3, 0))]

    def a_forward(g, da):
        if da == 3:
            return halved(g, 12, 8, 0, 2, peer(g, 1, 0))
        return halved(g, 4, 8, 1, 3, peer(g, 3, 0))

    def b_sends(g, da):
        return [
            whole(g, da * 4, da * 4 + 3, 4 + 4 * da, peer(g, 0, 1)),
            whole(g, da * 4, da * 4 + 1, 5 + 4 * da, peer(g, 0, 3)),
        ]

    def b_forwards(g, da):
        return [
            halved(g, da * 4 + 3, da * 4 + 2, 0, 6 + 4 * da, peer(g, 0, 1)),
            halved(g, da * 4 + 1, da * 4 + 2, 1, 7 + 4 * da, peer(g, 0, 3)),
        ]

    def turned(x):
        return x * cos + pltpu.roll(x, HEAD_DIM // 2, 1) * sin

    pl.semaphore_wait(barrier, len(others))
    later = {(0, 0): q_loads[1][1], (0, 1): kv_loads[0], (1, 0): kv_loads[1]}
    for g in range(2):
        total = None
        for n in range(2):
            q_loads[g][n].wait()
            if (g, n) in later:
                later[g, n].start()
            term = jnp.dot(
                normed[:, pl.ds(n * half_depth, half_depth)],
                wq[g, n],
                preferred_element_type=F32,
            )
            total = term if total is None else total + term
        for h in range(GROUP):
            qbuf[g, 0, pl.ds(h * SEL, SEL), :] = turned(total[:, h * 128 : (h + 1) * 128]).astype(
                BF16
            )
        for copy in a_sends(g) + b_sends(g, 0):
            copy.start()
        if g == 0:
            own_stored.wait()
            wide[...] = stored[...].astype(F32)
            for n, buf in enumerate((kbuf, vbuf)):
                for k in range(2):
                    rows = wide[pl.ds(2 * n + k, BLOCK, stride=4), :]
                    buf[k, pl.ds(0, BLOCK), :] = rows.astype(BF16)
                stored_copies[n].start()

    for n in range(2):
        kv_loads[n].wait()
        made = jnp.dot(normed[...], wkv[n], preferred_element_type=F32)
        made_kv[0, n, pl.ds(SEL, FRESH - SEL), :] = jnp.zeros((FRESH - SEL, 256), BF16)
        for g in range(2):
            value = made[:, g * 128 : (g + 1) * 128]
            if n == 0:
                value = turned(value)
            made_kv[0, n, pl.ds(0, SEL), pl.ds(g * 128, 128)] = value.astype(BF16)
            fresh[pl.ds(2 * n + g, SEL, stride=4), :] = value
        fresh_copies[n].start()
    for copy in weights:
        copy.start()

    def put_in(n):
        replaced = row_pos[pl.ds(blocks[n], 1), :]
        source = jnp.concatenate(
            [made_kv[n, 0], made_kv[n, 1], jnp.ones((FRESH, 128), BF16)], 1
        )
        for first in range(0, BLOCK, 256):
            there = blocks[n] * BLOCK + first + lax.broadcasted_iota(jnp.int32, (256, 128), 0)
            usable = lax.broadcasted_iota(jnp.int32, (256, 128), 1) < SEL
            chosen = jnp.logical_and(there.astype(F32) == replaced, usable)
            rows = jnp.dot(
                jnp.where(chosen, 1.0, 0.0).astype(BF16), source, preferred_element_type=F32
            )
            gone = rows[:, 512:] > 0.5
            where = pl.ds(n * BLOCK + first, 256)
            for k, (buf, g) in enumerate(((kbuf, 0), (kbuf, 1), (vbuf, 0), (vbuf, 1))):
                old = buf[g, where, :].astype(F32)
                buf[g, where, :] = jnp.where(gone, rows[:, k * 128 : (k + 1) * 128], old).astype(
                    BF16
                )

    for copy in stored_copies:
        copy.wait_send()
    put_in(0)
    new_ref[...] = fresh[...].astype(BF16)

    def full(g, da, db):
        whole(g, 0, da * 4 + db, 0, peer(g, 1, 0)).wait_recv()

    def both_halves(g, da, db):
        for half in range(2):
            halved(g, 0, da * 4 + db, half, 0, peer(g, 1, 0)).wait_recv()

    def arrive(t, g):
        @pl.when(t < 3)
        def _():
            @pl.when(t == 0)
            def _():
                for db in (1, 3):
                    full(g, 0, db)
                for copy in b_forwards(g, 0):
                    copy.start()
                for da in (1, 3):
                    full(g, da, 0)
                    a_forward(g, da).start()

            @pl.when(t == 1)
            def _():
                for copy in b_sends(g, 1) + b_sends(g, 3):
                    copy.start()

            @pl.when(t == 2)
            def _():
                both_halves(g, 0, 2)
                both_halves(g, 2, 0)
                for copy in b_sends(g, 2):
                    copy.start()

        @pl.when(jnp.logical_or(jnp.logical_or(t == 3, t == 5), t == 7))
        def _():
            da = jnp.where(t == 3, 1, jnp.where(t == 5, 3, 2))
            for db in (1, 3):
                full(g, da, db)
            for copy in b_forwards(g, da):
                copy.start()

        @pl.when(jnp.logical_and(t >= 9, t < 12))
        def _():
            both_halves(g, t - 8, 2)

    def score(t, g):
        da, db = offset(t, 0), offset(t, 1)
        owner = peer(g, da, db)
        s = lax.dot_general(
            qbuf[g, da * 4 + db],
            kbuf[g],
            (((1,), (1,)), ((), ())),
            preferred_element_type=F32,
        )
        row = jnp.broadcast_to(row_pos[pl.ds(owner, 1), :], (128, 128)).T[:SEL, :1]
        pos = jnp.concatenate([row] * GROUP, 0)
        s = jnp.where(key_pos[...] <= pos, s, NEG)
        scores[g] = s
        tops[g] = functools.reduce(
            jnp.maximum, [s[:, n * 128 : (n + 1) * 128] for n in range(KEYS // 128)]
        )

    def weigh(t, g):
        top = jnp.broadcast_to(jnp.max(tops[g], -1, keepdims=True), (ROWS, 128))
        e = jnp.exp2((scores[g] - top[:, :1]) * LOG_SCALE).astype(BF16)
        table = jnp.concatenate([vbuf[g], jnp.ones((KEYS, 128), BF16)], 1)
        summed = jnp.dot(e, table, preferred_element_type=F32)
        total = summed[:, 128:]
        part[g, t] = (summed[:, :128] / total).astype(BF16)
        stat[g, t] = pack_rows(top * LOG_SCALE + jnp.log2(total))

    def b_result(g, t, da, db):
        to = at(peer(g, 0, db))
        return [
            pltpu.make_async_remote_copy(
                src_ref=src.at[g, t],
                dst_ref=dst.at[g, da, db - 1],
                send_sem=ssem.at[g, da, db - 1],
                recv_sem=rsem.at[g, da, db - 1],
                device_id=to,
                device_id_type=MESH,
            )
            for src, dst, ssem, rsem in (
                (part, rb_part, bp_ssem, bp_rsem),
                (stat, rb_stat, bs_ssem, bs_rsem),
            )
        ]

    def a_result(g, da):
        to = at(peer(g, da, 0))
        return [
            pltpu.make_async_remote_copy(
                src_ref=src.at[g, da - 1],
                dst_ref=dst.at[g, da - 1],
                send_sem=ssem.at[g, da - 1],
                recv_sem=rsem.at[g, da - 1],
                device_id=to,
                device_id_type=MESH,
            )
            for src, dst, ssem, rsem in (
                (mid, ra_part, ap_ssem, ap_rsem),
                (mid_stat, ra_stat, as_ssem, as_rsem),
            )
        ]

    def line(g, da):
        t = OWN[da]
        return (
            [part[g, t]] + [rb_part[g, da, n] for n in range(3)],
            [stat[g, t]] + [rb_stat[g, da, n] for n in range(3)],
        )

    def line_arrives(da):
        for g in range(2):
            for db in range(1, SIDE):
                for copy in b_result(g, 0, da, db):
                    copy.wait_recv()

    def merge_line(da):
        for g in range(2):
            merged, logs = merge(*line(g, da))
            mid[g, da - 1] = merged.astype(BF16)
            mid_stat[g, da - 1] = logs

    def send_line(da):
        for g in range(2):
            for copy in a_result(g, da):
                copy.start()

    def pass_on(t, g):
        for copy in b_result(g, t, offset(t, 0), offset(t, 1)):
            copy.start()

    for copy in stored_copies + fresh_copies:
        copy.wait_recv()
    put_in(1)
    arrive(jnp.int32(0), 0)
    score(0, 0)

    def step(t, carry):
        arrive(t, 1)
        score(t, 1)
        weigh(t, 0)
        pass_on(t, 0)
        arrive(t + 1, 0)
        score(t + 1, 0)
        weigh(t, 1)
        pass_on(t, 1)
        return carry

    lax.fori_loop(0, 12, step, 0)
    for t, da in ((12, None), (13, 2), (14, 1)):
        if da is not None:
            line_arrives(da)
        score(t, 1)
        weigh(t, 0)
        if da is not None:
            merge_line(da)
        score(t + 1, 0)
        weigh(t, 1)
        if da is not None:
            send_line(da)
    line_arrives(3)
    score(15, 1)
    weigh(15, 0)
    merge_line(3)
    send_line(3)
    weigh(15, 1)
    line_arrives(0)
    for g in range(2):
        parts, stats = line(g, 0)
        for da in (1, 2, 3):
            for copy in a_result(g, da):
                copy.wait_recv()
        merged, _ = merge(
            parts + [ra_part[g, n] for n in range(3)], stats + [ra_stat[g, n] for n in range(3)]
        )
        for h in range(GROUP):
            ctx[:, pl.ds((g * GROUP + h) * 128, 128)] = merged[h * SEL : (h + 1) * SEL].astype(BF16)

    for copy in weights:
        copy.wait()

    lower = pl.ds(0, SEL // 2)
    upper = pl.ds(SEL // 2, SEL // 2)

    def z_copy(index, src, dst, dz):
        return pltpu.make_async_remote_copy(
            src_ref=src,
            dst_ref=dst,
            send_sem=z_ssem.at[index],
            recv_sem=z_rsem.at[index],
            device_id=above(dz),
            device_id_type=MESH,
        )

    def projected(dz):
        return jnp.dot(ctx[...], wbuf[lax.rem(head + dz, SIDE)], preferred_element_type=F32)

    up_far = z_copy(0, zsend.at[0, lower], zrelay.at[0], 1)
    down_far = z_copy(1, zsend.at[0, upper], zrelay.at[1], 3)
    up_free = z_copy(2, zsend.at[1, upper], zrecv.at[0, upper], 1)
    up_sum = z_copy(3, zsend.at[1, lower], zrecv.at[0, lower], 1)
    down_free = z_copy(4, zsend.at[2, lower], zrecv.at[1, lower], 3)
    down_sum = z_copy(5, zsend.at[2, upper], zrecv.at[1, upper], 3)
    zsend[0] = projected(2).astype(BF16)
    up_far.start()
    down_far.start()
    up = projected(1)
    zsend[1, upper] = up[SEL // 2 :].astype(BF16)
    up_free.start()
    up_far.wait_recv()
    zsend[1, lower] = (up[: SEL // 2] + zrelay[0].astype(F32)).astype(BF16)
    up_sum.start()
    down = projected(3)
    zsend[2, lower] = down[: SEL // 2].astype(BF16)
    down_free.start()
    down_far.wait_recv()
    zsend[2, upper] = (down[SEL // 2 :] + zrelay[1].astype(F32)).astype(BF16)
    down_sum.start()
    total = projected(0)
    for copy in (up_free, up_sum, down_free, down_sum):
        copy.wait_recv()
    out_ref[...] = (total + zrecv[0].astype(F32) + zrecv[1].astype(F32)).astype(BF16)

    for copy in fresh_copies:
        copy.wait_send()
    for g in range(2):
        for copy in a_sends(g) + [a_forward(g, 3), a_forward(g, 1)]:
            copy.wait_send()
        for da in range(4):
            for copy in b_sends(g, da) + b_forwards(g, da):
                copy.wait_send()
            for db in range(1, 4):
                for copy in b_result(g, 0, da, db):
                    copy.wait_send()
        for da in range(1, 4):
            for copy in a_result(g, da):
                copy.wait_send()
    for copy in (up_far, down_far, up_free, up_sum, down_free, down_sum):
        copy.wait_send()


def attend(*operands):
    vmem = pl.BlockSpec(memory_space=pltpu.VMEM)
    hbm = pl.BlockSpec(memory_space=pl.ANY)
    dma = pltpu.SemaphoreType.DMA
    return pl.pallas_call(
        kernel,
        out_shape=(
            pltpu.VMEM((SEL, 1024), BF16),
            pltpu.VMEM((4 * SEL, 128), BF16),
        ),
        in_specs=[hbm] * 11,
        out_specs=(vmem, vmem),
        scratch_shapes=[
            pltpu.SMEM((PASSAGES,), jnp.int32),
            pltpu.SMEM((PASSAGES,), jnp.int32),
            pltpu.VMEM((1, D), F32),
            pltpu.VMEM((1, 128), F32),
            pltpu.VMEM((24, 128), jnp.int32),
            pltpu.VMEM((32, 128), F32),
            pltpu.VMEM((SEL, D), BF16),
            pltpu.VMEM((SEL, D), BF16),
            pltpu.VMEM((2, 2, D // 2, 512), BF16),
            pltpu.VMEM((2, D, 256), BF16),
            pltpu.VMEM((4 * BLOCK, 128), BF16),
            pltpu.VMEM((4 * BLOCK, 128), F32),
            pltpu.VMEM((4 * SEL, 128), F32),
            pltpu.VMEM((2, 2, FRESH, 256), BF16),
            pltpu.VMEM((1, KEYS), F32),
            pltpu.VMEM((2, 16, ROWS, 128), BF16),
            pltpu.VMEM((2, KEYS, 128), BF16),
            pltpu.VMEM((2, KEYS, 128), BF16),
            pltpu.VMEM((SIDE, 1024, 1024), BF16),
            pltpu.VMEM((2, ROWS, KEYS), F32),
            pltpu.VMEM((2, ROWS, 128), F32),
            pltpu.VMEM((2, 16, ROWS, 128), BF16),
            pltpu.VMEM((2, 16, 8, 128), F32),
            pltpu.VMEM((2, 4, 3, ROWS, 128), BF16),
            pltpu.VMEM((2, 4, 3, 8, 128), F32),
            pltpu.VMEM((2, 3, ROWS, 128), BF16),
            pltpu.VMEM((2, 3, 8, 128), F32),
            pltpu.VMEM((2, 3, ROWS, 128), BF16),
            pltpu.VMEM((2, 3, 8, 128), F32),
            pltpu.VMEM((SEL, 1024), BF16),
            pltpu.VMEM((3, SEL, 1024), BF16),
            pltpu.VMEM((2, SEL // 2, 1024), BF16),
            pltpu.VMEM((2, SEL, 1024), BF16),
            dma((17,)),
            dma((4,)),
            dma((4,)),
            dma((2, 20)),
            dma((2, 16, 2)),
            dma((2, 4, 3)),
            dma((2, 4, 3)),
            dma((2, 4, 3)),
            dma((2, 4, 3)),
            dma((2, 3)),
            dma((2, 3)),
            dma((2, 3)),
            dma((2, 3)),
            dma((6,)),
            dma((6,)),
        ],
        compiler_params=pltpu.CompilerParams(
            collective_id=0, has_side_effects=True, vmem_limit_bytes=64_000_000
        ),
    )(*operands)


def body(
    hidden, norm_gain, w_query, w_key, w_value, w_out, stored_kv, selected, prompt_order, store_slot
):
    half = HEAD_DIM // 2
    index = jnp.arange(HEAD_DIM, dtype=jnp.int32) % half
    freq = 500000.0 ** (-(index.astype(F32) * 2.0 / HEAD_DIM))
    attn_out, new_kv = attend(
        prompt_order,
        store_slot,
        hidden,
        norm_gain[None],
        freq[None],
        selected.reshape(24, 128),
        stored_kv.reshape(-1, HEAD_DIM),
        w_query,
        w_key,
        w_value,
        w_out,
    )
    return (attn_out, new_kv.reshape(SEL, 2, 2, HEAD_DIM))


def solution(mesh):
    in_specs = (
        P("seq", None),
        P(),
        P(None, "head"),
        P(None, "head"),
        P(None, "head"),
        P("head", None),
        P("seq", None, "head", None),
        P(),
        P(),
        P(),
    )
    out_specs = (P("seq", "head"), P("seq", None, "head", None))
    return jax.shard_map(body, mesh=mesh, in_specs=in_specs, out_specs=out_specs, check_vma=False)
```

```python
import functools

import jax
import jax.numpy as jnp
from jax import lax
from jax.experimental import pallas as pl
from jax.experimental.pallas import tpu as pltpu
from jax.sharding import PartitionSpec as P

D = 4096
HEADS = 32
KV_HEADS = 8
HEAD_DIM = 128
PASSAGE = 4096
PASSAGES = 8
SIDE = 4
GROUP = HEADS // KV_HEADS
BLOCK = 1024
SEL = 96
FRESH = 128
KEYS = 2 * BLOCK
ROWS = GROUP * SEL
NEG = -1.0e30
LOG_SCALE = 1.4426950408889634 / HEAD_DIM**0.5
F32 = jnp.float32
BF16 = jnp.bfloat16
MESH = pl.DeviceIdType.MESH


WALK = (
    (0, 0), (0, 1), (0, 3), (0, 2), (1, 1), (1, 3), (3, 1), (3, 3),
    (2, 1), (2, 3), (1, 2), (2, 2), (3, 2), (2, 0), (1, 0), (3, 0),
)
OWN = {da: t for t, (da, db) in enumerate(WALK) if db == 0}


def offset(t, axis):
    if isinstance(t, int):
        return WALK[t][axis]
    found = jnp.int32(0)
    for n, pair in enumerate(WALK):
        found = jnp.where(t == n, pair[axis], found)
    return found


def pack_rows(column):
    lane = lax.broadcasted_iota(jnp.int32, (SEL, 128), 1)
    total = jnp.zeros((SEL, 128), F32)
    for h in range(GROUP):
        total = jnp.where(lane == h, column[h * SEL : (h + 1) * SEL], total)
    square = jnp.concatenate([total, jnp.zeros((128 - SEL, 128), F32)], 0)
    return square.T[:8]


def unpack_rows(packed):
    square = jnp.concatenate([packed, jnp.zeros((120, 128), F32)], 0).T
    return jnp.concatenate(
        [jnp.broadcast_to(square[:SEL, h : h + 1], (SEL, 128)) for h in range(GROUP)], 0
    )


def merge(parts, stats):
    top = functools.reduce(jnp.maximum, stats)
    factors = [jnp.exp2(s - top) for s in stats]
    total = functools.reduce(jnp.add, factors)
    merged = sum(
        part.astype(F32) * unpack_rows(factor / total) for part, factor in zip(parts, factors)
    )
    return merged, top + jnp.log2(total)


def kernel(
    order_in,
    slot_in,
    hidden_in,
    gain_in,
    freq_in,
    selected_in,
    stored_in,
    w_query_in,
    w_key_in,
    w_value_in,
    w_out_in,
    out_ref,
    new_ref,
    prompt_order,
    store_slot,
    gain,
    freq,
    listed,
    row_pos,
    hid,
    normed,
    wq,
    wkv,
    stored,
    wide,
    fresh,
    made_kv,
    key_pos,
    qbuf,
    kbuf,
    vbuf,
    wbuf,
    scores,
    tops,
    part,
    stat,
    rb_part,
    rb_stat,
    mid,
    mid_stat,
    ra_part,
    ra_stat,
    ctx,
    zsend,
    zrelay,
    zrecv,
    local_sem,
    kv_ssem,
    kv_rsem,
    g_ssem,
    g_rsem,
    bp_ssem,
    bp_rsem,
    bs_ssem,
    bs_rsem,
    ap_ssem,
    ap_rsem,
    as_ssem,
    as_rsem,
    z_ssem,
    z_rsem,
):
    seq = lax.axis_index("seq")
    head = lax.axis_index("head")
    core = lax.rem(seq, 2)
    chip_x = lax.rem(seq // 2, SIDE)
    chip_y = seq // (2 * SIDE)

    def chip_seq(dx, dy):
        return (lax.rem(chip_y + dy, SIDE) * SIDE + lax.rem(chip_x + dx, SIDE)) * 2 + core

    def peer(g, da, db):
        return chip_seq(da, db) if g == 0 else chip_seq(db, da)

    def at(index):
        return (index, head)

    def above(dz):
        return (seq, lax.rem(head + dz, SIDE))

    other_seq = seq + 1 - 2 * core
    partner = (other_seq, head)

    barrier = pltpu.get_barrier_semaphore()
    others = [partner]
    for d in range(1, SIDE):
        others.append(at(chip_seq(d, 0)))
        others.append(at(chip_seq(0, d)))
    others += [above(1), above(3)]
    for other in others:
        pl.semaphore_signal(barrier, inc=1, device_id=other, device_id_type=MESH)

    load = pltpu.make_async_copy
    half_depth = D // 2
    own_hidden = load(hidden_in, hid, local_sem.at[0])
    own_stored = load(stored_in, stored, local_sem.at[1])
    q_loads = [
        [
            load(
                w_query_in.at[pl.ds(n * half_depth, half_depth), pl.ds(g * 512, 512)],
                wq.at[g, n],
                local_sem.at[2 + 2 * g + n],
            )
            for n in range(2)
        ]
        for g in range(2)
    ]
    kv_loads = [
        load(src, wkv.at[n], local_sem.at[6 + n]) for n, src in enumerate((w_key_in, w_value_in))
    ]
    weights = [
        load(w_out_in.at[:, pl.ds(n * 1024, 1024)], wbuf.at[n], local_sem.at[8 + n])
        for n in range(SIDE)
    ]
    small = [
        load(src, dst, local_sem.at[12 + n])
        for n, (src, dst) in enumerate(
            (
                (selected_in, listed),
                (freq_in, freq),
                (gain_in, gain),
                (order_in, prompt_order),
                (slot_in, store_slot),
            )
        )
    ]
    for copy in small:
        copy.start()
    own_hidden.start()
    for copy in q_loads[0]:
        copy.start()

    for copy in small:
        copy.wait()

    wide[pl.ds(0, 24), :] = listed[...].astype(F32)
    thirds = [wide[pl.ds(n, 8, stride=3), :] for n in range(3)]
    lane = lax.broadcasted_iota(jnp.int32, (8, 128), 1)
    roll = pltpu.roll
    for n, rows in enumerate(
        (
            thirds[0],
            jnp.where(lane < 32, roll(thirds[0], 32, 1), roll(thirds[1], 32, 1)),
            jnp.where(lane < 64, roll(thirds[1], 64, 1), roll(thirds[2], 64, 1)),
            roll(thirds[2], 96, 1),
        )
    ):
        row_pos[pl.ds(n, 8, stride=4), :] = rows

    angle = jnp.broadcast_to(row_pos[pl.ds(seq, 1), :], (128, 128)).T[:SEL] * freq[...]
    cos = jnp.cos(angle)
    sin = jnp.sin(angle)
    sin = jnp.where(lax.broadcasted_iota(jnp.int32, (SEL, 128), 1) < HEAD_DIM // 2, -sin, sin)

    order = [store_slot[prompt_order[i]] for i in range(PASSAGES)]
    lanes = lax.broadcasted_iota(jnp.int32, (1, BLOCK), 1)
    per_passage = PASSAGE // BLOCK
    blocks = []
    for n, device in enumerate((seq, other_seq)):
        place = jnp.int32(0)
        for i in range(PASSAGES):
            place = jnp.where(order[i] == device // per_passage, i, place)
        block = place * per_passage + lax.rem(device, per_passage)
        blocks.append(block)
        there = (block * BLOCK + lanes).astype(F32)
        replaced = jnp.broadcast_to(row_pos[pl.ds(block, 1), :], (128, 128)).T[:SEL, :1]
        made = jnp.broadcast_to(row_pos[pl.ds(device, 1), :], (128, 128)).T[:SEL, :1]
        put = jnp.sum(jnp.where(replaced == there, made + 1.0, 0.0), 0, keepdims=True)
        key_pos[:, pl.ds(n * BLOCK, BLOCK)] = jnp.where(put > 0.0, put - 1.0, there)

    own_hidden.wait()
    own_stored.start()
    q_loads[1][0].start()
    widened = hid[...].astype(F32)
    mean = jnp.mean(widened * widened, -1, keepdims=True)
    normed[...] = (widened * lax.rsqrt(mean + 1e-05) * gain[...]).astype(BF16)

    def to_partner(index, src, dst):
        return pltpu.make_async_remote_copy(
            src_ref=src,
            dst_ref=dst,
            send_sem=kv_ssem.at[index],
            recv_sem=kv_rsem.at[index],
            device_id=partner,
            device_id_type=MESH,
        )

    stored_copies = [
        to_partner(n, buf.at[:, pl.ds(0, BLOCK)], buf.at[:, pl.ds(BLOCK, BLOCK)])
        for n, buf in enumerate((kbuf, vbuf))
    ]
    fresh_copies = [to_partner(2 + n, made_kv.at[0, n], made_kv.at[1, n]) for n in range(2)]

    def whole(g, src, dst, sem, to):
        return pltpu.make_async_remote_copy(
            src_ref=qbuf.at[g, src],
            dst_ref=qbuf.at[g, dst],
            send_sem=g_ssem.at[g, sem],
            recv_sem=g_rsem.at[g, dst, 0],
            device_id=at(to),
            device_id_type=MESH,
        )

    def halved(g, src, dst, half, sem, to):
        rows = pl.ds(half * (ROWS // 2), ROWS // 2)
        return pltpu.make_async_remote_copy(
            src_ref=qbuf.at[g, src, rows],
            dst_ref=qbuf.at[g, dst, rows],
            send_sem=g_ssem.at[g, sem],
            recv_sem=g_rsem.at[g, dst, half],
            device_id=at(to),
            device_id_type=MESH,
        )

    def a_sends(g):
        return [whole(g, 0, 12, 0, peer(g, 1, 0)), whole(g, 0, 4, 1, peer(g, 3, 0))]

    def a_forward(g, da):
        if da == 3:
            return halved(g, 12, 8, 0, 2, peer(g, 1, 0))
        return halved(g, 4, 8, 1, 3, peer(g, 3, 0))

    def b_sends(g, da):
        return [
            whole(g, da * 4, da * 4 + 3, 4 + 4 * da, peer(g, 0, 1)),
            whole(g, da * 4, da * 4 + 1, 5 + 4 * da, peer(g, 0, 3)),
        ]

    def b_forwards(g, da):
        return [
            halved(g, da * 4 + 3, da * 4 + 2, 0, 6 + 4 * da, peer(g, 0, 1)),
            halved(g, da * 4 + 1, da * 4 + 2, 1, 7 + 4 * da, peer(g, 0, 3)),
        ]

    def turned(x):
        return x * cos + pltpu.roll(x, HEAD_DIM // 2, 1) * sin

    pl.semaphore_wait(barrier, len(others))
    later = {(0, 0): q_loads[1][1], (0, 1): kv_loads[0], (1, 0): kv_loads[1]}
    for g in range(2):
        total = None
        for n in range(2):
            q_loads[g][n].wait()
            if (g, n) in later:
                later[g, n].start()
            term = jnp.dot(
                normed[:, pl.ds(n * half_depth, half_depth)],
                wq[g, n],
                preferred_element_type=F32,
            )
            total = term if total is None else total + term
        for h in range(GROUP):
            qbuf[g, 0, pl.ds(h * SEL, SEL), :] = turned(total[:, h * 128 : (h + 1) * 128]).astype(
                BF16
            )
        for copy in a_sends(g) + b_sends(g, 0):
            copy.start()
        if g == 0:
            own_stored.wait()
            wide[...] = stored[...].astype(F32)
            for n, buf in enumerate((kbuf, vbuf)):
                for k in range(2):
                    rows = wide[pl.ds(2 * n + k, BLOCK, stride=4), :]
                    buf[k, pl.ds(0, BLOCK), :] = rows.astype(BF16)
                stored_copies[n].start()

    for n in range(2):
        kv_loads[n].wait()
        made = jnp.dot(normed[...], wkv[n], preferred_element_type=F32)
        made_kv[0, n, pl.ds(SEL, FRESH - SEL), :] = jnp.zeros((FRESH - SEL, 256), BF16)
        for g in range(2):
            value = made[:, g * 128 : (g + 1) * 128]
            if n == 0:
                value = turned(value)
            made_kv[0, n, pl.ds(0, SEL), pl.ds(g * 128, 128)] = value.astype(BF16)
            fresh[pl.ds(2 * n + g, SEL, stride=4), :] = value
        fresh_copies[n].start()
    for copy in weights:
        copy.start()

    def put_in(n):
        replaced = row_pos[pl.ds(blocks[n], 1), :]
        source = jnp.concatenate(
            [made_kv[n, 0], made_kv[n, 1], jnp.ones((FRESH, 128), BF16)], 1
        )
        for first in range(0, BLOCK, 256):
            there = blocks[n] * BLOCK + first + lax.broadcasted_iota(jnp.int32, (256, 128), 0)
            usable = lax.broadcasted_iota(jnp.int32, (256, 128), 1) < SEL
            chosen = jnp.logical_and(there.astype(F32) == replaced, usable)
            rows = jnp.dot(
                jnp.where(chosen, 1.0, 0.0).astype(BF16), source, preferred_element_type=F32
            )
            gone = rows[:, 512:] > 0.5
            where = pl.ds(n * BLOCK + first, 256)
            for k, (buf, g) in enumerate(((kbuf, 0), (kbuf, 1), (vbuf, 0), (vbuf, 1))):
                old = buf[g, where, :].astype(F32)
                buf[g, where, :] = jnp.where(gone, rows[:, k * 128 : (k + 1) * 128], old).astype(
                    BF16
                )

    for copy in stored_copies:
        copy.wait_send()
    put_in(0)
    new_ref[...] = fresh[...].astype(BF16)

    def full(g, da, db):
        whole(g, 0, da * 4 + db, 0, peer(g, 1, 0)).wait_recv()

    def both_halves(g, da, db):
        for half in range(2):
            halved(g, 0, da * 4 + db, half, 0, peer(g, 1, 0)).wait_recv()

    def arrive(t, g):
        @pl.when(t < 4)
        def _():
            @pl.when(t == 1)
            def _():
                for db in (1, 3):
                    full(g, 0, db)
                for copy in b_forwards(g, 0):
                    copy.start()
                for da in (1, 3):
                    full(g, da, 0)
                    a_forward(g, da).start()

            @pl.when(t == 2)
            def _():
                for copy in b_sends(g, 1) + b_sends(g, 3):
                    copy.start()

            @pl.when(t == 3)
            def _():
                both_halves(g, 0, 2)
                both_halves(g, 2, 0)
                for copy in b_sends(g, 2):
                    copy.start()

        @pl.when(jnp.logical_or(jnp.logical_or(t == 4, t == 6), t == 8))
        def _():
            da = jnp.where(t == 4, 1, jnp.where(t == 6, 3, 2))
            for db in (1, 3):
                full(g, da, db)
            for copy in b_forwards(g, da):
                copy.start()

        @pl.when(jnp.logical_and(t >= 10, t < 13))
        def _():
            both_halves(g, t - 9, 2)

    def score(t, g):
        da, db = offset(t, 0), offset(t, 1)
        owner = peer(g, da, db)
        s = lax.dot_general(
            qbuf[g, da * 4 + db],
            kbuf[g],
            (((1,), (1,)), ((), ())),
            preferred_element_type=F32,
        )
        row = jnp.broadcast_to(row_pos[pl.ds(owner, 1), :], (128, 128)).T[:SEL, :1]
        pos = jnp.concatenate([row] * GROUP, 0)
        s = jnp.where(key_pos[...] <= pos, s, NEG)
        scores[g] = s
        tops[g] = functools.reduce(
            jnp.maximum, [s[:, n * 128 : (n + 1) * 128] for n in range(KEYS // 128)]
        )

    def weigh(t, g):
        top = jnp.broadcast_to(jnp.max(tops[g], -1, keepdims=True), (ROWS, 128))
        e = jnp.exp2((scores[g] - top[:, :1]) * LOG_SCALE).astype(BF16)
        table = jnp.concatenate([vbuf[g], jnp.ones((KEYS, 128), BF16)], 1)
        summed = jnp.dot(e, table, preferred_element_type=F32)
        total = summed[:, 128:]
        part[g, t] = (summed[:, :128] / total).astype(BF16)
        stat[g, t] = pack_rows(top * LOG_SCALE + jnp.log2(total))

    def b_result(g, t, da, db):
        to = at(peer(g, 0, db))
        return [
            pltpu.make_async_remote_copy(
                src_ref=src.at[g, t],
                dst_ref=dst.at[g, da, db - 1],
                send_sem=ssem.at[g, da, db - 1],
                recv_sem=rsem.at[g, da, db - 1],
                device_id=to,
                device_id_type=MESH,
            )
            for src, dst, ssem, rsem in (
                (part, rb_part, bp_ssem, bp_rsem),
                (stat, rb_stat, bs_ssem, bs_rsem),
            )
        ]

    def a_result(g, da):
        to = at(peer(g, da, 0))
        return [
            pltpu.make_async_remote_copy(
                src_ref=src.at[g, da - 1],
                dst_ref=dst.at[g, da - 1],
                send_sem=ssem.at[g, da - 1],
                recv_sem=rsem.at[g, da - 1],
                device_id=to,
                device_id_type=MESH,
            )
            for src, dst, ssem, rsem in (
                (mid, ra_part, ap_ssem, ap_rsem),
                (mid_stat, ra_stat, as_ssem, as_rsem),
            )
        ]

    def line(g, da):
        t = OWN[da]
        return (
            [part[g, t]] + [rb_part[g, da, n] for n in range(3)],
            [stat[g, t]] + [rb_stat[g, da, n] for n in range(3)],
        )

    def line_arrives(da):
        for g in range(2):
            for db in range(1, SIDE):
                for copy in b_result(g, 0, da, db):
                    copy.wait_recv()

    def merge_line(da, halves=(0, 1)):
        for g in halves:
            merged, logs = merge(*line(g, da))
            mid[g, da - 1] = merged.astype(BF16)
            mid_stat[g, da - 1] = logs

    def send_line(da, halves=(0, 1)):
        for g in halves:
            for copy in a_result(g, da):
                copy.start()

    def pass_on(t, g):
        for copy in b_result(g, t, offset(t, 0), offset(t, 1)):
            copy.start()

    for copy in stored_copies + fresh_copies:
        copy.wait_recv()
    put_in(1)
    score(0, 0)
    score(0, 1)
    weigh(0, 0)
    arrive(jnp.int32(1), 0)
    score(1, 0)
    weigh(0, 1)

    def step(t, carry):
        arrive(t, 1)
        score(t, 1)
        weigh(t, 0)
        pass_on(t, 0)
        arrive(t + 1, 0)
        score(t + 1, 0)
        weigh(t, 1)
        pass_on(t, 1)
        return carry

    lax.fori_loop(1, 13, step, 0)
    line_arrives(0)
    score(13, 1)
    weigh(13, 0)
    for g in range(2):
        merged, logs = merge(*line(g, 0))
        part[g, 0] = merged.astype(BF16)
        stat[g, 0] = logs
    score(14, 0)
    weigh(13, 1)
    line_arrives(2)
    score(14, 1)
    weigh(14, 0)
    merge_line(2)
    send_line(2)
    line_arrives(1)
    score(15, 0)
    weigh(14, 1)
    merge_line(1, (0,))
    send_line(1, (0,))
    line_arrives(3)
    score(15, 1)
    weigh(15, 0)
    merge_line(1, (1,))
    send_line(1, (1,))
    weigh(15, 1)
    merge_line(3, (0,))
    send_line(3, (0,))
    merge_line(3, (1,))
    send_line(3, (1,))
    for g in range(2):
        for da in (2, 1, 3):
            for copy in a_result(g, da):
                copy.wait_recv()
        merged, _ = merge(
            [part[g, 0]] + [ra_part[g, n] for n in range(3)],
            [stat[g, 0]] + [ra_stat[g, n] for n in range(3)],
        )
        for h in range(GROUP):
            ctx[:, pl.ds((g * GROUP + h) * 128, 128)] = merged[h * SEL : (h + 1) * SEL].astype(BF16)

    for copy in weights:
        copy.wait()

    lower = pl.ds(0, SEL // 2)
    upper = pl.ds(SEL // 2, SEL // 2)

    def z_copy(index, src, dst, dz):
        return pltpu.make_async_remote_copy(
            src_ref=src,
            dst_ref=dst,
            send_sem=z_ssem.at[index],
            recv_sem=z_rsem.at[index],
            device_id=above(dz),
            device_id_type=MESH,
        )

    def projected(dz):
        return jnp.dot(ctx[...], wbuf[lax.rem(head + dz, SIDE)], preferred_element_type=F32)

    up_far = z_copy(0, zsend.at[0, lower], zrelay.at[0], 1)
    down_far = z_copy(1, zsend.at[0, upper], zrelay.at[1], 3)
    up_free = z_copy(2, zsend.at[1, upper], zrecv.at[0, upper], 1)
    up_sum = z_copy(3, zsend.at[1, lower], zrecv.at[0, lower], 1)
    down_free = z_copy(4, zsend.at[2, lower], zrecv.at[1, lower], 3)
    down_sum = z_copy(5, zsend.at[2, upper], zrecv.at[1, upper], 3)
    zsend[0] = projected(2).astype(BF16)
    up_far.start()
    down_far.start()
    up = projected(1)
    zsend[1, upper] = up[SEL // 2 :].astype(BF16)
    up_free.start()
    up_far.wait_recv()
    zsend[1, lower] = (up[: SEL // 2] + zrelay[0].astype(F32)).astype(BF16)
    up_sum.start()
    down = projected(3)
    zsend[2, lower] = down[: SEL // 2].astype(BF16)
    down_free.start()
    down_far.wait_recv()
    zsend[2, upper] = (down[SEL // 2 :] + zrelay[1].astype(F32)).astype(BF16)
    down_sum.start()
    total = projected(0)
    for copy in (up_free, up_sum, down_free, down_sum):
        copy.wait_recv()
    out_ref[...] = (total + zrecv[0].astype(F32) + zrecv[1].astype(F32)).astype(BF16)

    for copy in fresh_copies:
        copy.wait_send()
    for g in range(2):
        for copy in a_sends(g) + [a_forward(g, 3), a_forward(g, 1)]:
            copy.wait_send()
        for da in range(4):
            for copy in b_sends(g, da) + b_forwards(g, da):
                copy.wait_send()
            for db in range(1, 4):
                for copy in b_result(g, 0, da, db):
                    copy.wait_send()
        for da in range(1, 4):
            for copy in a_result(g, da):
                copy.wait_send()
    for copy in (up_far, down_far, up_free, up_sum, down_free, down_sum):
        copy.wait_send()


def attend(*operands):
    vmem = pl.BlockSpec(memory_space=pltpu.VMEM)
    hbm = pl.BlockSpec(memory_space=pl.ANY)
    dma = pltpu.SemaphoreType.DMA
    return pl.pallas_call(
        kernel,
        out_shape=(
            pltpu.VMEM((SEL, 1024), BF16),
            pltpu.VMEM((4 * SEL, 128), BF16),
        ),
        in_specs=[hbm] * 11,
        out_specs=(vmem, vmem),
        scratch_shapes=[
            pltpu.SMEM((PASSAGES,), jnp.int32),
            pltpu.SMEM((PASSAGES,), jnp.int32),
            pltpu.VMEM((1, D), F32),
            pltpu.VMEM((1, 128), F32),
            pltpu.VMEM((24, 128), jnp.int32),
            pltpu.VMEM((32, 128), F32),
            pltpu.VMEM((SEL, D), BF16),
            pltpu.VMEM((SEL, D), BF16),
            pltpu.VMEM((2, 2, D // 2, 512), BF16),
            pltpu.VMEM((2, D, 256), BF16),
            pltpu.VMEM((4 * BLOCK, 128), BF16),
            pltpu.VMEM((4 * BLOCK, 128), F32),
            pltpu.VMEM((4 * SEL, 128), F32),
            pltpu.VMEM((2, 2, FRESH, 256), BF16),
            pltpu.VMEM((1, KEYS), F32),
            pltpu.VMEM((2, 16, ROWS, 128), BF16),
            pltpu.VMEM((2, KEYS, 128), BF16),
            pltpu.VMEM((2, KEYS, 128), BF16),
            pltpu.VMEM((SIDE, 1024, 1024), BF16),
            pltpu.VMEM((2, ROWS, KEYS), F32),
            pltpu.VMEM((2, ROWS, 128), F32),
            pltpu.VMEM((2, 16, ROWS, 128), BF16),
            pltpu.VMEM((2, 16, 8, 128), F32),
            pltpu.VMEM((2, 4, 3, ROWS, 128), BF16),
            pltpu.VMEM((2, 4, 3, 8, 128), F32),
            pltpu.VMEM((2, 3, ROWS, 128), BF16),
            pltpu.VMEM((2, 3, 8, 128), F32),
            pltpu.VMEM((2, 3, ROWS, 128), BF16),
            pltpu.VMEM((2, 3, 8, 128), F32),
            pltpu.VMEM((SEL, 1024), BF16),
            pltpu.VMEM((3, SEL, 1024), BF16),
            pltpu.VMEM((2, SEL // 2, 1024), BF16),
            pltpu.VMEM((2, SEL, 1024), BF16),
            dma((17,)),
            dma((4,)),
            dma((4,)),
            dma((2, 20)),
            dma((2, 16, 2)),
            dma((2, 4, 3)),
            dma((2, 4, 3)),
            dma((2, 4, 3)),
            dma((2, 4, 3)),
            dma((2, 3)),
            dma((2, 3)),
            dma((2, 3)),
            dma((2, 3)),
            dma((6,)),
            dma((6,)),
        ],
        compiler_params=pltpu.CompilerParams(
            collective_id=0, has_side_effects=True, vmem_limit_bytes=64_000_000
        ),
    )(*operands)


def body(
    hidden, norm_gain, w_query, w_key, w_value, w_out, stored_kv, selected, prompt_order, store_slot
):
    half = HEAD_DIM // 2
    index = jnp.arange(HEAD_DIM, dtype=jnp.int32) % half
    freq = 500000.0 ** (-(index.astype(F32) * 2.0 / HEAD_DIM))
    attn_out, new_kv = attend(
        prompt_order,
        store_slot,
        hidden,
        norm_gain[None],
        freq[None],
        selected.reshape(24, 128),
        stored_kv.reshape(-1, HEAD_DIM),
        w_query,
        w_key,
        w_value,
        w_out,
    )
    return (attn_out, new_kv.reshape(SEL, 2, 2, HEAD_DIM))


def solution(mesh):
    in_specs = (
        P("seq", None),
        P(),
        P(None, "head"),
        P(None, "head"),
        P(None, "head"),
        P("head", None),
        P("seq", None, "head", None),
        P(),
        P(),
        P(),
    )
    out_specs = (P("seq", "head"), P("seq", None, "head", None))
    return jax.shard_map(body, mesh=mesh, in_specs=in_specs, out_specs=out_specs, check_vma=False)
```

```python
import functools

import jax
import jax.numpy as jnp
from jax import lax
from jax.experimental import pallas as pl
from jax.experimental.pallas import tpu as pltpu
from jax.sharding import PartitionSpec as P

D = 4096
HEADS = 32
KV_HEADS = 8
HEAD_DIM = 128
PASSAGE = 4096
PASSAGES = 8
SIDE = 4
GROUP = HEADS // KV_HEADS
BLOCK = 1024
SEL = 96
FRESH = 128
KEYS = 2 * BLOCK
ROWS = GROUP * SEL
NEG = -1.0e30
LOG_SCALE = 1.4426950408889634 / HEAD_DIM**0.5
F32 = jnp.float32
BF16 = jnp.bfloat16
MESH = pl.DeviceIdType.MESH


WALK = (
    (0, 0), (0, 1), (0, 3), (0, 2), (1, 1), (1, 3), (3, 1), (3, 3),
    (2, 1), (2, 3), (1, 2), (2, 2), (3, 2), (2, 0), (1, 0), (3, 0),
)
OWN = {da: t for t, (da, db) in enumerate(WALK) if db == 0}


def offset(t, axis):
    if isinstance(t, int):
        return WALK[t][axis]
    found = jnp.int32(0)
    for n, pair in enumerate(WALK):
        found = jnp.where(t == n, pair[axis], found)
    return found


def pack_rows(column):
    lane = lax.broadcasted_iota(jnp.int32, (SEL, 128), 1)
    total = jnp.zeros((SEL, 128), F32)
    for h in range(GROUP):
        total = jnp.where(lane == h, column[h * SEL : (h + 1) * SEL], total)
    square = jnp.concatenate([total, jnp.zeros((128 - SEL, 128), F32)], 0)
    return square.T[:8]


def unpack_rows(packed):
    square = jnp.concatenate([packed, jnp.zeros((120, 128), F32)], 0).T
    return jnp.concatenate(
        [jnp.broadcast_to(square[:SEL, h : h + 1], (SEL, 128)) for h in range(GROUP)], 0
    )


def merge(parts, stats):
    top = functools.reduce(jnp.maximum, stats)
    factors = [jnp.exp2(s - top) for s in stats]
    total = functools.reduce(jnp.add, factors)
    merged = sum(
        part.astype(F32) * unpack_rows(factor / total) for part, factor in zip(parts, factors)
    )
    return merged, top + jnp.log2(total)


def kernel(
    order_in,
    slot_in,
    hidden_in,
    gain_in,
    freq_in,
    selected_in,
    stored_in,
    w_query_in,
    w_key_in,
    w_value_in,
    w_out_in,
    out_ref,
    new_ref,
    prompt_order,
    store_slot,
    gain,
    freq,
    listed,
    row_pos,
    hid,
    normed,
    wq,
    wkv,
    stored,
    wide,
    fresh,
    made_kv,
    key_pos,
    qbuf,
    kbuf,
    vbuf,
    wbuf,
    scores,
    tops,
    part,
    stat,
    rb_part,
    rb_stat,
    mid,
    mid_stat,
    ra_part,
    ra_stat,
    ctx,
    zsend,
    zrelay,
    zrecv,
    local_sem,
    kv_ssem,
    kv_rsem,
    g_ssem,
    g_rsem,
    bp_ssem,
    bp_rsem,
    bs_ssem,
    bs_rsem,
    ap_ssem,
    ap_rsem,
    as_ssem,
    as_rsem,
    z_ssem,
    z_rsem,
):
    seq = lax.axis_index("seq")
    head = lax.axis_index("head")
    core = lax.rem(seq, 2)
    chip_x = lax.rem(seq // 2, SIDE)
    chip_y = seq // (2 * SIDE)

    def chip_seq(dx, dy):
        return (lax.rem(chip_y + dy, SIDE) * SIDE + lax.rem(chip_x + dx, SIDE)) * 2 + core

    def peer(g, da, db):
        return chip_seq(da, db) if g == 0 else chip_seq(db, da)

    def at(index):
        return (index, head)

    def above(dz):
        return (seq, lax.rem(head + dz, SIDE))

    other_seq = seq + 1 - 2 * core
    partner = (other_seq, head)

    barrier = pltpu.get_barrier_semaphore()
    others = [partner]
    for d in range(1, SIDE):
        others.append(at(chip_seq(d, 0)))
        others.append(at(chip_seq(0, d)))
    others += [above(1), above(3)]
    for other in others:
        pl.semaphore_signal(barrier, inc=1, device_id=other, device_id_type=MESH)

    load = pltpu.make_async_copy
    half_depth = D // 2
    own_hidden = load(hidden_in, hid, local_sem.at[0])
    own_stored = load(stored_in, stored, local_sem.at[1])
    q_loads = [
        [
            load(
                w_query_in.at[pl.ds(n * half_depth, half_depth), pl.ds(g * 512, 512)],
                wq.at[g, n],
                local_sem.at[2 + 2 * g + n],
            )
            for n in range(2)
        ]
        for g in range(2)
    ]
    kv_loads = [
        load(src, wkv.at[n], local_sem.at[6 + n]) for n, src in enumerate((w_key_in, w_value_in))
    ]
    weights = [
        load(w_out_in.at[:, pl.ds(n * 1024, 1024)], wbuf.at[n], local_sem.at[8 + n])
        for n in range(SIDE)
    ]
    small = [
        load(src, dst, local_sem.at[12 + n])
        for n, (src, dst) in enumerate(
            (
                (selected_in, listed),
                (freq_in, freq),
                (gain_in, gain),
                (order_in, prompt_order),
                (slot_in, store_slot),
            )
        )
    ]
    for copy in small:
        copy.start()
    own_hidden.start()
    for copy in q_loads[0]:
        copy.start()

    for copy in small:
        copy.wait()

    wide[pl.ds(0, 24), :] = listed[...].astype(F32)
    thirds = [wide[pl.ds(n, 8, stride=3), :] for n in range(3)]
    lane = lax.broadcasted_iota(jnp.int32, (8, 128), 1)
    roll = pltpu.roll
    for n, rows in enumerate(
        (
            thirds[0],
            jnp.where(lane < 32, roll(thirds[0], 32, 1), roll(thirds[1], 32, 1)),
            jnp.where(lane < 64, roll(thirds[1], 64, 1), roll(thirds[2], 64, 1)),
            roll(thirds[2], 96, 1),
        )
    ):
        row_pos[pl.ds(n, 8, stride=4), :] = rows

    angle = jnp.broadcast_to(row_pos[pl.ds(seq, 1), :], (128, 128)).T[:SEL] * freq[...]
    cos = jnp.cos(angle)
    sin = jnp.sin(angle)
    sin = jnp.where(lax.broadcasted_iota(jnp.int32, (SEL, 128), 1) < HEAD_DIM // 2, -sin, sin)

    order = [store_slot[prompt_order[i]] for i in range(PASSAGES)]
    lanes = lax.broadcasted_iota(jnp.int32, (1, BLOCK), 1)
    per_passage = PASSAGE // BLOCK
    blocks = []
    for n, device in enumerate((seq, other_seq)):
        place = jnp.int32(0)
        for i in range(PASSAGES):
            place = jnp.where(order[i] == device // per_passage, i, place)
        block = place * per_passage + lax.rem(device, per_passage)
        blocks.append(block)
        there = (block * BLOCK + lanes).astype(F32)
        replaced = jnp.broadcast_to(row_pos[pl.ds(block, 1), :], (128, 128)).T[:SEL, :1]
        made = jnp.broadcast_to(row_pos[pl.ds(device, 1), :], (128, 128)).T[:SEL, :1]
        put = jnp.sum(jnp.where(replaced == there, made + 1.0, 0.0), 0, keepdims=True)
        key_pos[:, pl.ds(n * BLOCK, BLOCK)] = jnp.where(put > 0.0, put - 1.0, there)

    own_hidden.wait()
    own_stored.start()
    kv_loads[0].start()
    widened = hid[...].astype(F32)
    mean = jnp.mean(widened * widened, -1, keepdims=True)
    normed[...] = (widened * lax.rsqrt(mean + 1e-05) * gain[...]).astype(BF16)

    def to_partner(index, src, dst):
        return pltpu.make_async_remote_copy(
            src_ref=src,
            dst_ref=dst,
            send_sem=kv_ssem.at[index],
            recv_sem=kv_rsem.at[index],
            device_id=partner,
            device_id_type=MESH,
        )

    stored_copies = [
        to_partner(n, buf.at[:, pl.ds(0, BLOCK)], buf.at[:, pl.ds(BLOCK, BLOCK)])
        for n, buf in enumerate((kbuf, vbuf))
    ]
    fresh_copies = [to_partner(2 + n, made_kv.at[0, n], made_kv.at[1, n]) for n in range(2)]

    def whole(g, src, dst, sem, to):
        return pltpu.make_async_remote_copy(
            src_ref=qbuf.at[g, src],
            dst_ref=qbuf.at[g, dst],
            send_sem=g_ssem.at[g, sem],
            recv_sem=g_rsem.at[g, dst, 0],
            device_id=at(to),
            device_id_type=MESH,
        )

    def halved(g, src, dst, half, sem, to):
        rows = pl.ds(half * (ROWS // 2), ROWS // 2)
        return pltpu.make_async_remote_copy(
            src_ref=qbuf.at[g, src, rows],
            dst_ref=qbuf.at[g, dst, rows],
            send_sem=g_ssem.at[g, sem],
            recv_sem=g_rsem.at[g, dst, half],
            device_id=at(to),
            device_id_type=MESH,
        )

    def a_sends(g):
        return [whole(g, 0, 12, 0, peer(g, 1, 0)), whole(g, 0, 4, 1, peer(g, 3, 0))]

    def a_forward(g, da):
        if da == 3:
            return halved(g, 12, 8, 0, 2, peer(g, 1, 0))
        return halved(g, 4, 8, 1, 3, peer(g, 3, 0))

    def b_sends(g, da):
        return [
            whole(g, da * 4, da * 4 + 3, 4 + 4 * da, peer(g, 0, 1)),
            whole(g, da * 4, da * 4 + 1, 5 + 4 * da, peer(g, 0, 3)),
        ]

    def b_forwards(g, da):
        return [
            halved(g, da * 4 + 3, da * 4 + 2, 0, 6 + 4 * da, peer(g, 0, 1)),
            halved(g, da * 4 + 1, da * 4 + 2, 1, 7 + 4 * da, peer(g, 0, 3)),
        ]

    def turned(x):
        return x * cos + pltpu.roll(x, HEAD_DIM // 2, 1) * sin

    pl.semaphore_wait(barrier, len(others))
    later = {(0, 0): kv_loads[1], (0, 1): q_loads[1][0]}

    def make_query(g):
        total = None
        for n in range(2):
            q_loads[g][n].wait()
            if (g, n) in later:
                later[g, n].start()
            term = jnp.dot(
                normed[:, pl.ds(n * half_depth, half_depth)],
                wq[g, n],
                preferred_element_type=F32,
            )
            total = term if total is None else total + term
        for h in range(GROUP):
            qbuf[g, 0, pl.ds(h * SEL, SEL), :] = turned(total[:, h * 128 : (h + 1) * 128]).astype(
                BF16
            )
        for copy in a_sends(g) + b_sends(g, 0):
            copy.start()

    make_query(0)
    own_stored.wait()
    q_loads[1][1].start()
    wide[...] = stored[...].astype(F32)
    for n, buf in enumerate((kbuf, vbuf)):
        for g in range(2):
            rows = wide[pl.ds(2 * n + g, BLOCK, stride=4), :]
            buf[g, pl.ds(0, BLOCK), :] = rows.astype(BF16)
        stored_copies[n].start()

    for n in range(2):
        kv_loads[n].wait()
        made = jnp.dot(normed[...], wkv[n], preferred_element_type=F32)
        made_kv[0, n, pl.ds(SEL, FRESH - SEL), :] = jnp.zeros((FRESH - SEL, 256), BF16)
        for g in range(2):
            value = made[:, g * 128 : (g + 1) * 128]
            if n == 0:
                value = turned(value)
            made_kv[0, n, pl.ds(0, SEL), pl.ds(g * 128, 128)] = value.astype(BF16)
            fresh[pl.ds(2 * n + g, SEL, stride=4), :] = value
        fresh_copies[n].start()
    make_query(1)
    for copy in weights:
        copy.start()

    def put_in(n):
        replaced = row_pos[pl.ds(blocks[n], 1), :]
        source = jnp.concatenate(
            [made_kv[n, 0], made_kv[n, 1], jnp.ones((FRESH, 128), BF16)], 1
        )
        for first in range(0, BLOCK, 256):
            there = blocks[n] * BLOCK + first + lax.broadcasted_iota(jnp.int32, (256, 128), 0)
            usable = lax.broadcasted_iota(jnp.int32, (256, 128), 1) < SEL
            chosen = jnp.logical_and(there.astype(F32) == replaced, usable)
            rows = jnp.dot(
                jnp.where(chosen, 1.0, 0.0).astype(BF16), source, preferred_element_type=F32
            )
            gone = rows[:, 512:] > 0.5
            where = pl.ds(n * BLOCK + first, 256)
            for k, (buf, g) in enumerate(((kbuf, 0), (kbuf, 1), (vbuf, 0), (vbuf, 1))):
                old = buf[g, where, :].astype(F32)
                buf[g, where, :] = jnp.where(gone, rows[:, k * 128 : (k + 1) * 128], old).astype(
                    BF16
                )

    for copy in stored_copies:
        copy.wait_send()
    put_in(0)
    new_ref[...] = fresh[...].astype(BF16)

    def full(g, da, db):
        whole(g, 0, da * 4 + db, 0, peer(g, 1, 0)).wait_recv()

    def both_halves(g, da, db):
        for half in range(2):
            halved(g, 0, da * 4 + db, half, 0, peer(g, 1, 0)).wait_recv()

    def arrive(t, g):
        @pl.when(t < 4)
        def _():
            @pl.when(t == 1)
            def _():
                for db in (1, 3):
                    full(g, 0, db)
                for copy in b_forwards(g, 0):
                    copy.start()
                for da in (1, 3):
                    full(g, da, 0)
                    a_forward(g, da).start()
                for copy in b_sends(g, 1):
                    copy.start()

            @pl.when(t == 2)
            def _():
                for copy in b_sends(g, 3):
                    copy.start()

            @pl.when(t == 3)
            def _():
                both_halves(g, 0, 2)
                both_halves(g, 2, 0)
                for copy in b_sends(g, 2):
                    copy.start()

        @pl.when(jnp.logical_or(jnp.logical_or(t == 4, t == 6), t == 8))
        def _():
            da = jnp.where(t == 4, 1, jnp.where(t == 6, 3, 2))
            for db in (1, 3):
                full(g, da, db)
            for copy in b_forwards(g, da):
                copy.start()

        @pl.when(jnp.logical_and(t >= 10, t < 13))
        def _():
            both_halves(g, t - 9, 2)

    def score(t, g):
        da, db = offset(t, 0), offset(t, 1)
        owner = peer(g, da, db)
        s = lax.dot_general(
            qbuf[g, da * 4 + db],
            kbuf[g],
            (((1,), (1,)), ((), ())),
            preferred_element_type=F32,
        )
        row = jnp.broadcast_to(row_pos[pl.ds(owner, 1), :], (128, 128)).T[:SEL, :1]
        pos = jnp.concatenate([row] * GROUP, 0)
        s = jnp.where(key_pos[...] <= pos, s, NEG)
        scores[g] = s
        tops[g] = functools.reduce(
            jnp.maximum, [s[:, n * 128 : (n + 1) * 128] for n in range(KEYS // 128)]
        )

    def weigh(t, g):
        top = jnp.broadcast_to(jnp.max(tops[g], -1, keepdims=True), (ROWS, 128))
        e = jnp.exp2((scores[g] - top[:, :1]) * LOG_SCALE).astype(BF16)
        table = jnp.concatenate([vbuf[g], jnp.ones((KEYS, 128), BF16)], 1)
        summed = jnp.dot(e, table, preferred_element_type=F32)
        total = summed[:, 128:]
        part[g, t] = (summed[:, :128] / total).astype(BF16)
        stat[g, t] = pack_rows(top * LOG_SCALE + jnp.log2(total))

    def b_result(g, t, da, db):
        to = at(peer(g, 0, db))
        return [
            pltpu.make_async_remote_copy(
                src_ref=src.at[g, t],
                dst_ref=dst.at[g, da, db - 1],
                send_sem=ssem.at[g, da, db - 1],
                recv_sem=rsem.at[g, da, db - 1],
                device_id=to,
                device_id_type=MESH,
            )
            for src, dst, ssem, rsem in (
                (part, rb_part, bp_ssem, bp_rsem),
                (stat, rb_stat, bs_ssem, bs_rsem),
            )
        ]

    def a_result(g, da):
        to = at(peer(g, da, 0))
        return [
            pltpu.make_async_remote_copy(
                src_ref=src.at[g, da - 1],
                dst_ref=dst.at[g, da - 1],
                send_sem=ssem.at[g, da - 1],
                recv_sem=rsem.at[g, da - 1],
                device_id=to,
                device_id_type=MESH,
            )
            for src, dst, ssem, rsem in (
                (mid, ra_part, ap_ssem, ap_rsem),
                (mid_stat, ra_stat, as_ssem, as_rsem),
            )
        ]

    def line(g, da):
        t = OWN[da]
        return (
            [part[g, t]] + [rb_part[g, da, n] for n in range(3)],
            [stat[g, t]] + [rb_stat[g, da, n] for n in range(3)],
        )

    def line_arrives(da):
        for g in range(2):
            for db in range(1, SIDE):
                for copy in b_result(g, 0, da, db):
                    copy.wait_recv()

    def merge_line(da, halves=(0, 1)):
        for g in halves:
            merged, logs = merge(*line(g, da))
            mid[g, da - 1] = merged.astype(BF16)
            mid_stat[g, da - 1] = logs

    def send_line(da, halves=(0, 1)):
        for g in halves:
            for copy in a_result(g, da):
                copy.start()

    def pass_on(t, g):
        for copy in b_result(g, t, offset(t, 0), offset(t, 1)):
            copy.start()

    for copy in stored_copies + fresh_copies:
        copy.wait_recv()
    put_in(1)
    score(0, 0)
    score(0, 1)
    weigh(0, 0)
    arrive(jnp.int32(1), 0)
    score(1, 0)
    weigh(0, 1)

    def step(t, carry):
        arrive(t, 1)
        score(t, 1)
        weigh(t, 0)
        pass_on(t, 0)
        arrive(t + 1, 0)
        score(t + 1, 0)
        weigh(t, 1)
        pass_on(t, 1)
        return carry

    lax.fori_loop(1, 13, step, 0)
    line_arrives(0)
    score(13, 1)
    weigh(13, 0)
    for g in range(2):
        merged, logs = merge(*line(g, 0))
        part[g, 0] = merged.astype(BF16)
        stat[g, 0] = logs
    score(14, 0)
    weigh(13, 1)
    line_arrives(2)
    score(14, 1)
    weigh(14, 0)
    merge_line(2)
    send_line(2)
    line_arrives(1)
    score(15, 0)
    weigh(14, 1)
    merge_line(1, (0,))
    send_line(1, (0,))
    line_arrives(3)
    score(15, 1)
    weigh(15, 0)
    merge_line(1, (1,))
    send_line(1, (1,))
    weigh(15, 1)
    merge_line(3, (0,))
    send_line(3, (0,))
    merge_line(3, (1,))
    send_line(3, (1,))
    for g in range(2):
        for da in (2, 1, 3):
            for copy in a_result(g, da):
                copy.wait_recv()
        merged, _ = merge(
            [part[g, 0]] + [ra_part[g, n] for n in range(3)],
            [stat[g, 0]] + [ra_stat[g, n] for n in range(3)],
        )
        for h in range(GROUP):
            ctx[:, pl.ds((g * GROUP + h) * 128, 128)] = merged[h * SEL : (h + 1) * SEL].astype(BF16)

    for copy in weights:
        copy.wait()

    lower = pl.ds(0, SEL // 2)
    upper = pl.ds(SEL // 2, SEL // 2)

    def z_copy(index, src, dst, dz):
        return pltpu.make_async_remote_copy(
            src_ref=src,
            dst_ref=dst,
            send_sem=z_ssem.at[index],
            recv_sem=z_rsem.at[index],
            device_id=above(dz),
            device_id_type=MESH,
        )

    def projected(dz):
        return jnp.dot(ctx[...], wbuf[lax.rem(head + dz, SIDE)], preferred_element_type=F32)

    up_far = z_copy(0, zsend.at[0, lower], zrelay.at[0], 1)
    down_far = z_copy(1, zsend.at[0, upper], zrelay.at[1], 3)
    up_free = z_copy(2, zsend.at[1, upper], zrecv.at[0, upper], 1)
    up_sum = z_copy(3, zsend.at[1, lower], zrecv.at[0, lower], 1)
    down_free = z_copy(4, zsend.at[2, lower], zrecv.at[1, lower], 3)
    down_sum = z_copy(5, zsend.at[2, upper], zrecv.at[1, upper], 3)
    zsend[0] = projected(2).astype(BF16)
    up_far.start()
    down_far.start()
    up = projected(1)
    zsend[1, upper] = up[SEL // 2 :].astype(BF16)
    up_free.start()
    up_far.wait_recv()
    zsend[1, lower] = (up[: SEL // 2] + zrelay[0].astype(F32)).astype(BF16)
    up_sum.start()
    down = projected(3)
    zsend[2, lower] = down[: SEL // 2].astype(BF16)
    down_free.start()
    down_far.wait_recv()
    zsend[2, upper] = (down[SEL // 2 :] + zrelay[1].astype(F32)).astype(BF16)
    down_sum.start()
    total = projected(0)
    for copy in (up_free, up_sum, down_free, down_sum):
        copy.wait_recv()
    out_ref[...] = (total + zrecv[0].astype(F32) + zrecv[1].astype(F32)).astype(BF16)

    for copy in fresh_copies:
        copy.wait_send()
    for g in range(2):
        for copy in a_sends(g) + [a_forward(g, 3), a_forward(g, 1)]:
            copy.wait_send()
        for da in range(4):
            for copy in b_sends(g, da) + b_forwards(g, da):
                copy.wait_send()
            for db in range(1, 4):
                for copy in b_result(g, 0, da, db):
                    copy.wait_send()
        for da in range(1, 4):
            for copy in a_result(g, da):
                copy.wait_send()
    for copy in (up_far, down_far, up_free, up_sum, down_free, down_sum):
        copy.wait_send()


def attend(*operands):
    vmem = pl.BlockSpec(memory_space=pltpu.VMEM)
    hbm = pl.BlockSpec(memory_space=pl.ANY)
    dma = pltpu.SemaphoreType.DMA
    return pl.pallas_call(
        kernel,
        out_shape=(
            pltpu.VMEM((SEL, 1024), BF16),
            pltpu.VMEM((4 * SEL, 128), BF16),
        ),
        in_specs=[hbm] * 11,
        out_specs=(vmem, vmem),
        scratch_shapes=[
            pltpu.SMEM((PASSAGES,), jnp.int32),
            pltpu.SMEM((PASSAGES,), jnp.int32),
            pltpu.VMEM((1, D), F32),
            pltpu.VMEM((1, 128), F32),
            pltpu.VMEM((24, 128), jnp.int32),
            pltpu.VMEM((32, 128), F32),
            pltpu.VMEM((SEL, D), BF16),
            pltpu.VMEM((SEL, D), BF16),
            pltpu.VMEM((2, 2, D // 2, 512), BF16),
            pltpu.VMEM((2, D, 256), BF16),
            pltpu.VMEM((4 * BLOCK, 128), BF16),
            pltpu.VMEM((4 * BLOCK, 128), F32),
            pltpu.VMEM((4 * SEL, 128), F32),
            pltpu.VMEM((2, 2, FRESH, 256), BF16),
            pltpu.VMEM((1, KEYS), F32),
            pltpu.VMEM((2, 16, ROWS, 128), BF16),
            pltpu.VMEM((2, KEYS, 128), BF16),
            pltpu.VMEM((2, KEYS, 128), BF16),
            pltpu.VMEM((SIDE, 1024, 1024), BF16),
            pltpu.VMEM((2, ROWS, KEYS), F32),
            pltpu.VMEM((2, ROWS, 128), F32),
            pltpu.VMEM((2, 16, ROWS, 128), BF16),
            pltpu.VMEM((2, 16, 8, 128), F32),
            pltpu.VMEM((2, 4, 3, ROWS, 128), BF16),
            pltpu.VMEM((2, 4, 3, 8, 128), F32),
            pltpu.VMEM((2, 3, ROWS, 128), BF16),
            pltpu.VMEM((2, 3, 8, 128), F32),
            pltpu.VMEM((2, 3, ROWS, 128), BF16),
            pltpu.VMEM((2, 3, 8, 128), F32),
            pltpu.VMEM((SEL, 1024), BF16),
            pltpu.VMEM((3, SEL, 1024), BF16),
            pltpu.VMEM((2, SEL // 2, 1024), BF16),
            pltpu.VMEM((2, SEL, 1024), BF16),
            dma((17,)),
            dma((4,)),
            dma((4,)),
            dma((2, 20)),
            dma((2, 16, 2)),
            dma((2, 4, 3)),
            dma((2, 4, 3)),
            dma((2, 4, 3)),
            dma((2, 4, 3)),
            dma((2, 3)),
            dma((2, 3)),
            dma((2, 3)),
            dma((2, 3)),
            dma((6,)),
            dma((6,)),
        ],
        compiler_params=pltpu.CompilerParams(
            collective_id=0, has_side_effects=True, vmem_limit_bytes=64_000_000
        ),
    )(*operands)


def body(
    hidden, norm_gain, w_query, w_key, w_value, w_out, stored_kv, selected, prompt_order, store_slot
):
    half = HEAD_DIM // 2
    index = jnp.arange(HEAD_DIM, dtype=jnp.int32) % half
    freq = 500000.0 ** (-(index.astype(F32) * 2.0 / HEAD_DIM))
    attn_out, new_kv = attend(
        prompt_order,
        store_slot,
        hidden,
        norm_gain[None],
        freq[None],
        selected.reshape(24, 128),
        stored_kv.reshape(-1, HEAD_DIM),
        w_query,
        w_key,
        w_value,
        w_out,
    )
    return (attn_out, new_kv.reshape(SEL, 2, 2, HEAD_DIM))


def solution(mesh):
    in_specs = (
        P("seq", None),
        P(),
        P(None, "head"),
        P(None, "head"),
        P(None, "head"),
        P("head", None),
        P("seq", None, "head", None),
        P(),
        P(),
        P(),
    )
    out_specs = (P("seq", "head"), P("seq", None, "head", None))
    return jax.shard_map(body, mesh=mesh, in_specs=in_specs, out_specs=out_specs, check_vma=False)
```

```python
import functools

import jax
import jax.numpy as jnp
from jax import lax
from jax.experimental import pallas as pl
from jax.experimental.pallas import tpu as pltpu
from jax.sharding import PartitionSpec as P

D = 4096
HEADS = 32
KV_HEADS = 8
HEAD_DIM = 128
PASSAGE = 4096
PASSAGES = 8
SIDE = 4
GROUP = HEADS // KV_HEADS
BLOCK = 1024
SEL = 96
FRESH = 128
KEYS = 2 * BLOCK
ROWS = GROUP * SEL
NEG = -1.0e30
LOG_SCALE = 1.4426950408889634 / HEAD_DIM**0.5
F32 = jnp.float32
BF16 = jnp.bfloat16
MESH = pl.DeviceIdType.MESH


WALK = (
    (0, 0), (0, 1), (0, 3), (0, 2), (1, 1), (1, 3), (3, 1), (3, 3),
    (2, 1), (2, 3), (1, 2), (2, 2), (3, 2), (2, 0), (1, 0), (3, 0),
)
OWN = {da: t for t, (da, db) in enumerate(WALK) if db == 0}


def offset(t, axis):
    if isinstance(t, int):
        return WALK[t][axis]
    found = jnp.int32(0)
    for n, pair in enumerate(WALK):
        found = jnp.where(t == n, pair[axis], found)
    return found


def pack_rows(column):
    lane = lax.broadcasted_iota(jnp.int32, (SEL, 128), 1)
    total = jnp.zeros((SEL, 128), F32)
    for h in range(GROUP):
        total = jnp.where(lane == h, column[h * SEL : (h + 1) * SEL], total)
    square = jnp.concatenate([total, jnp.zeros((128 - SEL, 128), F32)], 0)
    return square.T[:8]


def unpack_rows(packed):
    square = jnp.concatenate([packed, jnp.zeros((120, 128), F32)], 0).T
    return jnp.concatenate(
        [jnp.broadcast_to(square[:SEL, h : h + 1], (SEL, 128)) for h in range(GROUP)], 0
    )


def merge(parts, stats):
    top = functools.reduce(jnp.maximum, stats)
    factors = [jnp.exp2(s - top) for s in stats]
    total = functools.reduce(jnp.add, factors)
    merged = sum(
        part.astype(F32) * unpack_rows(factor / total) for part, factor in zip(parts, factors)
    )
    return merged, top + jnp.log2(total)


def kernel(
    order_in,
    slot_in,
    hidden_in,
    gain_in,
    freq_in,
    selected_in,
    stored_in,
    w_query_in,
    w_key_in,
    w_value_in,
    w_out_in,
    out_ref,
    new_ref,
    prompt_order,
    store_slot,
    gain,
    freq,
    listed,
    row_pos,
    hid,
    normed,
    wq,
    wkv,
    stored,
    wide,
    fresh,
    made_kv,
    key_pos,
    qbuf,
    kbuf,
    vbuf,
    wbuf,
    scores,
    tops,
    part,
    stat,
    rb_part,
    rb_stat,
    mid,
    mid_stat,
    ra_part,
    ra_stat,
    ctx,
    zsend,
    zrelay,
    zrecv,
    local_sem,
    kv_ssem,
    kv_rsem,
    g_ssem,
    g_rsem,
    bp_ssem,
    bp_rsem,
    bs_ssem,
    bs_rsem,
    ap_ssem,
    ap_rsem,
    as_ssem,
    as_rsem,
    z_ssem,
    z_rsem,
):
    seq = lax.axis_index("seq")
    head = lax.axis_index("head")
    core = lax.rem(seq, 2)
    chip_x = lax.rem(seq // 2, SIDE)
    chip_y = seq // (2 * SIDE)

    def chip_seq(dx, dy):
        return (lax.rem(chip_y + dy, SIDE) * SIDE + lax.rem(chip_x + dx, SIDE)) * 2 + core

    def peer(g, da, db):
        return chip_seq(da, db) if g == 0 else chip_seq(db, da)

    def at(index):
        return (index, head)

    def above(dz):
        return (seq, lax.rem(head + dz, SIDE))

    other_seq = seq + 1 - 2 * core
    partner = (other_seq, head)

    barrier = pltpu.get_barrier_semaphore()
    others = [partner]
    for d in range(1, SIDE):
        others.append(at(chip_seq(d, 0)))
        others.append(at(chip_seq(0, d)))
    others += [above(1), above(3)]
    for other in others:
        pl.semaphore_signal(barrier, inc=1, device_id=other, device_id_type=MESH)

    load = pltpu.make_async_copy
    half_depth = D // 2
    own_hidden = load(hidden_in, hid, local_sem.at[0])
    own_stored = load(stored_in, stored, local_sem.at[1])
    q_loads = [
        [
            load(
                w_query_in.at[pl.ds(n * half_depth, half_depth), pl.ds(g * 512, 512)],
                wq.at[g, n],
                local_sem.at[2 + 2 * g + n],
            )
            for n in range(2)
        ]
        for g in range(2)
    ]
    kv_loads = [
        load(src, wkv.at[n], local_sem.at[6 + n]) for n, src in enumerate((w_key_in, w_value_in))
    ]
    weights = [
        load(w_out_in.at[:, pl.ds(n * 1024, 1024)], wbuf.at[n], local_sem.at[8 + n])
        for n in range(SIDE)
    ]
    small = [
        load(src, dst, local_sem.at[12 + n])
        for n, (src, dst) in enumerate(
            (
                (selected_in, listed),
                (freq_in, freq),
                (gain_in, gain),
                (order_in, prompt_order),
                (slot_in, store_slot),
            )
        )
    ]
    for copy in small:
        copy.start()
    own_hidden.start()
    for copy in q_loads[0]:
        copy.start()

    for copy in small:
        copy.wait()

    wide[pl.ds(0, 24), :] = listed[...].astype(F32)
    thirds = [wide[pl.ds(n, 8, stride=3), :] for n in range(3)]
    lane = lax.broadcasted_iota(jnp.int32, (8, 128), 1)
    roll = pltpu.roll
    for n, rows in enumerate(
        (
            thirds[0],
            jnp.where(lane < 32, roll(thirds[0], 32, 1), roll(thirds[1], 32, 1)),
            jnp.where(lane < 64, roll(thirds[1], 64, 1), roll(thirds[2], 64, 1)),
            roll(thirds[2], 96, 1),
        )
    ):
        row_pos[pl.ds(n, 8, stride=4), :] = rows

    angle = jnp.broadcast_to(row_pos[pl.ds(seq, 1), :], (128, 128)).T[:SEL] * freq[...]
    cos = jnp.cos(angle)
    sin = jnp.sin(angle)
    sin = jnp.where(lax.broadcasted_iota(jnp.int32, (SEL, 128), 1) < HEAD_DIM // 2, -sin, sin)

    order = [store_slot[prompt_order[i]] for i in range(PASSAGES)]
    lanes = lax.broadcasted_iota(jnp.int32, (1, BLOCK), 1)
    per_passage = PASSAGE // BLOCK
    blocks = []
    for n, device in enumerate((seq, other_seq)):
        place = jnp.int32(0)
        for i in range(PASSAGES):
            place = jnp.where(order[i] == device // per_passage, i, place)
        block = place * per_passage + lax.rem(device, per_passage)
        blocks.append(block)
        there = (block * BLOCK + lanes).astype(F32)
        replaced = jnp.broadcast_to(row_pos[pl.ds(block, 1), :], (128, 128)).T[:SEL, :1]
        made = jnp.broadcast_to(row_pos[pl.ds(device, 1), :], (128, 128)).T[:SEL, :1]
        put = jnp.sum(jnp.where(replaced == there, made + 1.0, 0.0), 0, keepdims=True)
        key_pos[:, pl.ds(n * BLOCK, BLOCK)] = jnp.where(put > 0.0, put - 1.0, there)

    own_hidden.wait()
    own_stored.start()
    kv_loads[0].start()
    widened = hid[...].astype(F32)
    mean = jnp.mean(widened * widened, -1, keepdims=True)
    normed[...] = (widened * lax.rsqrt(mean + 1e-05) * gain[...]).astype(BF16)

    def to_partner(index, src, dst):
        return pltpu.make_async_remote_copy(
            src_ref=src,
            dst_ref=dst,
            send_sem=kv_ssem.at[index],
            recv_sem=kv_rsem.at[index],
            device_id=partner,
            device_id_type=MESH,
        )

    stored_copies = [
        to_partner(n, buf.at[:, pl.ds(0, BLOCK)], buf.at[:, pl.ds(BLOCK, BLOCK)])
        for n, buf in enumerate((kbuf, vbuf))
    ]
    fresh_copies = [to_partner(2 + n, made_kv.at[0, n], made_kv.at[1, n]) for n in range(2)]

    def whole(g, src, dst, sem, to):
        return pltpu.make_async_remote_copy(
            src_ref=qbuf.at[g, src],
            dst_ref=qbuf.at[g, dst],
            send_sem=g_ssem.at[g, sem],
            recv_sem=g_rsem.at[g, dst, 0],
            device_id=at(to),
            device_id_type=MESH,
        )

    def halved(g, src, dst, half, sem, to):
        rows = pl.ds(half * (ROWS // 2), ROWS // 2)
        return pltpu.make_async_remote_copy(
            src_ref=qbuf.at[g, src, rows],
            dst_ref=qbuf.at[g, dst, rows],
            send_sem=g_ssem.at[g, sem],
            recv_sem=g_rsem.at[g, dst, half],
            device_id=at(to),
            device_id_type=MESH,
        )

    def a_sends(g):
        return [whole(g, 0, 12, 0, peer(g, 1, 0)), whole(g, 0, 4, 1, peer(g, 3, 0))]

    def a_forward(g, da):
        if da == 3:
            return halved(g, 12, 8, 0, 2, peer(g, 1, 0))
        return halved(g, 4, 8, 1, 3, peer(g, 3, 0))

    def b_sends(g, da):
        return [
            whole(g, da * 4, da * 4 + 3, 4 + 4 * da, peer(g, 0, 1)),
            whole(g, da * 4, da * 4 + 1, 5 + 4 * da, peer(g, 0, 3)),
        ]

    def b_forwards(g, da):
        return [
            halved(g, da * 4 + 3, da * 4 + 2, 0, 6 + 4 * da, peer(g, 0, 1)),
            halved(g, da * 4 + 1, da * 4 + 2, 1, 7 + 4 * da, peer(g, 0, 3)),
        ]

    def turned(x):
        return x * cos + pltpu.roll(x, HEAD_DIM // 2, 1) * sin

    pl.semaphore_wait(barrier, len(others))
    later = {(0, 0): kv_loads[1], (0, 1): q_loads[1][0]}

    def make_query(g):
        total = None
        for n in range(2):
            q_loads[g][n].wait()
            if (g, n) in later:
                later[g, n].start()
            term = jnp.dot(
                normed[:, pl.ds(n * half_depth, half_depth)],
                wq[g, n],
                preferred_element_type=F32,
            )
            total = term if total is None else total + term
        for h in range(GROUP):
            qbuf[g, 0, pl.ds(h * SEL, SEL), :] = turned(total[:, h * 128 : (h + 1) * 128]).astype(
                BF16
            )
        for copy in a_sends(g) + b_sends(g, 0):
            copy.start()

    make_query(0)
    own_stored.wait()
    q_loads[1][1].start()
    wide[...] = stored[...].astype(F32)
    for n, buf in enumerate((kbuf, vbuf)):
        for g in range(2):
            rows = wide[pl.ds(2 * n + g, BLOCK, stride=4), :]
            buf[g, pl.ds(0, BLOCK), :] = rows.astype(BF16)
        stored_copies[n].start()

    for n in range(2):
        kv_loads[n].wait()
        made = jnp.dot(normed[...], wkv[n], preferred_element_type=F32)
        made_kv[0, n, pl.ds(SEL, FRESH - SEL), :] = jnp.zeros((FRESH - SEL, 256), BF16)
        for g in range(2):
            value = made[:, g * 128 : (g + 1) * 128]
            if n == 0:
                value = turned(value)
            made_kv[0, n, pl.ds(0, SEL), pl.ds(g * 128, 128)] = value.astype(BF16)
            fresh[pl.ds(2 * n + g, SEL, stride=4), :] = value
        fresh_copies[n].start()
    make_query(1)
    for copy in weights:
        copy.start()

    def put_in(n):
        replaced = row_pos[pl.ds(blocks[n], 1), :]
        source = jnp.concatenate(
            [made_kv[n, 0], made_kv[n, 1], jnp.ones((FRESH, 128), BF16)], 1
        )
        for first in range(0, BLOCK, 256):
            there = blocks[n] * BLOCK + first + lax.broadcasted_iota(jnp.int32, (256, 128), 0)
            usable = lax.broadcasted_iota(jnp.int32, (256, 128), 1) < SEL
            chosen = jnp.logical_and(there.astype(F32) == replaced, usable)
            rows = jnp.dot(
                jnp.where(chosen, 1.0, 0.0).astype(BF16), source, preferred_element_type=F32
            )
            gone = rows[:, 512:] > 0.5
            where = pl.ds(n * BLOCK + first, 256)
            for k, (buf, g) in enumerate(((kbuf, 0), (kbuf, 1), (vbuf, 0), (vbuf, 1))):
                old = buf[g, where, :].astype(F32)
                buf[g, where, :] = jnp.where(gone, rows[:, k * 128 : (k + 1) * 128], old).astype(
                    BF16
                )

    for copy in stored_copies:
        copy.wait_send()
    put_in(0)
    new_ref[...] = fresh[...].astype(BF16)

    def full(g, da, db):
        whole(g, 0, da * 4 + db, 0, peer(g, 1, 0)).wait_recv()

    def both_halves(g, da, db):
        for half in range(2):
            halved(g, 0, da * 4 + db, half, 0, peer(g, 1, 0)).wait_recv()

    def arrive(t, g):
        @pl.when(t < 4)
        def _():
            @pl.when(t == 1)
            def _():
                for db in (1, 3):
                    full(g, 0, db)
                for copy in b_forwards(g, 0):
                    copy.start()
                for da in (1, 3):
                    full(g, da, 0)
                    a_forward(g, da).start()
                for copy in b_sends(g, 1) + b_sends(g, 3):
                    copy.start()

            @pl.when(t == 3)
            def _():
                both_halves(g, 0, 2)
                both_halves(g, 2, 0)
                for copy in b_sends(g, 2):
                    copy.start()

        @pl.when(jnp.logical_or(jnp.logical_or(t == 4, t == 6), t == 8))
        def _():
            da = jnp.where(t == 4, 1, jnp.where(t == 6, 3, 2))
            for db in (1, 3):
                full(g, da, db)
            for copy in b_forwards(g, da):
                copy.start()

        @pl.when(jnp.logical_and(t >= 10, t < 13))
        def _():
            both_halves(g, t - 9, 2)

    def score(t, g):
        da, db = offset(t, 0), offset(t, 1)
        owner = peer(g, da, db)
        s = lax.dot_general(
            qbuf[g, da * 4 + db],
            kbuf[g],
            (((1,), (1,)), ((), ())),
            preferred_element_type=F32,
        )
        row = jnp.broadcast_to(row_pos[pl.ds(owner, 1), :], (128, 128)).T[:SEL, :1]
        pos = jnp.concatenate([row] * GROUP, 0)
        s = jnp.where(key_pos[...] <= pos, s, NEG)
        scores[g] = s
        tops[g] = functools.reduce(
            jnp.maximum, [s[:, n * 128 : (n + 1) * 128] for n in range(KEYS // 128)]
        )

    def weigh(t, g):
        top = jnp.broadcast_to(jnp.max(tops[g], -1, keepdims=True), (ROWS, 128))
        e = jnp.exp2((scores[g] - top[:, :1]) * LOG_SCALE).astype(BF16)
        table = jnp.concatenate([vbuf[g], jnp.ones((KEYS, 128), BF16)], 1)
        summed = jnp.dot(e, table, preferred_element_type=F32)
        total = summed[:, 128:]
        part[g, t] = (summed[:, :128] / total).astype(BF16)
        stat[g, t] = pack_rows(top * LOG_SCALE + jnp.log2(total))

    def b_result(g, t, da, db):
        to = at(peer(g, 0, db))
        return [
            pltpu.make_async_remote_copy(
                src_ref=src.at[g, t],
                dst_ref=dst.at[g, da, db - 1],
                send_sem=ssem.at[g, da, db - 1],
                recv_sem=rsem.at[g, da, db - 1],
                device_id=to,
                device_id_type=MESH,
            )
            for src, dst, ssem, rsem in (
                (part, rb_part, bp_ssem, bp_rsem),
                (stat, rb_stat, bs_ssem, bs_rsem),
            )
        ]

    def a_result(g, da):
        to = at(peer(g, da, 0))
        return [
            pltpu.make_async_remote_copy(
                src_ref=src.at[g, da - 1],
                dst_ref=dst.at[g, da - 1],
                send_sem=ssem.at[g, da - 1],
                recv_sem=rsem.at[g, da - 1],
                device_id=to,
                device_id_type=MESH,
            )
            for src, dst, ssem, rsem in (
                (mid, ra_part, ap_ssem, ap_rsem),
                (mid_stat, ra_stat, as_ssem, as_rsem),
            )
        ]

    def line(g, da):
        t = OWN[da]
        return (
            [part[g, t]] + [rb_part[g, da, n] for n in range(3)],
            [stat[g, t]] + [rb_stat[g, da, n] for n in range(3)],
        )

    def line_arrives(da):
        for g in range(2):
            for db in range(1, SIDE):
                for copy in b_result(g, 0, da, db):
                    copy.wait_recv()

    def merge_line(da, halves=(0, 1)):
        for g in halves:
            merged, logs = merge(*line(g, da))
            mid[g, da - 1] = merged.astype(BF16)
            mid_stat[g, da - 1] = logs

    def send_line(da, halves=(0, 1)):
        for g in halves:
            for copy in a_result(g, da):
                copy.start()

    def pass_on(t, g):
        for copy in b_result(g, t, offset(t, 0), offset(t, 1)):
            copy.start()

    for copy in stored_copies + fresh_copies:
        copy.wait_recv()
    put_in(1)
    score(0, 0)
    score(0, 1)
    weigh(0, 0)
    arrive(jnp.int32(1), 0)
    score(1, 0)
    weigh(0, 1)

    def step(t, carry):
        arrive(t, 1)
        score(t, 1)
        weigh(t, 0)
        pass_on(t, 0)
        arrive(t + 1, 0)
        score(t + 1, 0)
        weigh(t, 1)
        pass_on(t, 1)
        return carry

    lax.fori_loop(1, 13, step, 0)
    line_arrives(0)
    score(13, 1)
    weigh(13, 0)
    for g in range(2):
        merged, logs = merge(*line(g, 0))
        part[g, 0] = merged.astype(BF16)
        stat[g, 0] = logs
    score(14, 0)
    weigh(13, 1)
    line_arrives(2)
    score(14, 1)
    weigh(14, 0)
    merge_line(2)
    send_line(2)
    line_arrives(1)
    score(15, 0)
    weigh(14, 1)
    merge_line(1, (0,))
    send_line(1, (0,))
    line_arrives(3)
    score(15, 1)
    weigh(15, 0)
    merge_line(1, (1,))
    send_line(1, (1,))
    weigh(15, 1)
    merge_line(3, (0,))
    send_line(3, (0,))
    merge_line(3, (1,))
    send_line(3, (1,))
    for g in range(2):
        for da in (2, 1, 3):
            for copy in a_result(g, da):
                copy.wait_recv()
        merged, _ = merge(
            [part[g, 0]] + [ra_part[g, n] for n in range(3)],
            [stat[g, 0]] + [ra_stat[g, n] for n in range(3)],
        )
        for h in range(GROUP):
            ctx[:, pl.ds((g * GROUP + h) * 128, 128)] = merged[h * SEL : (h + 1) * SEL].astype(BF16)

    for copy in weights:
        copy.wait()

    lower = pl.ds(0, SEL // 2)
    upper = pl.ds(SEL // 2, SEL // 2)

    def z_copy(index, src, dst, dz):
        return pltpu.make_async_remote_copy(
            src_ref=src,
            dst_ref=dst,
            send_sem=z_ssem.at[index],
            recv_sem=z_rsem.at[index],
            device_id=above(dz),
            device_id_type=MESH,
        )

    def projected(dz):
        return jnp.dot(ctx[...], wbuf[lax.rem(head + dz, SIDE)], preferred_element_type=F32)

    up_far = z_copy(0, zsend.at[0, lower], zrelay.at[0], 1)
    down_far = z_copy(1, zsend.at[0, upper], zrelay.at[1], 3)
    up_free = z_copy(2, zsend.at[1, upper], zrecv.at[0, upper], 1)
    up_sum = z_copy(3, zsend.at[1, lower], zrecv.at[0, lower], 1)
    down_free = z_copy(4, zsend.at[2, lower], zrecv.at[1, lower], 3)
    down_sum = z_copy(5, zsend.at[2, upper], zrecv.at[1, upper], 3)
    zsend[0] = projected(2).astype(BF16)
    up_far.start()
    down_far.start()
    up = projected(1)
    zsend[1, upper] = up[SEL // 2 :].astype(BF16)
    up_free.start()
    up_far.wait_recv()
    zsend[1, lower] = (up[: SEL // 2] + zrelay[0].astype(F32)).astype(BF16)
    up_sum.start()
    down = projected(3)
    zsend[2, lower] = down[: SEL // 2].astype(BF16)
    down_free.start()
    down_far.wait_recv()
    zsend[2, upper] = (down[SEL // 2 :] + zrelay[1].astype(F32)).astype(BF16)
    down_sum.start()
    total = projected(0)
    for copy in (up_free, up_sum, down_free, down_sum):
        copy.wait_recv()
    out_ref[...] = (total + zrecv[0].astype(F32) + zrecv[1].astype(F32)).astype(BF16)

    for copy in fresh_copies:
        copy.wait_send()
    for g in range(2):
        for copy in a_sends(g) + [a_forward(g, 3), a_forward(g, 1)]:
            copy.wait_send()
        for da in range(4):
            for copy in b_sends(g, da) + b_forwards(g, da):
                copy.wait_send()
            for db in range(1, 4):
                for copy in b_result(g, 0, da, db):
                    copy.wait_send()
        for da in range(1, 4):
            for copy in a_result(g, da):
                copy.wait_send()
    for copy in (up_far, down_far, up_free, up_sum, down_free, down_sum):
        copy.wait_send()


def attend(*operands):
    vmem = pl.BlockSpec(memory_space=pltpu.VMEM)
    hbm = pl.BlockSpec(memory_space=pl.ANY)
    dma = pltpu.SemaphoreType.DMA
    return pl.pallas_call(
        kernel,
        out_shape=(
            pltpu.VMEM((SEL, 1024), BF16),
            pltpu.VMEM((4 * SEL, 128), BF16),
        ),
        in_specs=[hbm] * 11,
        out_specs=(vmem, vmem),
        scratch_shapes=[
            pltpu.SMEM((PASSAGES,), jnp.int32),
            pltpu.SMEM((PASSAGES,), jnp.int32),
            pltpu.VMEM((1, D), F32),
            pltpu.VMEM((1, 128), F32),
            pltpu.VMEM((24, 128), jnp.int32),
            pltpu.VMEM((32, 128), F32),
            pltpu.VMEM((SEL, D), BF16),
            pltpu.VMEM((SEL, D), BF16),
            pltpu.VMEM((2, 2, D // 2, 512), BF16),
            pltpu.VMEM((2, D, 256), BF16),
            pltpu.VMEM((4 * BLOCK, 128), BF16),
            pltpu.VMEM((4 * BLOCK, 128), F32),
            pltpu.VMEM((4 * SEL, 128), F32),
            pltpu.VMEM((2, 2, FRESH, 256), BF16),
            pltpu.VMEM((1, KEYS), F32),
            pltpu.VMEM((2, 16, ROWS, 128), BF16),
            pltpu.VMEM((2, KEYS, 128), BF16),
            pltpu.VMEM((2, KEYS, 128), BF16),
            pltpu.VMEM((SIDE, 1024, 1024), BF16),
            pltpu.VMEM((2, ROWS, KEYS), F32),
            pltpu.VMEM((2, ROWS, 128), F32),
            pltpu.VMEM((2, 16, ROWS, 128), BF16),
            pltpu.VMEM((2, 16, 8, 128), F32),
            pltpu.VMEM((2, 4, 3, ROWS, 128), BF16),
            pltpu.VMEM((2, 4, 3, 8, 128), F32),
            pltpu.VMEM((2, 3, ROWS, 128), BF16),
            pltpu.VMEM((2, 3, 8, 128), F32),
            pltpu.VMEM((2, 3, ROWS, 128), BF16),
            pltpu.VMEM((2, 3, 8, 128), F32),
            pltpu.VMEM((SEL, 1024), BF16),
            pltpu.VMEM((3, SEL, 1024), BF16),
            pltpu.VMEM((2, SEL // 2, 1024), BF16),
            pltpu.VMEM((2, SEL, 1024), BF16),
            dma((17,)),
            dma((4,)),
            dma((4,)),
            dma((2, 20)),
            dma((2, 16, 2)),
            dma((2, 4, 3)),
            dma((2, 4, 3)),
            dma((2, 4, 3)),
            dma((2, 4, 3)),
            dma((2, 3)),
            dma((2, 3)),
            dma((2, 3)),
            dma((2, 3)),
            dma((6,)),
            dma((6,)),
        ],
        compiler_params=pltpu.CompilerParams(
            collective_id=0, has_side_effects=True, vmem_limit_bytes=64_000_000
        ),
    )(*operands)


def body(
    hidden, norm_gain, w_query, w_key, w_value, w_out, stored_kv, selected, prompt_order, store_slot
):
    half = HEAD_DIM // 2
    index = jnp.arange(HEAD_DIM, dtype=jnp.int32) % half
    freq = 500000.0 ** (-(index.astype(F32) * 2.0 / HEAD_DIM))
    attn_out, new_kv = attend(
        prompt_order,
        store_slot,
        hidden,
        norm_gain[None],
        freq[None],
        selected.reshape(24, 128),
        stored_kv.reshape(-1, HEAD_DIM),
        w_query,
        w_key,
        w_value,
        w_out,
    )
    return (attn_out, new_kv.reshape(SEL, 2, 2, HEAD_DIM))


def solution(mesh):
    in_specs = (
        P("seq", None),
        P(),
        P(None, "head"),
        P(None, "head"),
        P(None, "head"),
        P("head", None),
        P("seq", None, "head", None),
        P(),
        P(),
        P(),
    )
    out_specs = (P("seq", "head"), P("seq", None, "head", None))
    return jax.shard_map(body, mesh=mesh, in_specs=in_specs, out_specs=out_specs, check_vma=False)
```
